32 devices in a mesh: dp: 8 (over z, x), fsdp: 4 (over y, core).
Axes of the slice: x: 2, y: 2, z: 4, core: 2. Of those that a mesh axis runs over, the one named last changes fastest.
Arguments:
- tokens: bfloat16 [12288, 768], P(('dp', 'fsdp')), may hold values from -6 to 6
- cotangent: bfloat16 [12288, 768], P(('dp', 'fsdp')), may hold values from -6 to 6
- lengths: int32 [8], P('dp'), may hold values from 512 to 1536, as said below
- input_weight: bfloat16 [2, 768, 2304], P(None, 'fsdp'), may hold values from -0.21875 to 0.21875
- input_bias: bfloat16 [2, 2304], P(None, 'fsdp'), may hold values from -1.1953125 to 1.1953125
- output_weight: bfloat16 [2, 768, 768], P(None, 'fsdp'), may hold values from -3.5 to 3.5
- output_bias: bfloat16 [2, 768], P(None, 'fsdp'), may hold values from -1.1953125 to 1.1953125
- first_gain: bfloat16 [2, 768], P(None, 'fsdp'), may hold values from 0.25 to 1.75
- first_shift: bfloat16 [2, 768], P(None, 'fsdp'), may hold values from -1.1953125 to 1.1953125
- up_weight: bfloat16 [2, 768, 3072], P(None, 'fsdp'), may hold values from -0.21875 to 0.21875
- up_bias: bfloat16 [2, 3072], P(None, 'fsdp'), may hold values from -1.1953125 to 1.1953125
- down_weight: bfloat16 [2, 3072, 768], P(None, 'fsdp'), may hold values from -0.109375 to 0.109375
- down_bias: bfloat16 [2, 768], P(None, 'fsdp'), may hold values from -1.1953125 to 1.1953125
- second_gain: bfloat16 [2, 768], P(None, 'fsdp'), may hold values from 0.25 to 1.75
- second_shift: bfloat16 [2, 768], P(None, 'fsdp'), may hold values from -1.1953125 to 1.1953125
Outputs:
- result: bfloat16 [12288, 768], P(('dp', 'fsdp'))
- grad_tokens: float32 [12288, 768], P(('dp', 'fsdp'))
- grad_input_weight: float32 [2, 768, 2304], P(None, 'fsdp')
- grad_input_bias: float32 [2, 2304], P(None, 'fsdp')
- grad_output_weight: float32 [2, 768, 768], P(None, 'fsdp')
- grad_output_bias: float32 [2, 768], P(None, 'fsdp')
- grad_first_gain: float32 [2, 768], P(None, 'fsdp')
- grad_first_shift: float32 [2, 768], P(None, 'fsdp')
- grad_up_weight: float32 [2, 768, 3072], P(None, 'fsdp')
- grad_up_bias: float32 [2, 3072], P(None, 'fsdp')
- grad_down_weight: float32 [2, 3072, 768], P(None, 'fsdp')
- grad_down_bias: float32 [2, 768], P(None, 'fsdp')
- grad_second_gain: float32 [2, 768], P(None, 'fsdp')
- grad_second_shift: float32 [2, 768], P(None, 'fsdp')
The draws below stay inside these ranges and needn't reach their ends.
Inputs may be any that keep to these rules, and one draw needn't show every extreme that they name: `lengths`: some sequence fills its whole bucket of 1536 rows.
All inputs are finite; a program needn't handle non-finite values.
Results may differ from the reference program's by a relative error of at most 0.023.
Values may be sent and summed in bfloat16 or wider, within the bound.
No kernel may reach another device: no remote copies, remote signals or barrier semaphores. Data moves between devices by JAX's collectives and lax.ppermute only.
A program may use at most 192 MiB of HBM per device.

```python
import jax
import jax.numpy as jnp
from jax import lax

D = 768
HEADS = 12
HEAD = 64
FF = 3072
LAYERS = 2
CAP = 1536
SEQS = 8
TOKENS = 12288


def draw_lengths(key, part):
    key_length = jax.random.fold_in(key, 11)
    key_choice = jax.random.fold_in(key, 23)
    sampled = jax.random.randint(key_length, (SEQS,), CAP // 3, CAP + 1, dtype=jnp.int32)
    chosen = jax.random.randint(key_choice, (), 0, SEQS, dtype=jnp.int32)
    return jnp.where(jnp.arange(SEQS, dtype=jnp.int32) == chosen, CAP, sampled).astype(jnp.int32)


def steps_of(own_key, dims, pieces, smallest, largest):
    level = 1.0
    for axis_at, shards_of in pieces:
        draws = jax.random.uniform(jax.random.fold_in(jax.random.fold_in(own_key, 6), axis_at), (shards_of,), jnp.float32, smallest / len(pieces), largest / len(pieces))
        level = level * jnp.repeat(jnp.exp(draws), dims[axis_at] // shards_of).reshape((-1,) + (1,) * (len(dims) - 1 - axis_at))
    return level


def normal_values(stream_key, shape, deviation, bound, pieces=(), kind=jnp.bfloat16):
    array = deviation * jax.random.normal(stream_key, shape, jnp.float32)
    if pieces:
        array = array * steps_of(stream_key, shape, pieces, -0.22, 0.18)
    return jnp.clip(array, -bound, bound).astype(kind)


def setup_inputs(seed: int = 0) -> dict:
    key_of = jax.random.split(jax.random.key(seed), 16)
    tokens = normal_values(key_of[0], (TOKENS, D), 1.0, 6.0, ((0, 32),))
    cotangent = normal_values(key_of[1], (TOKENS, D), 1.0, 6.0, ((0, 32),))
    lengths = draw_lengths(jax.random.fold_in(key_of[15], 71), 0)
    input_weight = normal_values(key_of[3], (LAYERS, D, 3 * D), D ** -0.5, 0.21875, ((1, 4),))
    input_bias = normal_values(key_of[4], (LAYERS, 3 * D), 0.2, 1.1953125, ((1, 4),))
    output_weight = normal_values(key_of[5], (LAYERS, D, D), 3 ** -0.5, 3.5, ((1, 4),))
    output_bias = normal_values(key_of[6], (LAYERS, D), 0.2, 1.1953125, ((1, 4),))
    first_gain = jnp.clip(1.0 + 0.15 * jax.random.normal(key_of[7], (LAYERS, D), jnp.float32), 0.25, 1.75).astype(jnp.bfloat16)
    first_shift = normal_values(key_of[8], (LAYERS, D), 0.2, 1.1953125, ((1, 4),))
    up_weight = normal_values(key_of[9], (LAYERS, D, FF), D ** -0.5, 0.21875, ((1, 4),))
    up_bias = normal_values(key_of[10], (LAYERS, FF), 0.2, 1.1953125, ((1, 4),))
    down_weight = normal_values(key_of[11], (LAYERS, FF, D), FF ** -0.5, 0.109375, ((1, 4),))
    down_bias = normal_values(key_of[12], (LAYERS, D), 0.2, 1.1953125, ((1, 4),))
    second_gain = jnp.clip(1.0 + 0.15 * jax.random.normal(key_of[13], (LAYERS, D), jnp.float32), 0.25, 1.75).astype(jnp.bfloat16)
    second_shift = normal_values(key_of[14], (LAYERS, D), 0.2, 1.1953125, ((1, 4),))
    return dict(tokens=tokens, cotangent=cotangent, lengths=lengths, input_weight=input_weight, input_bias=input_bias, output_weight=output_weight, output_bias=output_bias, first_gain=first_gain, first_shift=first_shift, up_weight=up_weight, up_bias=up_bias, down_weight=down_weight, down_bias=down_bias, second_gain=second_gain, second_shift=second_shift)


norm_eps = 1e-12
highest = lax.Precision.HIGHEST

@jax.custom_vjp
def low(v):
    return lax.optimization_barrier(v.astype(jnp.bfloat16)).astype(jnp.float32)

@jax.custom_vjp
def low_back(v):
    return v

def low_keep(v):
    return (low(v), None)

def low_pass(kept, grad):
    return (grad,)

def back_keep(v):
    return (v, None)

def back_low(kept, grad):
    return (low(grad),)
low.defvjp(low_keep, low_pass)
low_back.defvjp(back_keep, back_low)

def matmul(left_side, right_side):
    return jnp.dot(left_side, right_side, precision=highest, preferred_element_type=jnp.float32)

def layer_norm(matrix, norm_gain, norm_shift):
    row_mean = lax.optimization_barrier(jnp.mean(matrix, axis=-1, keepdims=True))
    centred = matrix - row_mean
    spread = lax.optimization_barrier(jnp.mean(centred * centred, axis=-1, keepdims=True))
    return centred * lax.rsqrt(spread + norm_eps) * norm_gain + norm_shift

def rotary_tables(positions):
    frequency = 10000.0 ** (-2.0 * jnp.arange(HEAD // 2, dtype=jnp.float32) / HEAD)
    angles = positions[:, None] * frequency[None, :]
    return (jnp.cos(angles), jnp.sin(angles))

def rotate(matrix, cosine_table, sine_table):
    row_count = matrix.shape[0]
    halves = matrix.reshape(row_count, HEADS, 2, HEAD // 2)
    leading = halves[:, :, 0, :]
    trailing = halves[:, :, 1, :]
    cosine = cosine_table[:, None, :]
    sine_part = sine_table[:, None, :]
    turned = jnp.stack([leading * cosine - trailing * sine_part, trailing * cosine + leading * sine_part], axis=2)
    return turned.reshape(row_count, HEADS * HEAD)

def attend(items):
    queries, keys_rot, values, length = items
    key_count = keys_rot.shape[0]
    query_heads = queries.reshape(key_count, HEADS, HEAD)
    key_heads = keys_rot.reshape(key_count, HEADS, HEAD)
    value_heads = values.reshape(key_count, HEADS, HEAD)
    scores = low_back(jnp.einsum('qhd,khd->hqk', query_heads, key_heads, precision=highest) * HEAD ** (-0.5))
    key_valid = jnp.arange(key_count, dtype=jnp.int32) < length
    scores = jnp.where(key_valid[None, None, :], scores, -1e+30)
    probabilities = low(jax.nn.softmax(scores, axis=-1))
    context = jnp.einsum('hqk,khd->qhd', probabilities, value_heads, precision=highest)
    return context.reshape(key_count, HEADS * HEAD)

def layer_forward(hidden, weights, cosine_table, sine_table, lengths):
    input_weight, input_bias, output_weight, output_bias, first_gain, first_shift, up_weight, up_bias, down_weight, down_bias, second_gain, second_shift = weights
    rounded = low(hidden)
    joint_proj = low_back(matmul(rounded, input_weight) + input_bias)
    queries = low(rotate(joint_proj[:, :D], cosine_table, sine_table))
    keys_rot = low(rotate(joint_proj[:, D:2 * D], cosine_table, sine_table))
    values = low(joint_proj[:, 2 * D:])
    context = lax.map(jax.checkpoint(attend), (queries.reshape(SEQS, CAP, D), keys_rot.reshape(SEQS, CAP, D), values.reshape(SEQS, CAP, D), lengths))
    context = low(low_back(context.reshape(TOKENS, D)))
    attn_out = low_back(matmul(context, output_weight) + output_bias)
    normed = layer_norm(hidden + attn_out, first_gain, first_shift)
    up_value = low_back(matmul(low(normed), up_weight) + up_bias)
    activated = low(jax.nn.gelu(up_value, approximate=False))
    down_value = low_back(matmul(activated, down_weight) + down_bias)
    return layer_norm(normed + down_value, second_gain, second_shift)

def reference(tokens, cotangent, lengths, input_weight, input_bias, output_weight, output_bias, first_gain, first_shift, up_weight, up_bias, down_weight, down_bias, second_gain, second_shift):
    params = (input_weight.astype(jnp.float32), input_bias.astype(jnp.float32), output_weight.astype(jnp.float32), output_bias.astype(jnp.float32), first_gain.astype(jnp.float32), first_shift.astype(jnp.float32), up_weight.astype(jnp.float32), up_bias.astype(jnp.float32), down_weight.astype(jnp.float32), down_bias.astype(jnp.float32), second_gain.astype(jnp.float32), second_shift.astype(jnp.float32))
    row_index = jnp.arange(TOKENS, dtype=jnp.int32)
    places = row_index % CAP
    cosine_table, sine_table = rotary_tables(places.astype(jnp.float32))
    row_valid = (places < lengths[row_index // CAP]).astype(jnp.float32)

    def stacked(inputs, weights_all):
        hidden = inputs
        for layer_index in range(LAYERS):
            hidden = layer_forward(hidden, tuple((member[layer_index] for member in weights_all)), cosine_table, sine_table, lengths)
        return hidden
    output_value, pullback = jax.vjp(stacked, tokens.astype(jnp.float32), params)
    grad_tokens, grad_params = pullback(cotangent.astype(jnp.float32) * row_valid[:, None])
    return (output_value.astype(jnp.bfloat16), grad_tokens, grad_params[0], grad_params[1], grad_params[2], grad_params[3], grad_params[4], grad_params[5], grad_params[6], grad_params[7], grad_params[8], grad_params[9], grad_params[10], grad_params[11])
```

```python
import functools

import jax
import jax.numpy as jnp
from jax import lax
from jax.experimental import pallas as pl
from jax.experimental.pallas import tpu as pltpu
from jax.sharding import PartitionSpec as P

D = 768
HEADS = 12
HEAD = 64
PAIRS = HEADS // 2
LAYERS = 2
LOG2E = 1.4426950408889634
SCALE = HEAD ** (-0.5)
NEG = -1e30
BF = jnp.bfloat16
F32 = jnp.float32

norm_eps = 1e-12


def swap(value, axis, bit):
    count = lax.axis_size(axis)
    return lax.ppermute(value, axis, [(i, i ^ bit) for i in range(count)])


def layer_norm(matrix, norm_gain, norm_shift):
    row_mean = jnp.mean(matrix, axis=-1, keepdims=True)
    centred = matrix - row_mean
    spread = jnp.mean(centred * centred, axis=-1, keepdims=True)
    return centred * lax.rsqrt(spread + norm_eps) * norm_gain + norm_shift


def gelu_exact(values_in):
    return jax.nn.gelu(values_in, approximate=False)


def contract_rows(left_side, right_side):
    return lax.dot_general(
        left_side, right_side, (((0,), (0,)), ((), ())), preferred_element_type=F32
    )


def contract_cols(left_side, right_side):
    return lax.dot_general(
        left_side, right_side, (((1,), (1,)), ((), ())), preferred_element_type=F32
    )


def cost(flops, bytes_accessed, transcendentals=0):
    return pl.CostEstimate(
        flops=int(flops), bytes_accessed=int(bytes_accessed), transcendentals=int(transcendentals)
    )


def rotary_tables(places):
    frequency = 10000.0 ** (-2.0 * jnp.arange(HEAD // 2, dtype=F32) / HEAD)
    angles = places[:, None] * frequency[None, :]
    cosine, sine = jnp.cos(angles), jnp.sin(angles)
    nothing = jnp.zeros_like(sine)
    wide = jnp.concatenate([cosine] * 4, axis=1)
    first = jnp.concatenate([-sine, nothing] * 2, axis=1)
    second = jnp.concatenate([nothing, sine] * 2, axis=1)
    return wide, first, second


def turn(block, wide, first, second):
    return (
        block * wide
        + pltpu.roll(block, 96, 1) * first
        + pltpu.roll(block, 32, 1) * second
    )


def assemble_kernel(spec, count, pos_ref, *refs):
    pieces = refs[:count]
    outs = refs[count : count + len(spec)]
    held, in_sem, out_sem = refs[count + len(spec) :]
    copies = []
    for index, piece in enumerate(pieces):
        rows = piece.shape[0]
        start = pl.multiple_of(pos_ref[index], 16)
        copies.append(
            pltpu.make_async_copy(piece, held.at[pl.ds(start, rows), :], in_sem.at[index])
        )
    for copy in copies:
        copy.start()
    for copy in copies:
        copy.wait()
    copies = []
    column = 0
    for slot, (kind, width) in enumerate(spec):
        if kind == "rows":
            copies.append((held.at[:, pl.ds(column, width)], outs[slot]))
        else:
            shard = held.shape[0] // 4
            for source in range(4):
                for part in range(width // D):
                    copies.append(
                        (
                            held.at[pl.ds(source * shard, shard), pl.ds(column + part * D, D)],
                            outs[slot].at[pl.ds(source * 4 * shard + part * shard, shard), :],
                        )
                    )
        column += width
    copies = [
        pltpu.make_async_copy(src, dst, out_sem.at[index])
        for index, (src, dst) in enumerate(copies)
    ]
    for copy in copies:
        copy.start()
    for copy in copies:
        copy.wait()


def assemble(pieces, positions, spec):
    width = pieces[0].shape[1]
    out_shape = []
    outputs = 0
    for kind, columns in spec:
        if kind == "rows":
            out_shape.append(jax.ShapeDtypeStruct((D, columns), BF))
            outputs += 1
        else:
            out_shape.append(jax.ShapeDtypeStruct((columns, D), BF))
            outputs += 4 * (columns // D)
    return pl.pallas_call(
        functools.partial(assemble_kernel, spec, len(pieces)),
        out_shape=out_shape,
        in_specs=[pl.BlockSpec(memory_space=pltpu.SMEM)]
        + [pl.BlockSpec(memory_space=pl.ANY)] * len(pieces),
        out_specs=[pl.BlockSpec(memory_space=pl.ANY)] * len(spec),
        scratch_shapes=[
            pltpu.VMEM((D, width), BF),
            pltpu.SemaphoreType.DMA((len(pieces),)),
            pltpu.SemaphoreType.DMA((outputs,)),
        ],
        cost_estimate=cost(0, 4 * D * width),
        name="assemble",
    )(positions, *pieces)


def project_kernel(count, pos_ref, h_ref, b_ref, cos_ref, first_ref, second_ref, *refs):
    pieces = refs[:count]
    q_ref, kv_ref, whole_ref, held, in_sem, out_sem = refs[count:]
    copies = []
    for part in range(3):
        for index, piece in enumerate(pieces):
            rows = piece.shape[0]
            start = pl.multiple_of(pos_ref[index], 16)
            copies.append(
                pltpu.make_async_copy(
                    piece.at[:, pl.ds(part * D, D)],
                    held.at[part, pl.ds(start, rows), :],
                    in_sem.at[part * count + index],
                )
            )
    for copy in copies:
        copy.start()
    outs = [
        pltpu.make_async_copy(
            held.at[part], whole_ref.at[:, pl.ds(part * D, D)], out_sem.at[part]
        )
        for part in range(3)
    ]
    for part in range(3):
        for copy in copies[part * count : part * count + count]:
            copy.wait()
        outs[part].start()
        joint = jnp.dot(h_ref[...], held[part], preferred_element_type=F32)
        joint = joint + b_ref[:, part * D : part * D + D]
        if part == 2:
            kv_ref[:, D:] = joint.astype(BF)
            continue
        for pair in range(PAIRS):
            span = slice(pair * 128, pair * 128 + 128)
            turned = turn(joint[:, span], cos_ref[...], first_ref[...], second_ref[...])
            (q_ref, kv_ref)[part][:, span] = turned.astype(BF)
    for copy in outs:
        copy.wait()


def project(rounded, pieces, positions, bias, tables):
    rows = rounded.shape[0]
    count = len(pieces)
    return pl.pallas_call(
        functools.partial(project_kernel, count),
        out_shape=[
            jax.ShapeDtypeStruct((rows, D), BF),
            jax.ShapeDtypeStruct((rows, 2 * D), BF),
            jax.ShapeDtypeStruct((D, 3 * D), BF),
        ],
        in_specs=[pl.BlockSpec(memory_space=pltpu.SMEM)]
        + [pl.BlockSpec(memory_space=pltpu.VMEM)] * 5
        + [pl.BlockSpec(memory_space=pl.ANY)] * count,
        out_specs=[
            pl.BlockSpec(memory_space=pltpu.VMEM),
            pl.BlockSpec(memory_space=pltpu.VMEM),
            pl.BlockSpec(memory_space=pl.ANY),
        ],
        scratch_shapes=[
            pltpu.VMEM((3, D, D), BF),
            pltpu.SemaphoreType.DMA((3 * count,)),
            pltpu.SemaphoreType.DMA((3,)),
        ],
        cost_estimate=cost(2 * rows * D * 3 * D, 2 * (rows * 4 * D + 3 * D * D)),
        name="project",
    )(positions, rounded, bias, *tables, *pieces)


def unpack_kernel(widths, place_ref, *refs):
    pieces, outs, held = refs[:4], refs[4:-1], refs[-1]
    place = place_ref[0]
    for index in range(4):
        held[index] = pieces[index][...].astype(F32)
    for source in range(4):
        shard = held[source ^ place]
        offset = 0
        for slot, width in enumerate(widths):
            part = width // 4
            for layer in range(LAYERS):
                outs[layer * len(widths) + slot][:, source * part : source * part + part] = shard[
                    layer : layer + 1, offset : offset + part
                ]
            offset += part


def unpack(info, pieces, widths):
    vmem = pl.BlockSpec(memory_space=pltpu.VMEM)
    return pl.pallas_call(
        functools.partial(unpack_kernel, widths),
        out_shape=[jax.ShapeDtypeStruct((1, width), F32) for width in widths] * LAYERS,
        in_specs=[pl.BlockSpec(memory_space=pltpu.SMEM)] + [vmem] * 4,
        out_specs=[vmem] * (LAYERS * len(widths)),
        scratch_shapes=[pltpu.VMEM((4,) + pieces[0].shape, F32)],
        cost_estimate=cost(0, 100000),
        name="unpack",
    )(info, *pieces)


def attend_kernel(info_ref, q_ref, *refs):
    keys, values = refs[0:4], refs[4:8]
    out_ref, log_ref, column_ref = refs[8:11]
    pair = pl.program_id(0)
    rows = q_ref.shape[0]
    block = 128
    place, length = info_ref[0], info_ref[1]
    lane = lax.broadcasted_iota(jnp.int32, (1, 128), 1)
    key_lane = lax.broadcasted_iota(jnp.int32, (1, rows), 1)
    biases = [
        jnp.where((place ^ k) * rows + key_lane < length, 0.0, NEG).astype(F32) for k in range(4)
    ]
    factor = SCALE * LOG2E
    for part in range(rows // block):
        span = pl.ds(part * block, block)
        query = q_ref[span, :]
        result = jnp.zeros((block, 128), F32)
        for head in range(2):
            own = (lane >= head * HEAD) & (lane < head * HEAD + HEAD)
            masked = jnp.where(own, query, jnp.zeros_like(query))
            scores = [
                contract_cols(masked, keys[k][...]) + biases[k] for k in range(4)
            ]
            peak = jnp.max(
                jnp.maximum(
                    jnp.maximum(scores[0], scores[1]), jnp.maximum(scores[2], scores[3])
                ),
                axis=1,
                keepdims=True,
            )
            parts = [jnp.exp2((s - peak) * factor) for s in scores]
            total = jnp.sum(
                (parts[0] + parts[1]) + (parts[2] + parts[3]), axis=1, keepdims=True
            )
            inverse = 1.0 / total
            gathered = jnp.zeros((block, 128), F32)
            for k in range(4):
                gathered += jnp.dot(
                    (parts[k] * inverse).astype(BF), values[k][...], preferred_element_type=F32
                )
            result = jnp.where(own, gathered, result)
            logged = peak * factor + jnp.log2(total)
            column_ref[span, :] = jnp.where(
                lane == 2 * pair + head, logged, column_ref[span, :]
            )
        out_ref[span, :] = result.astype(BF)

    @pl.when(pair == PAIRS - 1)
    def _():
        log_ref[...] = jnp.transpose(column_ref[...])[0:16, :]


def attend(info, queries, chunks):
    rows = queries.shape[0]
    key_specs = [pl.BlockSpec((rows, 128), lambda p: (0, p))] * 4
    value_specs = [pl.BlockSpec((rows, 128), lambda p: (0, PAIRS + p))] * 4
    return pl.pallas_call(
        attend_kernel,
        out_shape=[
            jax.ShapeDtypeStruct((rows, D), BF),
            jax.ShapeDtypeStruct((16, rows), F32),
        ],
        grid=(PAIRS,),
        in_specs=[
            pl.BlockSpec(memory_space=pltpu.SMEM),
            pl.BlockSpec((rows, 128), lambda p: (0, p)),
            *key_specs,
            *value_specs,
        ],
        out_specs=[
            pl.BlockSpec((rows, 128), lambda p: (0, p)),
            pl.BlockSpec((16, rows), lambda p: (0, 0)),
        ],
        scratch_shapes=[pltpu.VMEM((rows, 128), F32)],
        cost_estimate=cost(
            4 * rows * 4 * rows * D, 2 * rows * 10 * D, rows * 4 * rows * HEADS
        ),
        name="attend",
    )(info, queries, *chunks, *chunks)


def pull_kernel(first_pair, info_ref, q_ref, g_ref, log_ref, *refs):
    keys, values = refs[0:4], refs[4:8]
    dq_ref, own_ref, give_ref = refs[8:11]
    probs_ref, dp_ref = refs[11:13]
    pair = pl.program_id(0) + first_pair
    rows = q_ref.shape[0]
    block = 128
    place, length = info_ref[0], info_ref[1]
    lane = lax.broadcasted_iota(jnp.int32, (1, 128), 1)
    row = lax.broadcasted_iota(jnp.int32, (block, 1), 0)
    factor = SCALE * LOG2E
    query, grad = q_ref[...], g_ref[...]
    nothing = jnp.zeros_like(query)
    dq = jnp.zeros((128, rows), F32)
    for head in range(2):
        own = (lane >= head * HEAD) & (lane < head * HEAD + HEAD)
        query_one = jnp.where(own, query, nothing)
        grad_one = jnp.where(own, grad, nothing)
        logged = log_ref[pl.ds(2 * pair + head, 1), :]
        inner = jnp.zeros((8, rows), F32)
        for chunk in range(4):
            base = (place ^ chunk) * rows
            for part in range(rows // block):
                span = pl.ds(part * block, block)
                at = pl.ds(chunk * rows + part * block, block)
                bias = jnp.where(base + part * block + row < length, 0.0, NEG).astype(F32)
                scores = contract_cols(keys[chunk][span, :], query_one)
                probs = jnp.exp2(scores * factor + (bias - logged))
                dp = contract_cols(values[chunk][span, :], grad_one)
                inner += jnp.sum((probs * dp).reshape(block // 8, 8, rows), axis=0)
                probs_ref[at, :] = probs
                dp_ref[at, :] = dp
        inner = jnp.sum(inner, axis=0, keepdims=True)
        for chunk in range(4):
            slot, out = 2 * (chunk // 2), (own_ref, give_ref)[chunk % 2]
            for part in range(rows // block):
                span = pl.ds(part * block, block)
                at = pl.ds(chunk * rows + part * block, block)
                probs = probs_ref[at, :]
                ds = (probs * (dp_ref[at, :] - inner)).astype(BF)
                key = keys[chunk][span, :]
                dv = jnp.dot(probs.astype(BF), grad_one, preferred_element_type=F32)
                dk = jnp.dot(ds, query_one, preferred_element_type=F32)
                dq += contract_rows(jnp.where(own, key, jnp.zeros_like(key)), ds)
                if head == 0:
                    out[slot, span, :] = dk.astype(out.dtype)
                    out[slot + 1, span, :] = dv.astype(out.dtype)
                else:
                    out[slot, span, :] = jnp.where(own, dk.astype(out.dtype), out[slot, span, :])
                    out[slot + 1, span, :] = jnp.where(
                        own, dv.astype(out.dtype), out[slot + 1, span, :]
                    )
    dq_ref[...] = jnp.transpose(dq)


def pull(info, queries, grads, logs, chunks, first_pair, pairs):
    rows = queries.shape[0]
    column = pl.BlockSpec((rows, 128), lambda p: (0, first_pair + p))
    later = pl.BlockSpec((rows, 128), lambda p: (0, PAIRS + first_pair + p))
    width = pairs * 128
    return pl.pallas_call(
        functools.partial(pull_kernel, first_pair),
        out_shape=[
            jax.ShapeDtypeStruct((rows, width), F32),
            jax.ShapeDtypeStruct((4, rows, width), F32),
            jax.ShapeDtypeStruct((4, rows, width), BF),
        ],
        grid=(pairs,),
        in_specs=[
            pl.BlockSpec(memory_space=pltpu.SMEM),
            column,
            column,
            pl.BlockSpec((16, rows), lambda p: (0, 0)),
        ]
        + [column] * 4
        + [later] * 4,
        out_specs=[
            pl.BlockSpec((rows, 128), lambda p: (0, p)),
            pl.BlockSpec((4, rows, 128), lambda p: (0, 0, p)),
            pl.BlockSpec((4, rows, 128), lambda p: (0, 0, p)),
        ],
        scratch_shapes=[
            pltpu.VMEM((4 * rows, rows), F32),
            pltpu.VMEM((4 * rows, rows), F32),
        ],
        cost_estimate=cost(
            10 * rows * 4 * rows * width, 2 * rows * 24 * width, rows * 4 * rows * width // HEAD
        ),
        name="pull",
    )(info, queries, grads, logs, *chunks, *chunks)


def unturn_kernel(halves, *refs):
    cos_ref, first_ref, second_ref, out_ref = refs[4 * halves :]
    wide, first, second = cos_ref[...], -first_ref[...], -second_ref[...]
    column = 0
    for half in range(halves):
        dq_ref, own_ref, near_ref, far_ref = refs[4 * half : 4 * half + 4]
        width = dq_ref.shape[1]
        for part in range(width // 128):
            span = slice(part * 128, part * 128 + 128)
            at = column + part * 128
            out_ref[:, at : at + 128] = turn(dq_ref[:, span] * SCALE, wide, first, second).astype(
                BF
            )
            dk = own_ref[0, :, span] + near_ref[0, :, span].astype(F32)
            dk = (dk + far_ref[0, :, span].astype(F32)) * SCALE
            out_ref[:, D + at : D + at + 128] = turn(dk, wide, first, second).astype(BF)
            dv = own_ref[1, :, span] + near_ref[1, :, span].astype(F32)
            dv = dv + far_ref[1, :, span].astype(F32)
            out_ref[:, 2 * D + at : 2 * D + at + 128] = dv.astype(BF)
        column += width


def unturn(parts, tables):
    rows = tables[0].shape[0]
    specs, arrays = [], []
    for dq, own, near, far in parts:
        width = dq.shape[1]
        pair = pl.BlockSpec((2, rows, width), lambda i: (0, 0, 0))
        specs += [pl.BlockSpec((rows, width), lambda i: (0, 0)), pair, pair, pair]
        arrays += [dq, own, near, far]
    specs += [pl.BlockSpec((rows, 128), lambda i: (0, 0))] * 3
    return pl.pallas_call(
        functools.partial(unturn_kernel, len(parts)),
        out_shape=jax.ShapeDtypeStruct((rows, 3 * D), BF),
        grid=(1,),
        in_specs=specs,
        out_specs=pl.BlockSpec((rows, 3 * D), lambda i: (0, 0)),
        cost_estimate=cost(20 * rows * 3 * D, rows * D * 30),
        name="unturn",
    )(*arrays, *tables)


def piece_bits(order, index):
    picked = dict(zip(order, ((index >> 2) & 1, (index >> 1) & 1, index & 1)))
    return picked["y"], picked["x"], picked["z"]


def rows_kernel(order, lefts, spots_ref, *refs):
    left_refs = refs[: 2 * lefts]
    right_refs = refs[2 * lefts : 4 * lefts]
    keep_ref, send_ref, turned_ref, picked_ref = refs[4 * lefts :]
    step = pl.program_id(0)
    y, core, x, z = spots_ref[0], spots_ref[1], spots_ref[2], spots_ref[3]
    rows = left_refs[0].shape[0]
    high = D // 16

    def pick(own_ref, other_ref):
        turned_ref[:, 0:rows] = jnp.transpose(own_ref[...])
        turned_ref[:, rows : 2 * rows] = jnp.transpose(other_ref[...])
        for index in range(8):
            dy, dx, dz = piece_bits(order, index)
            start = (y ^ dy) * (D // 2) + core * (D // 4) + ((x ^ dx) * 2 + (z ^ dz)) * high
            picked_ref[index * high : index * high + high, :] = turned_ref[
                pl.ds(pl.multiple_of(start, 16), high), :
            ]

    def multiply(own_ref, other_ref):
        product = jnp.dot(picked_ref[:, 0:rows], own_ref[...], preferred_element_type=F32)
        product += jnp.dot(
            picked_ref[:, rows : 2 * rows], other_ref[...], preferred_element_type=F32
        )
        span = pl.ds(pl.multiple_of(step * high, 16), high)
        for index in range(4):
            keep_ref[index, span, :] = product[index * high : index * high + high, :]
            send_ref[index, span, :] = product[
                (4 + index) * high : (4 + index) * high + high, :
            ].astype(BF)

    @pl.when(step == 0)
    def _():
        pick(left_refs[0], left_refs[1])

    if lefts == 1:
        multiply(right_refs[0], right_refs[1])
    else:

        @pl.when(step < 3)
        def _():
            multiply(right_refs[0], right_refs[1])

        @pl.when(step == 3)
        def _():
            pick(left_refs[2], left_refs[3])
            multiply(right_refs[2], right_refs[3])


def rows_unit(spots, order, lefts, rights):
    rows = lefts[0][0].shape[0]
    specs, arrays = [], []
    for own, other in lefts:
        specs += [pl.BlockSpec((rows, D), lambda b, spots: (0, 0))] * 2
        arrays += [own, other]
    for own, other in rights:
        last = own.shape[1] // D - 1
        specs += [
            pl.BlockSpec((rows, D), lambda b, spots, last=last: (0, jnp.minimum(b, last)))
        ] * 2
        arrays += [own, other]
    return pl.pallas_call(
        functools.partial(rows_kernel, order, len(lefts)),
        out_shape=[
            jax.ShapeDtypeStruct((4, D // 4, D), F32),
            jax.ShapeDtypeStruct((4, D // 4, D), BF),
        ],
        grid_spec=pltpu.PrefetchScalarGridSpec(
            num_scalar_prefetch=1,
            grid=(4,),
            in_specs=specs,
            out_specs=[pl.BlockSpec((4, D // 4, D), lambda b, spots: (0, 0, 0))] * 2,
            scratch_shapes=[
                pltpu.VMEM((D, 2 * rows), BF),
                pltpu.VMEM((D // 2, 2 * rows), BF),
            ],
        ),
        cost_estimate=cost(4 * rows * (D // 2) * 4 * D, rows * D * 20 + 3 * D * D),
        name="rows_unit",
    )(spots, *arrays)


def blocks_kernel(order, spots_ref, a0, a1, b0, b1, own_ref, other_ref, keep_ref, send_ref, turned_ref):
    x, z = spots_ref[2], spots_ref[3]
    rows = own_ref.shape[0]
    high = D // 4
    for dy, (mine, partner) in enumerate(((a0, a1), (b0, b1))):
        turned_ref[dy, :, 0:rows] = jnp.transpose(mine[...])
        turned_ref[dy, :, rows : 2 * rows] = jnp.transpose(partner[...])
        for dx in range(2):
            for dz in range(2):
                start = pl.multiple_of(((x ^ dx) * 2 + (z ^ dz)) * high, 16)
                left = turned_ref[dy, pl.ds(start, high), :]
                product = jnp.dot(left[:, 0:rows], own_ref[...], preferred_element_type=F32)
                product += jnp.dot(
                    left[:, rows : 2 * rows], other_ref[...], preferred_element_type=F32
                )
                index = [k for k in range(8) if piece_bits(order, k) == (dy, dx, dz)][0]
                if index < 4:
                    keep_ref[index, :, :] = product
                else:
                    send_ref[index - 4, :, :] = product.astype(BF)


def blocks_unit(spots, order, left, right):
    rows = left[0].shape[0]
    wanted = [
        pl.BlockSpec((rows, D), lambda i, spots, dy=dy: (0, (spots[0] ^ dy) * 2 + spots[1]))
        for dy in (0, 1)
    ]
    whole = pl.BlockSpec((rows, D), lambda i, spots: (0, 0))
    return pl.pallas_call(
        functools.partial(blocks_kernel, order),
        out_shape=[
            jax.ShapeDtypeStruct((4, D // 4, D), F32),
            jax.ShapeDtypeStruct((4, D // 4, D), BF),
        ],
        grid_spec=pltpu.PrefetchScalarGridSpec(
            num_scalar_prefetch=1,
            grid=(1,),
            in_specs=[wanted[0], wanted[0], wanted[1], wanted[1], whole, whole],
            out_specs=[pl.BlockSpec((4, D // 4, D), lambda i, spots: (0, 0, 0))] * 2,
            scratch_shapes=[pltpu.VMEM((2, D, 2 * rows), BF)],
        ),
        cost_estimate=cost(4 * rows * (D // 2) * 4 * D, rows * D * 20 + 3 * D * D),
        name="blocks_unit",
    )(spots, left[0], left[1], left[0], left[1], right[0], right[1])


AXES = {"y": ("fsdp", 2), "x": ("dp", 1), "z": ("dp", 2)}


class Sum:
    def __init__(self, line, unit, order):
        self.line, self.order, self.stage = line, order, 0
        self.keep, send = unit
        self.moving = swap(send, *AXES[order[0]])
        self.far = [1 << k for k in range(2, 20) if (1 << k) < lax.axis_size("dp")]
        self.rest = [name for name in order if name != "y"]

    def step(self):
        got, keep = self.line.enter(self.moving, self.keep)
        line, stage = self.line, self.stage
        self.stage += 1
        if stage < 3:
            total = keep + got.astype(F32)
            if stage < 2:
                half = total.shape[0] // 2
                self.keep, send = total[:half], total[half:].astype(BF)
                line.leave(self.keep, send)
                self.moving = swap(send, *AXES[self.order[stage + 1]])
                return
            self.keep = total.astype(BF)
        elif stage < 3 + len(self.far):
            self.keep = (keep.astype(F32) + got.astype(F32)).astype(BF)
        elif stage == 3 + len(self.far):
            self.keep = jnp.concatenate([keep, got], axis=0)
            line.leave(self.keep)
            self.moving = swap(self.keep, *AXES[self.rest[0]])
            return
        else:
            self.result = (keep, got)
            return
        line.leave(self.keep)
        if stage - 2 < len(self.far):
            self.moving = swap(self.keep, "dp", self.far[stage - 2])
        else:
            self.moving = swap(self.keep, *AXES[self.rest[1]])

    def finish(self):
        while self.stage < 5 + len(self.far):
            self.step()
        return self.result


def emit_kernel(order, kinds, layer, spots_ref, first_ref, second_ref, *refs):
    outs = refs[-len(kinds) :]
    rest = [name for name in order if name != "y"]
    x, z = spots_ref[2], spots_ref[3]
    high = D // 16
    for outer in range(2):
        for inner in range(2):
            picked = dict(zip(rest, (outer, inner)))
            which = (x ^ picked["x"]) * 2 + (z ^ picked["z"])
            piece = (first_ref, second_ref)[outer]
            at = 0
            for slot, kind in enumerate(kinds):
                if kind == 0:
                    start = pl.multiple_of(which * 4 * high, 16)
                    outs[slot][0, pl.ds(start, 4 * high), :] = piece[
                        inner, at : at + 4 * high, :
                    ].astype(F32)
                    at += 4 * high
                    continue
                start = pl.multiple_of(which * high, 16)
                for part in range(kind):
                    outs[slot][0, pl.ds(start, high), part * D : part * D + D] = piece[
                        inner, at : at + high, :
                    ].astype(F32)
                    at += high


def emit(spots, pieces, order, kinds, layer, before):
    shapes = [(D // 4, k * D) if k else (D, D) for k in kinds]
    out_shape = [jax.ShapeDtypeStruct((LAYERS,) + shape, F32) for shape in shapes]
    before = list(before) if before is not None else []
    whole = pl.BlockSpec(pieces[0].shape, lambda i, spots: (0, 0, 0))
    return pl.pallas_call(
        functools.partial(emit_kernel, order, kinds, layer),
        out_shape=out_shape,
        grid_spec=pltpu.PrefetchScalarGridSpec(
            num_scalar_prefetch=1,
            grid=(1,),
            in_specs=[whole, whole] + [pl.BlockSpec(memory_space=pl.ANY)] * len(before),
            out_specs=[
                pl.BlockSpec((1,) + shape, lambda i, spots: (layer, 0, 0)) for shape in shapes
            ],
        ),
        input_output_aliases={3 + i: i for i in range(len(before))},
        cost_estimate=cost(0, D * D * 6),
        name="emit",
    )(spots, *pieces, *before)


class Line:
    def __init__(self):
        self.last = ()

    def enter(self, *values):
        out = lax.optimization_barrier(tuple(values) + tuple(self.last))
        return out[: len(values)]

    def leave(self, *values):
        self.last = tuple(values)

    def sync(self, *values):
        out = self.enter(*values)
        self.last = tuple(out)
        return out


def after(value, *others):
    return lax.optimization_barrier((value,) + others)[0]


NAMES = (
    "input_bias",
    "output_bias",
    "first_gain",
    "first_shift",
    "up_bias",
    "down_bias",
    "second_gain",
    "second_shift",
)
WIDTHS = (3 * D, D, D, D, 4 * D, D, D, D)


def feed_forward(hidden, context, weights, small):
    _, output_weight, up_weight, down_weight = weights
    attn_out = jnp.dot(context, output_weight, preferred_element_type=F32) + small["output_bias"]
    first_in = hidden + attn_out
    normed = layer_norm(first_in, small["first_gain"], small["first_shift"])
    normed_low = normed.astype(BF)
    up_value = jnp.dot(normed_low, up_weight, preferred_element_type=F32) + small["up_bias"]
    activated = gelu_exact(up_value).astype(BF)
    down_value = (
        jnp.dot(activated, down_weight, preferred_element_type=F32) + small["down_bias"]
    )
    second_in = normed + down_value
    output = layer_norm(second_in, small["second_gain"], small["second_shift"])
    return output, first_in, normed_low, up_value, activated, second_in


def feed_backward(grad_output, weights, small, first_in, up_value, second_in):
    _, output_weight, up_weight, down_weight = weights
    pull_second = jax.vjp(layer_norm, second_in, small["second_gain"], small["second_shift"])[1]
    grad_second, grad_second_gain, grad_second_shift = pull_second(grad_output)
    grad_down = grad_second.astype(BF)
    grad_down_bias = jnp.sum(grad_down, axis=0, dtype=F32)
    grad_activated = contract_cols(grad_down, down_weight)
    pull_gelu = jax.vjp(gelu_exact, up_value)[1]
    grad_up = pull_gelu(grad_activated)[0].astype(BF)
    grad_up_bias = jnp.sum(grad_up, axis=0, dtype=F32)
    grad_normed = grad_second + contract_cols(grad_up, up_weight)
    pull_first = jax.vjp(layer_norm, first_in, small["first_gain"], small["first_shift"])[1]
    grad_first, grad_first_gain, grad_first_shift = pull_first(grad_normed)
    grad_attn = grad_first.astype(BF)
    grad_output_bias = jnp.sum(grad_attn, axis=0, dtype=F32)
    grad_context = contract_cols(grad_attn, output_weight).astype(BF)
    little = (
        grad_output_bias,
        grad_first_gain,
        grad_first_shift,
        grad_up_bias,
        grad_down_bias,
        grad_second_gain,
        grad_second_shift,
    )
    return grad_down, grad_up, grad_attn, grad_context, grad_first, little


def sum_little(littles, place):
    flat = jnp.concatenate(
        [part.reshape(4, -1) for layer in littles for part in layer], axis=1
    ).reshape(2, 2, -1)
    for axis, bit, dim in (("fsdp", 1, 1), ("fsdp", 2, 0)):
        mine = (place & 1) if bit == 1 else (place >> 1)
        keep = lax.dynamic_slice_in_dim(flat, mine, 1, dim)
        send = lax.dynamic_slice_in_dim(flat, 1 - mine, 1, dim)
        flat = keep + swap(send, axis, bit)
    bit = 1
    while bit < lax.axis_size("dp"):
        flat = flat + swap(flat, "dp", bit)
        bit *= 2
    return flat.reshape(LAYERS, -1)


UP_ORDER = ("xzy", "xzy")
DOWN_ORDER = ("yxz", "zxy")
JOINT_ORDER = ("yxz", "yzx")


def on_device(
    tokens,
    cotangent,
    lengths,
    input_weight,
    input_bias,
    output_weight,
    output_bias,
    first_gain,
    first_shift,
    up_weight,
    up_bias,
    down_weight,
    down_bias,
    second_gain,
    second_shift,
):
    place = lax.axis_index("fsdp")
    group = lax.axis_index("dp")
    core = place & 1
    x_bit, z_bit = group & 1, (group >> 1) & 1
    spots = jnp.stack([place >> 1, core, x_bit, z_bit]).astype(jnp.int32)
    row_count = tokens.shape[0]
    places = place * row_count + jnp.arange(row_count, dtype=jnp.int32)
    length = lengths[0]
    info = jnp.stack([place, length]).astype(jnp.int32)
    row_valid = (places < length).astype(F32)

    swap_core = lambda value: swap(value, "fsdp", 1)
    swap_y = lambda value: swap(value, "fsdp", 2)
    swap_x = lambda value: swap(value, "dp", 1)
    swap_z = lambda value: swap(value, "dp", 2)

    rows_of = D // 4
    quarter = rows_of // 4
    start = (x_bit * 2 + z_bit) * quarter
    quarters = [
        x_bit * 2 + z_bit,
        x_bit * 2 + (1 - z_bit),
        (1 - x_bit) * 2 + z_bit,
        (1 - x_bit) * 2 + (1 - z_bit),
    ]
    spread_spots = jnp.stack(
        [place * rows_of, (place ^ 1) * rows_of]
        + [(place ^ 2) * rows_of + q * quarter for q in quarters]
        + [(place ^ 3) * rows_of + q * quarter for q in quarters]
    ).astype(jnp.int32)
    direct_spots = jnp.stack([(place ^ k) * rows_of for k in range(4)]).astype(jnp.int32)
    rest_spec = (("rows", D), ("rows", 4 * D), ("split", 4 * D))

    def wide(i):
        split = [down_weight[i, k * 192 : k * 192 + 192] for k in range(4)]
        return jnp.concatenate([output_weight[i], up_weight[i]] + split, axis=1)

    line = Line()

    input_one, input_two = input_weight[0], input_weight[1]
    over_y = swap_y(input_one)
    packed = jnp.concatenate(
        (
            input_bias,
            output_bias,
            first_gain,
            first_shift,
            up_bias,
            down_bias,
            second_gain,
            second_shift,
        ),
        axis=1,
    )
    packed_y, packed_c, input_c = swap_y(packed), swap_core(packed), swap_core(input_one)
    tables = rotary_tables(places.astype(F32))
    rests = (wide(0), wide(1))
    mine = [lax.dynamic_slice(r, (start, 0), (quarter, r.shape[1])) for r in rests]
    line.leave(*mine)
    over_y, packed_y, packed_c, input_c = line.sync(over_y, packed_y, packed_c, input_c)
    spread_y = swap_y(after(mine[0], over_y))
    rest_c = swap_core(after(rests[0], over_y))
    packed_yc, input_yc = swap_core(packed_y), swap_core(over_y)
    fields = unpack(info, [packed, packed_c, packed_y, packed_yc], WIDTHS)
    smalls = [
        dict(zip(NAMES, fields[i * len(NAMES) : (i + 1) * len(NAMES)])) for i in range(LAYERS)
    ]
    pieces = [input_one, input_c, over_y, input_yc]
    line.leave(*fields)
    hidden, rounded = tokens.astype(F32), tokens
    kept, weights = [], []
    for i in range(LAYERS):
        more = i + 1 < LAYERS
        small = smalls[i]
        pieces = line.enter(*pieces)
        queries, kv, whole = project(rounded, pieces, direct_spots, small["input_bias"], tables)
        line.leave(queries, kv, whole)
        kv_y, kv_c = swap_y(kv), swap_core(kv)
        spread_y, rest_c = line.sync(spread_y, rest_c)
        spread_z, spread_x = swap_z(spread_y), swap_x(spread_y)
        spread_yc = swap_core(spread_y)
        spread_z, spread_x = line.sync(spread_z, spread_x)
        spread_xz = swap_x(spread_z)
        spread_zc, spread_xc = swap_core(spread_z), swap_core(spread_x)
        kv_y, kv_c, spread_yc = line.sync(kv_y, kv_c, spread_yc)
        kv_yc = swap_core(kv_y)
        kv_yc, spread_zc, spread_xc = line.sync(kv_yc, spread_zc, spread_xc)
        chunks = [kv, kv_c, kv_y, kv_yc]
        if more:
            over_y, input_c = swap_y(after(input_two, kv_yc)), swap_core(after(input_two, kv_yc))
        (queries,) = line.enter(queries)
        context, logs = attend(info, queries, chunks)
        line.leave(context, logs)
        if more:
            spread_xz, over_y, input_c = line.sync(spread_xz, over_y, input_c)
            next_y = swap_y(after(mine[1], over_y))
            input_yc = swap_core(over_y)
        else:
            (spread_xz,) = line.sync(spread_xz)
        pieces = [rests[i], rest_c, spread_y, spread_z, spread_x, spread_xz]
        pieces += [spread_yc, spread_zc, spread_xc, swap_core(spread_xz)]
        rest = assemble(pieces, spread_spots, rest_spec)
        weights.append((whole, *rest))
        line.leave(*rest)
        if more:
            rest_c = swap_core(after(rests[1], rest[0]))
        (context_in,) = line.enter(context)
        output, first_in, normed, up_value, activated, second_in = feed_forward(
            hidden, context_in, weights[i], small
        )
        kept.append(
            (rounded, queries, chunks, logs, context, first_in, normed, up_value, activated, second_in)
        )
        hidden, rounded = output, output.astype(BF)
        line.leave(hidden, rounded)
        if more:
            spread_y = next_y
            pieces = [input_two, input_c, over_y, input_yc]
    result = rounded

    def both_cores(*values):
        values = line.enter(*values)
        return [(value, swap_core(value)) for value in values]

    def feed_back(grad_output, i):
        (grad_output,) = line.enter(grad_output)
        _, _, _, _, _, first_in, _, up_value, _, second_in = kept[i]
        out = feed_backward(grad_output, weights[i], smalls[i], first_in, up_value, second_in)
        line.leave(*out[:5])
        return out

    def attention_back(i, grad_context, part):
        queries, chunks, logs = kept[i][1:4]
        (grad_context,) = line.enter(grad_context)
        dq, own, give = pull(info, queries, grad_context, logs, chunks, 2 * part, 2)
        line.leave(dq, own, give)
        return dq, own, swap_core(give)

    def far_back(pulled):
        dq, own, near = pulled
        own, near = line.enter(own, near)
        far = (own[2:] + near[2:].astype(F32)).astype(BF)
        line.leave(far)
        return dq, own, near, swap_y(far)

    def arrive(far):
        dq, own, near, moving = far
        (moving,) = line.sync(moving)
        return dq, own, near, moving

    def up_sum(i, normed, grad_up):
        left, right = line.enter(normed[1], grad_up[1])
        unit = rows_unit(spots, UP_ORDER[i], [(normed[0], left)], [(grad_up[0], right)])
        line.leave(*unit)
        return Sum(line, unit, UP_ORDER[i])

    def down_sum(i, activated, grad_down):
        left, right = line.enter(activated[1], grad_down[1])
        unit = blocks_unit(spots, DOWN_ORDER[i], (activated[0], left), (grad_down[0], right))
        line.leave(*unit)
        return Sum(line, unit, DOWN_ORDER[i])

    def joint_sum(i, rounded, grad_joint, context, grad_attn):
        got = line.enter(rounded[1], grad_joint[1], context[1], grad_attn[1])
        pairs = [(p[0], g) for p, g in zip((rounded, grad_joint, context, grad_attn), got)]
        unit = rows_unit(spots, JOINT_ORDER[i], [pairs[0], pairs[2]], [pairs[1], pairs[3]])
        line.leave(*unit)
        return Sum(line, unit, JOINT_ORDER[i])

    def joint_back(i, parts, grad_first):
        flat = line.enter(*[v for part in parts for v in part])
        parts = [flat[4 * k : 4 * k + 4] for k in range(len(parts))]
        grad_joint = unturn(parts, tables)
        line.leave(grad_joint)
        grad_hidden = grad_first + contract_cols(grad_joint, weights[i][0])
        return grad_joint, jnp.sum(grad_joint, axis=0, dtype=F32), grad_hidden

    grad_hidden = cotangent.astype(F32) * row_valid[:, None]
    act2, normed2 = both_cores(kept[1][8], kept[1][6])
    dd2, du2, da2, dc2, grad_first2, little2 = feed_back(grad_hidden, 1)
    dd2, du2 = both_cores(dd2, du2)
    p0 = attention_back(1, dc2, 0)
    p1 = attention_back(1, dc2, 1)
    p0 = far_back(p0)
    p2 = attention_back(1, dc2, 2)
    p0 = arrive(p0)
    p1 = far_back(p1)
    up2 = up_sum(1, normed2, du2)
    p1 = arrive(p1)
    p2 = far_back(p2)
    down2 = down_sum(1, act2, dd2)
    joint2, bias2, grad_hidden = joint_back(1, (p0, p1, p2), grad_first2)
    up2.step()
    rounded2, context2, da2, joint2 = both_cores(kept[1][0], kept[1][4], da2, joint2)
    act1, normed1 = both_cores(kept[0][8], kept[0][6])
    dd1, du1, da1, dc1, grad_first1, little1 = feed_back(grad_hidden, 0)
    down2.step()
    up2.step()
    dd1, du1 = both_cores(dd1, du1)
    j2 = joint_sum(1, rounded2, joint2, context2, da2)
    p0 = attention_back(0, dc1, 0)
    down2.step()
    up2.step()
    p1 = attention_back(0, dc1, 1)
    p0 = far_back(p0)
    j2.step()
    p2 = attention_back(0, dc1, 2)
    p0 = arrive(p0)
    p1 = far_back(p1)
    up2.step()
    down2.step()
    up1 = up_sum(0, normed1, du1)
    p1 = arrive(p1)
    p2 = far_back(p2)
    j2.step()
    down2.step()
    down1 = down_sum(0, act1, dd1)
    joint1, bias1, grad_hidden = joint_back(0, (p0, p1, p2), grad_first1)
    rounded1, context1, da1, joint1 = both_cores(kept[0][0], kept[0][4], da1, joint1)
    up1.step()
    down2.step()
    j1 = joint_sum(0, rounded1, joint1, context1, da1)
    littles = [(bias1, *little1), (bias2, *little2)]
    flat = sum_little(littles, place)
    for _ in range(5):
        for chain in (down1, up1, j2, j1):
            if chain.stage < 4:
                chain.step()
    out_up = emit(spots, up2.finish(), UP_ORDER[1], (4,), 1, None)
    out_down = emit(spots, down2.finish(), DOWN_ORDER[1], (0,), 1, None)
    out_joint = emit(spots, j2.finish(), JOINT_ORDER[1], (3, 1), 1, None)
    out_up = emit(spots, up1.finish(), UP_ORDER[0], (4,), 0, out_up)
    out_down = emit(spots, down1.finish(), DOWN_ORDER[0], (0,), 0, out_down)
    out_joint = emit(spots, j1.finish(), JOINT_ORDER[0], (3, 1), 0, out_joint)

    small_grads = {}
    offset = 0
    for name, width in zip(NAMES, WIDTHS):
        small_grads[name] = flat[:, offset : offset + width // 4]
        offset += width // 4
    return (
        result,
        grad_hidden,
        out_joint[0],
        small_grads["input_bias"],
        out_joint[1],
        small_grads["output_bias"],
        small_grads["first_gain"],
        small_grads["first_shift"],
        out_up[0],
        small_grads["up_bias"],
        out_down[0],
        small_grads["down_bias"],
        small_grads["second_gain"],
        small_grads["second_shift"],
    )


def solution(mesh):
    rows = P(("dp", "fsdp"), None)
    matrix = P(None, "fsdp", None)
    vector = P(None, "fsdp")
    parameters = (
        matrix,
        vector,
        matrix,
        vector,
        vector,
        vector,
        matrix,
        vector,
        matrix,
        vector,
        vector,
        vector,
    )
    return jax.shard_map(
        on_device,
        mesh=mesh,
        in_specs=(rows, rows, P("dp"), *parameters),
        out_specs=(rows, rows, *parameters),
        check_vma=False,
    )
```

```python
import functools

import jax
import jax.numpy as jnp
from jax import lax
from jax.experimental import pallas as pl
from jax.experimental.pallas import tpu as pltpu
from jax.sharding import PartitionSpec as P

D = 768
HEADS = 12
HEAD = 64
PAIRS = HEADS // 2
LAYERS = 2
PARTS = 3
GROUP = PAIRS // PARTS
WIDE = GROUP * 128
LOG2E = 1.4426950408889634
SCALE = HEAD ** (-0.5)
NEG = -1e30
BF = jnp.bfloat16
F32 = jnp.float32

norm_eps = 1e-12


def swap(value, axis, bit):
    count = lax.axis_size(axis)
    return lax.ppermute(value, axis, [(i, i ^ bit) for i in range(count)])


def layer_norm(matrix, norm_gain, norm_shift):
    row_mean = jnp.mean(matrix, axis=-1, keepdims=True)
    centred = matrix - row_mean
    spread = jnp.mean(centred * centred, axis=-1, keepdims=True)
    return centred * lax.rsqrt(spread + norm_eps) * norm_gain + norm_shift


def normal_part(value):
    return 0.5 + 0.5 * lax.erf(value * 0.7071067811865476)


def gelu_slope(value):
    return normal_part(value) + value * jnp.exp(-0.5 * value * value) * 0.3989422804014327


def contract_rows(left_side, right_side):
    return lax.dot_general(
        left_side, right_side, (((0,), (0,)), ((), ())), preferred_element_type=F32
    )


def contract_cols(left_side, right_side):
    return lax.dot_general(
        left_side, right_side, (((1,), (1,)), ((), ())), preferred_element_type=F32
    )


def cost(flops, bytes_accessed, transcendentals=0):
    return pl.CostEstimate(
        flops=int(flops), bytes_accessed=int(bytes_accessed), transcendentals=int(transcendentals)
    )


def rotary_tables(places):
    frequency = 10000.0 ** (-2.0 * jnp.arange(HEAD // 2, dtype=F32) / HEAD)
    angles = places[:, None] * frequency[None, :]
    cosine, sine = jnp.cos(angles), jnp.sin(angles)
    nothing = jnp.zeros_like(sine)
    wide = jnp.concatenate([cosine] * 4, axis=1)
    first = jnp.concatenate([-sine, nothing] * 2, axis=1)
    second = jnp.concatenate([nothing, sine] * 2, axis=1)
    return wide, first, second


def turn(block, wide, first, second):
    return (
        block * wide
        + pltpu.roll(block, 96, 1) * first
        + pltpu.roll(block, 32, 1) * second
    )


def assemble_kernel(spec, count, pos_ref, *refs):
    pieces = refs[:count]
    outs = refs[count : count + len(spec)]
    held, in_sem, out_sem = refs[count + len(spec) :]
    copies = []
    for index, piece in enumerate(pieces):
        rows = piece.shape[0]
        start = pl.multiple_of(pos_ref[index], 16)
        copies.append(
            pltpu.make_async_copy(piece, held.at[pl.ds(start, rows), :], in_sem.at[index])
        )
    for copy in copies:
        copy.start()
    for copy in copies:
        copy.wait()
    copies = []
    column = 0
    for slot, (kind, width) in enumerate(spec):
        if kind == "rows":
            copies.append((held.at[:, pl.ds(column, width)], outs[slot]))
        else:
            shard = held.shape[0] // 4
            for source in range(4):
                for part in range(width // D):
                    copies.append(
                        (
                            held.at[pl.ds(source * shard, shard), pl.ds(column + part * D, D)],
                            outs[slot].at[pl.ds(source * 4 * shard + part * shard, shard), :],
                        )
                    )
        column += width
    copies = [
        pltpu.make_async_copy(src, dst, out_sem.at[index])
        for index, (src, dst) in enumerate(copies)
    ]
    for copy in copies:
        copy.start()
    for copy in copies:
        copy.wait()


def assemble(pieces, positions, spec):
    width = pieces[0].shape[1]
    out_shape = []
    outputs = 0
    for kind, columns in spec:
        if kind == "rows":
            out_shape.append(jax.ShapeDtypeStruct((D, columns), BF))
            outputs += 1
        else:
            out_shape.append(jax.ShapeDtypeStruct((columns, D), BF))
            outputs += 4 * (columns // D)
    return pl.pallas_call(
        functools.partial(assemble_kernel, spec, len(pieces)),
        out_shape=out_shape,
        in_specs=[pl.BlockSpec(memory_space=pltpu.SMEM)]
        + [pl.BlockSpec(memory_space=pl.ANY)] * len(pieces),
        out_specs=[pl.BlockSpec(memory_space=pl.ANY)] * len(spec),
        scratch_shapes=[
            pltpu.VMEM((D, width), BF),
            pltpu.SemaphoreType.DMA((len(pieces),)),
            pltpu.SemaphoreType.DMA((outputs,)),
        ],
        cost_estimate=cost(0, 4 * D * width),
        name="assemble",
    )(positions, *pieces)


def pack_kernel(*refs):
    *parts, out_ref = refs
    offset = 0
    for part in parts:
        width = part.shape[1] // 4
        for owner in range(4):
            out_ref[owner : owner + 1, offset : offset + width] = part[
                :, owner * width : owner * width + width
            ]
        offset += width


def spread_kernel(count, flat_ref, *outs):
    offset = 0
    for layer in range(LAYERS):
        for slot in range(count):
            width = outs[slot].shape[1]
            outs[slot][layer : layer + 1, :] = flat_ref[:, offset : offset + width]
            offset += width


def pack(parts):
    vmem = pl.BlockSpec(memory_space=pltpu.VMEM)
    width = sum(part.shape[1] for part in parts) // 4
    return pl.pallas_call(
        pack_kernel,
        out_shape=jax.ShapeDtypeStruct((4, width), F32),
        in_specs=[vmem] * len(parts),
        out_specs=vmem,
        cost_estimate=cost(0, 200000),
        name="pack",
    )(*parts)


def spread(flat, widths):
    vmem = pl.BlockSpec(memory_space=pltpu.VMEM)
    return pl.pallas_call(
        functools.partial(spread_kernel, len(widths)),
        out_shape=[jax.ShapeDtypeStruct((LAYERS, width // 4), F32) for width in widths],
        in_specs=[vmem],
        out_specs=[vmem] * len(widths),
        cost_estimate=cost(0, 50000),
        name="spread",
    )(flat)


def project_kernel(count, pos_ref, h_ref, b_ref, cos_ref, first_ref, second_ref, *refs):
    pieces = refs[:count]
    q_ref, *kv_refs, whole_ref, held, in_sem, out_sem = refs[count:]
    copies = []
    for part in range(3):
        for index, piece in enumerate(pieces):
            rows = piece.shape[0]
            start = pl.multiple_of(pos_ref[index], 16)
            copies.append(
                pltpu.make_async_copy(
                    piece.at[:, pl.ds(part * D, D)],
                    held.at[part, pl.ds(start, rows), :],
                    in_sem.at[part * count + index],
                )
            )
    for copy in copies:
        copy.start()
    outs = [
        pltpu.make_async_copy(
            held.at[part], whole_ref.at[:, pl.ds(part * D, D)], out_sem.at[part]
        )
        for part in range(3)
    ]
    for part in range(3):
        for copy in copies[part * count : part * count + count]:
            copy.wait()
        outs[part].start()
        joint = jnp.dot(h_ref[...], held[part], preferred_element_type=F32)
        joint = joint + b_ref[:, part * D : part * D + D]
        if part == 2:
            for index in range(PARTS):
                kv_refs[index][:, WIDE:] = joint[:, index * WIDE : index * WIDE + WIDE].astype(BF)
            continue
        for pair in range(PAIRS):
            span = slice(pair * 128, pair * 128 + 128)
            turned = turn(joint[:, span], cos_ref[...], first_ref[...], second_ref[...]).astype(BF)
            if part == 0:
                q_ref[:, span] = turned
            else:
                at = pair % GROUP * 128
                kv_refs[pair // GROUP][:, at : at + 128] = turned
    for copy in outs:
        copy.wait()


def project(rounded, pieces, positions, bias, tables):
    rows = rounded.shape[0]
    count = len(pieces)
    return pl.pallas_call(
        functools.partial(project_kernel, count),
        out_shape=[
            jax.ShapeDtypeStruct((rows, D), BF),
            *[jax.ShapeDtypeStruct((rows, 2 * WIDE), BF)] * PARTS,
            jax.ShapeDtypeStruct((D, 3 * D), BF),
        ],
        in_specs=[pl.BlockSpec(memory_space=pltpu.SMEM)]
        + [pl.BlockSpec(memory_space=pltpu.VMEM)] * 5
        + [pl.BlockSpec(memory_space=pl.ANY)] * count,
        out_specs=[pl.BlockSpec(memory_space=pltpu.VMEM)] * (1 + PARTS)
        + [pl.BlockSpec(memory_space=pl.ANY)],
        scratch_shapes=[
            pltpu.VMEM((3, D, D), BF),
            pltpu.SemaphoreType.DMA((3 * count,)),
            pltpu.SemaphoreType.DMA((3,)),
        ],
        cost_estimate=cost(2 * rows * D * 3 * D, 2 * (rows * 4 * D + 3 * D * D)),
        name="project",
    )(positions, rounded, bias, *tables, *pieces)


def unpack_kernel(widths, place_ref, *refs):
    pieces, outs, held = refs[:4], refs[4:-1], refs[-1]
    place = place_ref[0]
    for index in range(4):
        held[index] = pieces[index][...].astype(F32)
    for source in range(4):
        shard = held[source ^ place]
        offset = 0
        for slot, width in enumerate(widths):
            part = width // 4
            for layer in range(LAYERS):
                outs[layer * len(widths) + slot][:, source * part : source * part + part] = shard[
                    layer : layer + 1, offset : offset + part
                ]
            offset += part


def unpack(info, pieces, widths):
    vmem = pl.BlockSpec(memory_space=pltpu.VMEM)
    return pl.pallas_call(
        functools.partial(unpack_kernel, widths),
        out_shape=[jax.ShapeDtypeStruct((1, width), F32) for width in widths] * LAYERS,
        in_specs=[pl.BlockSpec(memory_space=pltpu.SMEM)] + [vmem] * 4,
        out_specs=[vmem] * (LAYERS * len(widths)),
        scratch_shapes=[pltpu.VMEM((4,) + pieces[0].shape, F32)],
        cost_estimate=cost(0, 100000),
        name="unpack",
    )(info, *pieces)


def attend_kernel(part, info_ref, q_ref, *refs):
    keys, values = refs[0:4], refs[4:8]
    out_ref, log_ref, column_ref, score_ref, prob_ref = refs[-5:]
    pair = pl.program_id(0)
    rows = q_ref.shape[0]
    place, length = info_ref[0], info_ref[1]
    lane = lax.broadcasted_iota(jnp.int32, (1, 128), 1)
    key_lane = lax.broadcasted_iota(jnp.int32, (1, rows), 1)
    bias = jnp.concatenate(
        [
            jnp.where((place ^ k) * rows + key_lane < length, 0.0, NEG).astype(F32)
            for k in range(4)
        ],
        axis=1,
    )
    factor = SCALE * LOG2E
    block = 32
    query = q_ref[...]
    owns = [(lane >= head * HEAD) & (lane < head * HEAD + HEAD) for head in range(2)]
    for head in range(2):
        masked = jnp.where(owns[head], query, jnp.zeros_like(query))
        for k in range(4):
            score_ref[head, :, k * rows : (k + 1) * rows] = contract_cols(masked, keys[k][...])
    for head in range(2):
        for index in range(rows // block):
            span = slice(index * block, index * block + block)
            scores = score_ref[head, span, :] + bias
            peak = jnp.max(scores, axis=1, keepdims=True)
            powers = jnp.exp2((scores - peak) * factor)
            total = jnp.sum(powers, axis=1, keepdims=True)
            prob_ref[head, span, :] = (powers * (1.0 / total)).astype(BF)
            column_ref[span, :] = jnp.where(
                lane == 2 * pair + head, peak * factor + jnp.log2(total), column_ref[span, :]
            )
    outs = []
    for head in range(2):
        gathered = jnp.dot(prob_ref[head, :, 0:rows], values[0][...], preferred_element_type=F32)
        for k in range(1, 4):
            gathered += jnp.dot(
                prob_ref[head, :, k * rows : (k + 1) * rows],
                values[k][...],
                preferred_element_type=F32,
            )
        outs.append(gathered)
    out_ref[...] = jnp.where(owns[0], outs[0], outs[1]).astype(BF)

    @pl.when(pair == GROUP - 1)
    def _():
        log_ref[...] = jnp.transpose(column_ref[...])[0:8, :]


def attend(info, queries, chunks, part, before):
    rows = queries.shape[0]
    own = pl.BlockSpec((rows, 128), lambda p: (0, part * GROUP + p))
    before = [] if before is None else [before]
    return pl.pallas_call(
        functools.partial(attend_kernel, part),
        out_shape=[
            jax.ShapeDtypeStruct((rows, D), BF),
            jax.ShapeDtypeStruct((8, rows), F32),
        ],
        grid=(GROUP,),
        in_specs=[pl.BlockSpec(memory_space=pltpu.SMEM), own]
        + [pl.BlockSpec((rows, 128), lambda p: (0, p))] * 4
        + [pl.BlockSpec((rows, 128), lambda p: (0, GROUP + p))] * 4
        + [pl.BlockSpec(memory_space=pl.ANY)] * len(before),
        out_specs=[own, pl.BlockSpec((8, rows), lambda p: (0, 0))],
        scratch_shapes=[
            pltpu.VMEM((rows, 128), F32),
            pltpu.VMEM((2, rows, 4 * rows), F32),
            pltpu.VMEM((2, rows, 4 * rows), BF),
        ],
        input_output_aliases={10: 0} if before else {},
        cost_estimate=cost(
            4 * rows * 4 * rows * WIDE, 2 * rows * 10 * WIDE, rows * 8 * rows * GROUP
        ),
        name="attend",
    )(info, queries, *chunks, *chunks, *before)


def pull_kernel(info_ref, q_ref, g_ref, log_ref, *refs):
    keys, values = refs[0:4], refs[4:8]
    dq_ref, own_ref, give_ref = refs[8:11]
    probs_ref, dp_ref, low_ref, ds_ref = refs[11:15]
    pair = pl.program_id(0)
    rows = q_ref.shape[0]
    block = 64
    place, length = info_ref[0], info_ref[1]
    lane = lax.broadcasted_iota(jnp.int32, (1, 128), 1)
    row = lax.broadcasted_iota(jnp.int32, (block, 1), 0)
    factor = SCALE * LOG2E
    query, grad = q_ref[...], g_ref[...]
    nothing = jnp.zeros_like(query)
    owns = [(lane >= head * HEAD) & (lane < head * HEAD + HEAD) for head in range(2)]
    queries = [jnp.where(own, query, nothing) for own in owns]
    grads = [jnp.where(own, grad, nothing) for own in owns]
    for head in range(2):
        for chunk in range(4):
            at = slice(chunk * rows, chunk * rows + rows)
            probs_ref[head, at, :] = contract_cols(keys[chunk][...], queries[head])
            dp_ref[head, at, :] = contract_cols(values[chunk][...], grads[head])
    for head in range(2):
        logged = log_ref[pl.ds(2 * pair + head, 1), :]
        inner = jnp.zeros((8, rows), F32)
        for index in range(4 * rows // block):
            span = slice(index * block, index * block + block)
            chunk, start = divmod(index * block, rows)
            base = (place ^ chunk) * rows + start
            bias = jnp.where(base + row < length, 0.0, NEG).astype(F32)
            probs = jnp.exp2(probs_ref[head, span, :] * factor + (bias - logged))
            probs_ref[head, span, :] = probs
            low_ref[head, span, :] = probs.astype(BF)
            inner += jnp.sum((probs * dp_ref[head, span, :]).reshape(block // 8, 8, rows), axis=0)
        inner = jnp.sum(inner, axis=0, keepdims=True)
        for index in range(4 * rows // block):
            span = slice(index * block, index * block + block)
            ds_ref[head, span, :] = (
                probs_ref[head, span, :] * (dp_ref[head, span, :] - inner)
            ).astype(BF)
    dq = jnp.zeros((128, rows), F32)
    for chunk in range(4):
        slot, out = 2 * (chunk // 2), (own_ref, give_ref)[chunk % 2]
        at = slice(chunk * rows, chunk * rows + rows)
        dk = jnp.dot(ds_ref[0, at, :], queries[0], preferred_element_type=F32)
        dk += jnp.dot(ds_ref[1, at, :], queries[1], preferred_element_type=F32)
        dv = jnp.dot(low_ref[0, at, :], grads[0], preferred_element_type=F32)
        dv += jnp.dot(low_ref[1, at, :], grads[1], preferred_element_type=F32)
        out[slot, :, :] = dk.astype(out.dtype)
        out[slot + 1, :, :] = dv.astype(out.dtype)
        key = keys[chunk][...]
        for head in range(2):
            dq += contract_rows(jnp.where(owns[head], key, nothing), ds_ref[head, at, :])
    dq_ref[...] = jnp.transpose(dq)


def pull(info, queries, grads, logs, chunks, part):
    rows = queries.shape[0]
    own = pl.BlockSpec((rows, 128), lambda p: (0, part * GROUP + p))
    stacked = pl.BlockSpec((4, rows, 128), lambda p: (0, 0, p))
    return pl.pallas_call(
        pull_kernel,
        out_shape=[
            jax.ShapeDtypeStruct((rows, WIDE), F32),
            jax.ShapeDtypeStruct((4, rows, WIDE), F32),
            jax.ShapeDtypeStruct((4, rows, WIDE), BF),
        ],
        grid=(GROUP,),
        in_specs=[
            pl.BlockSpec(memory_space=pltpu.SMEM),
            own,
            own,
            pl.BlockSpec((8, rows), lambda p: (0, 0)),
        ]
        + [pl.BlockSpec((rows, 128), lambda p: (0, p))] * 4
        + [pl.BlockSpec((rows, 128), lambda p: (0, GROUP + p))] * 4,
        out_specs=[pl.BlockSpec((rows, 128), lambda p: (0, p)), stacked, stacked],
        scratch_shapes=[
            pltpu.VMEM((2, 4 * rows, rows), F32),
            pltpu.VMEM((2, 4 * rows, rows), F32),
            pltpu.VMEM((2, 4 * rows, rows), BF),
            pltpu.VMEM((2, 4 * rows, rows), BF),
        ],
        cost_estimate=cost(
            10 * rows * 4 * rows * WIDE, 2 * rows * 24 * WIDE, rows * 4 * rows * 2 * GROUP
        ),
        name="pull",
    )(info, queries, grads, logs, *chunks, *chunks)


def unturn_kernel(halves, *refs):
    cos_ref, first_ref, second_ref, out_ref = refs[4 * halves :]
    wide, first, second = cos_ref[...], -first_ref[...], -second_ref[...]
    column = 0
    for half in range(halves):
        dq_ref, own_ref, near_ref, far_ref = refs[4 * half : 4 * half + 4]
        width = dq_ref.shape[1]
        for part in range(width // 128):
            span = slice(part * 128, part * 128 + 128)
            at = column + part * 128
            out_ref[:, at : at + 128] = turn(dq_ref[:, span] * SCALE, wide, first, second).astype(
                BF
            )
            dk = own_ref[0, :, span] + near_ref[0, :, span].astype(F32)
            dk = (dk + far_ref[0, :, span].astype(F32)) * SCALE
            out_ref[:, D + at : D + at + 128] = turn(dk, wide, first, second).astype(BF)
            dv = own_ref[1, :, span] + near_ref[1, :, span].astype(F32)
            dv = dv + far_ref[1, :, span].astype(F32)
            out_ref[:, 2 * D + at : 2 * D + at + 128] = dv.astype(BF)
        column += width


def unturn(parts, tables):
    rows = tables[0].shape[0]
    arrays = [value for part in parts for value in part]
    vmem = pl.BlockSpec(memory_space=pltpu.VMEM)
    return pl.pallas_call(
        functools.partial(unturn_kernel, len(parts)),
        out_shape=jax.ShapeDtypeStruct((rows, 3 * D), BF),
        in_specs=[vmem] * (len(arrays) + 3),
        out_specs=vmem,
        cost_estimate=cost(20 * rows * 3 * D, rows * D * 30),
        name="unturn",
    )(*arrays, *tables)


def piece_bits(order, index):
    picked = dict(zip(order, ((index >> 2) & 1, (index >> 1) & 1, index & 1)))
    return picked["y"], picked["x"], picked["z"]


def rows_kernel(orders, lefts, spots_ref, *refs):
    left_refs = refs[: 2 * lefts]
    right_refs = refs[2 * lefts : 4 * lefts]
    outs = refs[4 * lefts : -2]
    turned_ref, picked_ref = refs[-2:]
    y, core, x, z = spots_ref[0], spots_ref[1], spots_ref[2], spots_ref[3]
    rows = left_refs[0].shape[0]
    high = D // 16

    def turned(own_ref, other_ref, slot):
        turned_ref[slot, :, 0:rows] = jnp.transpose(own_ref[...])
        turned_ref[slot, :, rows : 2 * rows] = jnp.transpose(other_ref[...])

    def pick(slot, order, place):
        for index in range(8):
            dy, dx, dz = piece_bits(order, index)
            start = (y ^ dy) * (D // 2) + core * (D // 4) + ((x ^ dx) * 2 + (z ^ dz)) * high
            picked_ref[place, index * high : index * high + high, :] = turned_ref[
                slot, pl.ds(pl.multiple_of(start, 16), high), :
            ]

    def multiply(place, own_ref, other_ref, source, block, keep_ref, send_ref):
        columns = pl.ds(pl.multiple_of(source * D, D), D)
        product = jnp.dot(
            picked_ref[place, :, 0:rows], own_ref[:, columns], preferred_element_type=F32
        )
        product += jnp.dot(
            picked_ref[place, :, rows : 2 * rows],
            other_ref[:, columns],
            preferred_element_type=F32,
        )
        span = pl.ds(pl.multiple_of(block * high, 16), high)
        for index in range(4):
            keep_ref[index, span, :] = product[index * high : index * high + high, :]
            send_ref[index, span, :] = product[
                (4 + index) * high : (4 + index) * high + high, :
            ].astype(BF)

    turned(left_refs[0], left_refs[1], 0)
    pick(0, orders[0], 0)
    blocks = right_refs[0].shape[1] // D
    split = 2 if len(orders) == 2 else blocks

    def body(block, carry):
        multiply(0, right_refs[0], right_refs[1], block, block, *outs[:2])
        return carry

    lax.fori_loop(0, split, body, 0)
    if len(orders) == 2:
        pick(0, orders[1], 1)
        multiply(1, right_refs[0], right_refs[1], 2, 0, *outs[2:])
    if lefts == 2:
        turned(left_refs[2], left_refs[3], 1)
        pick(1, orders[-1], 2)
        multiply(2, right_refs[2], right_refs[3], 0, 1 if len(orders) == 2 else blocks, *outs[-2:])


def rows_unit(spots, orders, lefts, rights):
    rows = lefts[0][0].shape[0]
    arrays = [value for pair in (*lefts, *rights) for value in pair]
    high = D // 4 // len(orders)
    vmem = pl.BlockSpec(memory_space=pltpu.VMEM)
    return pl.pallas_call(
        functools.partial(rows_kernel, orders, len(lefts)),
        out_shape=[
            jax.ShapeDtypeStruct((4, high, D), kind) for _ in orders for kind in (F32, BF)
        ],
        in_specs=[pl.BlockSpec(memory_space=pltpu.SMEM)] + [vmem] * len(arrays),
        out_specs=[vmem] * (2 * len(orders)),
        scratch_shapes=[
            pltpu.VMEM((len(lefts), D, 2 * rows), BF),
            pltpu.VMEM((3 if len(lefts) == 2 else 1, D // 2, 2 * rows), BF),
        ],
        cost_estimate=cost(4 * rows * (D // 2) * 4 * D, rows * D * 20 + 3 * D * D),
        name="rows_unit",
    )(spots, *arrays)


def forward_kernel(order, spots_ref, n0, n1, u0, u1, a0, a1, d0, d1, keep_ref, send_ref, *scratch):
    turned_ref, picked_ref, tall_ref = scratch
    y, core, x, z = spots_ref[0], spots_ref[1], spots_ref[2], spots_ref[3]
    rows = n0.shape[0]
    high = D // 16
    tall = D // 4
    turned_ref[:, 0:rows] = jnp.transpose(n0[...])
    turned_ref[:, rows : 2 * rows] = jnp.transpose(n1[...])
    for index in range(8):
        dy, dx, dz = piece_bits(order, index)
        start = (y ^ dy) * (D // 2) + core * (D // 4) + ((x ^ dx) * 2 + (z ^ dz)) * high
        picked_ref[index * high : index * high + high, :] = turned_ref[
            pl.ds(pl.multiple_of(start, 16), high), :
        ]

    def body(block, carry):
        columns = pl.ds(pl.multiple_of(block * D, D), D)
        product = jnp.dot(picked_ref[:, 0:rows], u0[:, columns], preferred_element_type=F32)
        product += jnp.dot(
            picked_ref[:, rows : 2 * rows], u1[:, columns], preferred_element_type=F32
        )
        span = pl.ds(pl.multiple_of(block * high, 16), high)
        for index in range(4):
            keep_ref[index, span, :] = product[index * high : index * high + high, :]
            send_ref[index, span, :] = product[
                (4 + index) * high : (4 + index) * high + high, :
            ].astype(BF)
        return carry

    lax.fori_loop(0, 4, body, 0)
    for dy in range(2):
        columns = pl.ds(pl.multiple_of(((y ^ dy) * 2 + core) * D, D), D)
        tall_ref[dy, :, 0:rows] = jnp.transpose(a0[:, columns])
        tall_ref[dy, :, rows : 2 * rows] = jnp.transpose(a1[:, columns])
        for dx in range(2):
            for dz in range(2):
                start = pl.multiple_of(((x ^ dx) * 2 + (z ^ dz)) * tall, 16)
                left = tall_ref[dy, pl.ds(start, tall), :]
                product = jnp.dot(left[:, 0:rows], d0[...], preferred_element_type=F32)
                product += jnp.dot(left[:, rows : 2 * rows], d1[...], preferred_element_type=F32)
                index = [k for k in range(8) if piece_bits(order, k) == (dy, dx, dz)][0]
                if index < 4:
                    keep_ref[index, tall : 2 * tall, :] = product
                else:
                    send_ref[index - 4, tall : 2 * tall, :] = product.astype(BF)


def forward_unit(spots, order, normed, grad_up, activated, grad_down):
    rows = normed[0].shape[0]
    vmem = pl.BlockSpec(memory_space=pltpu.VMEM)
    return pl.pallas_call(
        functools.partial(forward_kernel, order),
        out_shape=[
            jax.ShapeDtypeStruct((4, D // 2, D), F32),
            jax.ShapeDtypeStruct((4, D // 2, D), BF),
        ],
        in_specs=[pl.BlockSpec(memory_space=pltpu.SMEM)] + [vmem] * 8,
        out_specs=[vmem] * 2,
        scratch_shapes=[
            pltpu.VMEM((D, 2 * rows), BF),
            pltpu.VMEM((D // 2, 2 * rows), BF),
            pltpu.VMEM((2, D, 2 * rows), BF),
        ],
        cost_estimate=cost(8 * rows * (D // 2) * 4 * D, rows * D * 40 + 6 * D * D),
        name="forward_unit",
    )(spots, *normed, *grad_up, *activated, *grad_down)


AXES = {"y": ("fsdp", 2), "x": ("dp", 1), "z": ("dp", 2)}


class Sum:
    def __init__(self, line, unit, order):
        self.line, self.order, self.stage = line, order, 0
        self.keep, send = unit
        self.moving = swap(send, *AXES[order[0]])
        self.far = [1 << k for k in range(2, 20) if (1 << k) < lax.axis_size("dp")]
        self.rest = [name for name in order if name != "y"]

    def step(self):
        got, keep = self.line.enter(self.moving, self.keep)
        line, stage = self.line, self.stage
        self.stage += 1
        if stage < 3:
            half = keep.shape[0] // 2
            if stage < 2:
                self.keep = keep[:half] + got[:half].astype(F32)
                send = (keep[half:] + got[half:].astype(F32)).astype(BF)
                line.leave(self.keep, send)
                self.moving = swap(send, *AXES[self.order[stage + 1]])
                return
            self.keep = (keep + got.astype(F32)).astype(BF)
        elif stage < 3 + len(self.far):
            self.keep = (keep.astype(F32) + got.astype(F32)).astype(BF)
        elif stage == 3 + len(self.far):
            self.keep = jnp.concatenate([keep, got], axis=0)
            line.leave(self.keep)
            self.moving = swap(self.keep, *AXES[self.rest[0]])
            return
        else:
            self.result = (keep, got)
            return
        line.leave(self.keep)
        if stage - 2 < len(self.far):
            self.moving = swap(self.keep, "dp", self.far[stage - 2])
        else:
            self.moving = swap(self.keep, *AXES[self.rest[1]])

    def finish(self):
        while self.stage < 5 + len(self.far):
            self.step()
        return self.result


def emit_kernel(orders, places, count, spots_ref, *refs):
    outs = refs[-count:]
    x, z = spots_ref[2], spots_ref[3]
    high = D // 16
    for number, order in enumerate(orders):
        rest = [name for name in order if name != "y"]
        for outer in range(2):
            piece = refs[2 * number + outer]
            for inner in range(2):
                picked = dict(zip(rest, (outer, inner)))
                which = (x ^ picked["x"]) * 2 + (z ^ picked["z"])
                at = 0
                for slot, block in places[number]:
                    tall = high if block is not None else 4 * high
                    start = pl.multiple_of(which * tall, 16)
                    first = 0 if block is None else block * D
                    outs[slot][0, pl.ds(start, tall), first : first + D] = piece[
                        inner, at : at + tall, :
                    ].astype(F32)
                    at += tall


def emit(spots, sums, orders, places, shapes, layer, before):
    out_shape = [jax.ShapeDtypeStruct((LAYERS,) + shape, F32) for shape in shapes]
    before = list(before) if before is not None else []
    pieces = [piece for pair in sums for piece in pair]
    return pl.pallas_call(
        functools.partial(emit_kernel, orders, places, len(shapes)),
        out_shape=out_shape,
        grid_spec=pltpu.PrefetchScalarGridSpec(
            num_scalar_prefetch=1,
            grid=(1,),
            in_specs=[pl.BlockSpec(memory_space=pltpu.VMEM)] * len(pieces)
            + [pl.BlockSpec(memory_space=pl.ANY)] * len(before),
            out_specs=[
                pl.BlockSpec((1,) + shape, lambda i, spots: (layer, 0, 0)) for shape in shapes
            ],
        ),
        input_output_aliases={1 + len(pieces) + i: i for i in range(len(before))},
        cost_estimate=cost(0, D * D * 6),
        name="emit",
    )(spots, *pieces, *before)


class Line:
    def __init__(self):
        self.last = ()

    def enter(self, *values):
        out = lax.optimization_barrier(tuple(values) + tuple(self.last))
        return out[: len(values)]

    def leave(self, *values):
        self.last = tuple(values)

    def sync(self, *values):
        out = self.enter(*values)
        self.last = tuple(out)
        return out


def after(value, *others):
    return lax.optimization_barrier((value,) + others)[0]


NAMES = (
    "input_bias",
    "output_bias",
    "first_gain",
    "first_shift",
    "up_bias",
    "down_bias",
    "second_gain",
    "second_shift",
)
WIDTHS = (3 * D, D, D, D, 4 * D, D, D, D)


def feed_forward(hidden, context, weights, small):
    _, output_weight, up_weight, down_weight = weights
    attn_out = jnp.dot(context, output_weight, preferred_element_type=F32) + small["output_bias"]
    first_in = hidden + attn_out
    normed = layer_norm(first_in, small["first_gain"], small["first_shift"])
    normed_low = normed.astype(BF)
    up_value = jnp.dot(normed_low, up_weight, preferred_element_type=F32) + small["up_bias"]
    activated = (up_value * normal_part(up_value)).astype(BF)
    down_value = (
        jnp.dot(activated, down_weight, preferred_element_type=F32) + small["down_bias"]
    )
    second_in = normed + down_value
    output = layer_norm(second_in, small["second_gain"], small["second_shift"])
    return output, first_in, normed_low, up_value, activated, second_in


def feed_backward(grad_output, weights, small, first_in, up_value, second_in):
    _, output_weight, up_weight, down_weight = weights
    pull_second = jax.vjp(layer_norm, second_in, small["second_gain"], small["second_shift"])[1]
    grad_second, grad_second_gain, grad_second_shift = pull_second(grad_output)
    grad_down = grad_second.astype(BF)
    grad_down_bias = jnp.sum(grad_down, axis=0, dtype=F32)
    grad_activated = contract_cols(grad_down, down_weight)
    grad_up = (grad_activated * gelu_slope(up_value)).astype(BF)
    grad_up_bias = jnp.sum(grad_up, axis=0, dtype=F32)
    grad_normed = grad_second + contract_cols(grad_up, up_weight)
    pull_first = jax.vjp(layer_norm, first_in, small["first_gain"], small["first_shift"])[1]
    grad_first, grad_first_gain, grad_first_shift = pull_first(grad_normed)
    grad_attn = grad_first.astype(BF)
    grad_output_bias = jnp.sum(grad_attn, axis=0, dtype=F32)
    grad_context = contract_cols(grad_attn, output_weight).astype(BF)
    little = (
        grad_output_bias,
        grad_first_gain,
        grad_first_shift,
        grad_up_bias,
        grad_down_bias,
        grad_second_gain,
        grad_second_shift,
    )
    return grad_down, grad_up, grad_attn, grad_context, grad_first, little


class LittleSum:
    def __init__(self, line, packed, place):
        self.line, self.place = line, place
        self.todo = [("fsdp", 1, 1), ("fsdp", 2, 0)]
        bit = 1
        while bit < lax.axis_size("dp"):
            self.todo.append(("dp", bit, None))
            bit *= 2
        self.keep = packed.reshape(2, 2, -1)
        self.start()

    def start(self):
        axis, bit, dim = self.todo[0]
        send = self.keep
        if dim is not None:
            mine = (self.place // bit) & 1
            send = lax.dynamic_slice_in_dim(self.keep, 1 - mine, 1, dim)
            self.keep = lax.dynamic_slice_in_dim(self.keep, mine, 1, dim)
        self.moving = swap(send, axis, bit)

    def step(self):
        got, keep = self.line.enter(self.moving, self.keep)
        self.keep = keep + got
        self.line.leave(self.keep)
        self.todo.pop(0)
        if self.todo:
            self.start()

    def finish(self):
        while self.todo:
            self.step()
        return spread(self.keep.reshape(1, -1), WIDTHS)


FORWARD_ORDER = ("xzy", "xzy")
JOINT_ORDER = (("yxz", "xzy"), ("zyx",))


def on_device(
    tokens,
    cotangent,
    lengths,
    input_weight,
    input_bias,
    output_weight,
    output_bias,
    first_gain,
    first_shift,
    up_weight,
    up_bias,
    down_weight,
    down_bias,
    second_gain,
    second_shift,
):
    place = lax.axis_index("fsdp")
    group = lax.axis_index("dp")
    core = place & 1
    x_bit, z_bit = group & 1, (group >> 1) & 1
    spots = jnp.stack([place >> 1, core, x_bit, z_bit]).astype(jnp.int32)
    row_count = tokens.shape[0]
    places = place * row_count + jnp.arange(row_count, dtype=jnp.int32)
    length = lengths[0]
    info = jnp.stack([place, length]).astype(jnp.int32)
    row_valid = (places < length).astype(F32)

    swap_core = lambda value: swap(value, "fsdp", 1)
    swap_y = lambda value: swap(value, "fsdp", 2)
    swap_x = lambda value: swap(value, "dp", 1)
    swap_z = lambda value: swap(value, "dp", 2)

    rows_of = D // 4
    quarter = rows_of // 4
    start = (x_bit * 2 + z_bit) * quarter
    quarters = [
        x_bit * 2 + z_bit,
        x_bit * 2 + (1 - z_bit),
        (1 - x_bit) * 2 + z_bit,
        (1 - x_bit) * 2 + (1 - z_bit),
    ]
    spread_spots = jnp.stack(
        [place * rows_of, (place ^ 1) * rows_of]
        + [(place ^ 2) * rows_of + q * quarter for q in quarters]
        + [(place ^ 3) * rows_of + q * quarter for q in quarters]
    ).astype(jnp.int32)
    direct_spots = jnp.stack([(place ^ k) * rows_of for k in range(4)]).astype(jnp.int32)
    rest_spec = (("rows", D), ("rows", 4 * D), ("split", 4 * D))

    def wide(i):
        split = [down_weight[i, k * 192 : k * 192 + 192] for k in range(4)]
        return jnp.concatenate([output_weight[i], up_weight[i]] + split, axis=1)

    line = Line()

    input_one, input_two = input_weight[0], input_weight[1]
    over_y = swap_y(input_one)
    packed = jnp.concatenate(
        (
            input_bias,
            output_bias,
            first_gain,
            first_shift,
            up_bias,
            down_bias,
            second_gain,
            second_shift,
        ),
        axis=1,
    )
    packed_y, packed_c, input_c = swap_y(packed), swap_core(packed), swap_core(input_one)
    tables = rotary_tables(places.astype(F32))
    rests = (wide(0), wide(1))
    mine = [lax.dynamic_slice(r, (start, 0), (quarter, r.shape[1])) for r in rests]
    line.leave(*mine)
    over_y, packed_y, packed_c, input_c = line.sync(over_y, packed_y, packed_c, input_c)
    spread_y = swap_y(after(mine[0], over_y))
    rest_c = swap_core(after(rests[0], over_y))
    packed_yc, input_yc = swap_core(packed_y), swap_core(over_y)
    fields = unpack(info, [packed, packed_c, packed_y, packed_yc], WIDTHS)
    smalls = [
        dict(zip(NAMES, fields[i * len(NAMES) : (i + 1) * len(NAMES)])) for i in range(LAYERS)
    ]
    pieces = [input_one, input_c, over_y, input_yc]
    line.leave(*fields)
    hidden, rounded = tokens.astype(F32), tokens
    kept, weights = [], []
    for i in range(LAYERS):
        more = i + 1 < LAYERS
        small = smalls[i]
        pieces = line.enter(*pieces)
        queries, *kvs, whole = project(
            rounded, pieces, direct_spots, small["input_bias"], tables
        )
        line.leave(queries, *kvs, whole)
        kv_y, kv_c = [swap_y(kv) for kv in kvs], [swap_core(kv) for kv in kvs]
        spread_y, rest_c = line.sync(spread_y, rest_c)
        spread_z, spread_x = swap_z(spread_y), swap_x(spread_y)
        if i > 0:
            saved = [kept[0][8], kept[0][6], kept[0][4], rounded]
            shared = line.sync(*[swap_core(v) for v in saved[:2]])
            shared += line.sync(*[swap_core(v) for v in saved[2:]])
            act1, normed1, context1, rounded2 = list(zip(saved, shared))
        spread_z, spread_x = line.sync(spread_z, spread_x)
        spread_xz = swap_x(spread_z)
        crossed = [swap_core(v) for v in (spread_y, spread_z, spread_x)]
        chunks, logs = [], []
        context, rest = None, None
        for part in range(PARTS):
            if part == 1:
                crossed = list(line.sync(*crossed))
            got_y, got_c = line.sync(kv_y[part], kv_c[part])
            (got_yc,) = line.sync(swap_core(got_y))
            if more and part == PARTS - 1:
                over_y, input_c = swap_y(after(input_two, got_yc)), swap_core(after(input_two, got_yc))
            chunks.append([kvs[part], got_c, got_y, got_yc])
            (query_in,) = line.enter(queries)
            context, log = attend(info, query_in, chunks[-1], part, context)
            line.leave(context, log)
            logs.append(log)
            if part == PARTS - 2:
                (spread_xz,) = line.sync(spread_xz)
                crossed.append(swap_core(spread_xz))
        crossed[3:] = line.sync(*crossed[3:])
        if more:
            over_y, input_c = line.sync(over_y, input_c)
            next_y = swap_y(after(mine[1], over_y))
            input_yc = swap_core(over_y)
        pieces = [rests[i], rest_c, spread_y, spread_z, spread_x, spread_xz, *crossed]
        rest = assemble(pieces, spread_spots, rest_spec)
        weights.append((whole, *rest))
        line.leave(*rest)
        if more:
            rest_c = swap_core(after(rests[1], rest[0]))
        (context_in,) = line.enter(context)
        output, first_in, normed, up_value, activated, second_in = feed_forward(
            hidden, context_in, weights[i], small
        )
        kept.append(
            (rounded, queries, chunks, logs, context, first_in, normed, up_value, activated, second_in)
        )
        hidden, rounded = output, output.astype(BF)
        line.leave(hidden, rounded)
        if more:
            spread_y = next_y
            pieces = [input_two, input_c, over_y, input_yc]
    result = rounded

    def both_cores(*values):
        values = line.enter(*values)
        return [(value, swap_core(value)) for value in values]

    def feed_back(grad_output, i):
        (grad_output,) = line.enter(grad_output)
        _, _, _, _, _, first_in, _, up_value, _, second_in = kept[i]
        out = feed_backward(grad_output, weights[i], smalls[i], first_in, up_value, second_in)
        line.leave(*out[:5])
        return out

    def attention_back(i, grad_context, part):
        queries, chunks, logs = kept[i][1:4]
        (grad_context,) = line.enter(grad_context)
        dq, own, give = pull(info, queries, grad_context, logs[part], chunks[part], part)
        line.leave(dq, own, give)
        return dq, own, swap_core(give)

    def far_back(pulled):
        dq, own, near = pulled
        own, near = line.enter(own, near)
        far = (own[2:] + near[2:].astype(F32)).astype(BF)
        line.leave(far)
        return dq, own, near, swap_y(far)

    def arrive(far):
        dq, own, near, moving = far
        (moving,) = line.sync(moving)
        return dq, own, near, moving

    def forward_sum(i, normed, grad_up, activated, grad_down):
        pairs = (normed, grad_up, activated, grad_down)
        got = line.enter(*[pair[1] for pair in pairs])
        unit = forward_unit(
            spots, FORWARD_ORDER[i], *[(pair[0], g) for pair, g in zip(pairs, got)]
        )
        line.leave(*unit)
        return Sum(line, unit, FORWARD_ORDER[i])

    def joint_sum(i, rounded, grad_joint, context, grad_attn):
        got = line.enter(rounded[1], grad_joint[1], context[1], grad_attn[1])
        pairs = [(p[0], g) for p, g in zip((rounded, grad_joint, context, grad_attn), got)]
        unit = rows_unit(spots, JOINT_ORDER[i], [pairs[0], pairs[2]], [pairs[1], pairs[3]])
        line.leave(*unit)
        return [
            Sum(line, unit[2 * k : 2 * k + 2], order) for k, order in enumerate(JOINT_ORDER[i])
        ]

    def joint_back(i, parts, grad_first):
        flat = line.enter(*[v for part in parts for v in part])
        parts = [flat[4 * k : 4 * k + 4] for k in range(len(parts))]
        grad_joint = unturn(parts, tables)
        line.leave(grad_joint)
        grad_hidden = grad_first + contract_cols(grad_joint, weights[i][0])
        return grad_joint, jnp.sum(grad_joint, axis=0, dtype=F32), grad_hidden

    grad_hidden = cotangent.astype(F32) * row_valid[:, None]
    act2, normed2 = both_cores(kept[1][8], kept[1][6])
    dd2, du2, da2, dc2, grad_first2, little2 = feed_back(grad_hidden, 1)

    def retire(*pairs):
        got = line.sync(*[pair[1] for pair in pairs])
        return [(pair[0], value) for pair, value in zip(pairs, got)]

    act2, normed2 = retire(act2, normed2)
    dd2, du2 = both_cores(dd2, du2)
    p0 = attention_back(1, dc2, 0)
    dd2, du2 = retire(dd2, du2)
    context2, da2 = both_cores(kept[1][4], da2)
    p1 = attention_back(1, dc2, 1)
    context2, da2 = retire(context2, da2)
    p0 = far_back(p0)
    p2 = attention_back(1, dc2, 2)
    p0 = arrive(p0)
    p1 = far_back(p1)
    f2 = forward_sum(1, normed2, du2, act2, dd2)
    p1 = arrive(p1)
    p2 = far_back(p2)
    p2 = arrive(p2)
    joint2, bias2, grad_hidden = joint_back(1, (p0, p1, p2), grad_first2)
    (joint2,) = both_cores(joint2)
    dd1, du1, da1, dc1, grad_first1, little1 = feed_back(grad_hidden, 0)
    (joint2,) = retire(joint2)
    f2.step()
    dd1, du1 = both_cores(dd1, du1)
    (j2,) = joint_sum(1, rounded2, joint2, context2, da2)
    dd1, du1 = retire(dd1, du1)
    f1 = forward_sum(0, normed1, du1, act1, dd1)
    f2.step()
    rounded1, da1 = both_cores(kept[0][0], da1)
    p0 = attention_back(0, dc1, 0)
    rounded1, da1 = retire(rounded1, da1)
    j2.step()
    p1 = attention_back(0, dc1, 1)
    p0 = far_back(p0)
    f2.step()
    j2.step()
    p2 = attention_back(0, dc1, 2)
    p0 = arrive(p0)
    p1 = far_back(p1)
    f1.step()
    f2.step()
    p1 = arrive(p1)
    p2 = far_back(p2)
    j2.step()
    shape_forward = [(D // 4, 4 * D), (D, D)]
    shape_joint = [(D // 4, 3 * D), (D // 4, D)]
    place_forward = ([(0, 0), (0, 1), (0, 2), (0, 3), (1, None)],)

    def write(chains, orders, places, shapes, layer, before):
        sums = [chain.finish() for chain in chains]
        out = emit(spots, sums, orders, places, shapes, layer, before)
        line.leave(*out)
        return out

    f2.step()
    p2 = arrive(p2)
    joint1, bias1, grad_hidden = joint_back(0, (p0, p1, p2), grad_first1)
    (joint1,) = both_cores(joint1)
    packed = pack(
        [part.reshape(1, -1) for layer in ((bias1, *little1), (bias2, *little2)) for part in layer]
    )
    line.leave(packed)
    little = LittleSum(line, packed, place)
    f1.step()
    (joint1,) = retire(joint1)
    j1 = joint_sum(0, rounded1, joint1, context1, da1)
    little.step()
    f1.step()
    j2.step()
    out_forward = write([f2], (FORWARD_ORDER[1],), place_forward, shape_forward, 1, None)
    little.step()
    j1[0].step()
    j1[1].step()
    f1.step()
    j2.step()
    little.step()
    j1[0].step()
    j1[1].step()
    out_joint = write(
        [j2],
        JOINT_ORDER[1],
        ([(0, 0), (0, 1), (0, 2), (1, 0)],),
        shape_joint,
        1,
        None,
    )
    j1[0].step()
    j1[1].step()
    little.step()
    f1.step()
    j1[0].step()
    j1[1].step()
    flat = little.finish()
    j1[0].step()
    j1[1].step()
    out_forward = write([f1], (FORWARD_ORDER[0],), place_forward, shape_forward, 0, out_forward)
    out_joint = write(
        j1,
        JOINT_ORDER[0],
        ([(0, 0), (0, 1)], [(0, 2), (1, 0)]),
        shape_joint,
        0,
        out_joint,
    )

    small_grads = dict(zip(NAMES, flat))
    return (
        result,
        grad_hidden,
        out_joint[0],
        small_grads["input_bias"],
        out_joint[1],
        small_grads["output_bias"],
        small_grads["first_gain"],
        small_grads["first_shift"],
        out_forward[0],
        small_grads["up_bias"],
        out_forward[1],
        small_grads["down_bias"],
        small_grads["second_gain"],
        small_grads["second_shift"],
    )


def solution(mesh):
    rows = P(("dp", "fsdp"), None)
    matrix = P(None, "fsdp", None)
    vector = P(None, "fsdp")
    parameters = (
        matrix,
        vector,
        matrix,
        vector,
        vector,
        vector,
        matrix,
        vector,
        matrix,
        vector,
        vector,
        vector,
    )
    return jax.shard_map(
        on_device,
        mesh=mesh,
        in_specs=(rows, rows, P("dp"), *parameters),
        out_specs=(rows, rows, *parameters),
        check_vma=False,
    )
```

```python
import functools

import jax
import jax.numpy as jnp
from jax import lax
from jax.experimental import pallas as pl
from jax.experimental.pallas import tpu as pltpu
from jax.sharding import PartitionSpec as P

D = 768
HEADS = 12
HEAD = 64
PAIRS = HEADS // 2
LAYERS = 2
RIDER = -1
PARTS = 3
GROUP = PAIRS // PARTS
WIDE = GROUP * 128
LOG2E = 1.4426950408889634
SCALE = HEAD ** (-0.5)
NEG = -1e30
BF = jnp.bfloat16
F32 = jnp.float32

norm_eps = 1e-12


def swap(value, axis, bit):
    count = lax.axis_size(axis)
    return lax.ppermute(value, axis, [(i, i ^ bit) for i in range(count)])


def layer_norm(matrix, norm_gain, norm_shift):
    row_mean = jnp.mean(matrix, axis=-1, keepdims=True)
    centred = matrix - row_mean
    spread = jnp.mean(centred * centred, axis=-1, keepdims=True)
    return centred * lax.rsqrt(spread + norm_eps) * norm_gain + norm_shift


def normal_part(value):
    return 0.5 + 0.5 * lax.erf(value * 0.7071067811865476)


def gelu_slope(value, part):
    return part + value * jnp.exp(-0.5 * value * value) * 0.3989422804014327


def contract_rows(left_side, right_side):
    return lax.dot_general(
        left_side, right_side, (((0,), (0,)), ((), ())), preferred_element_type=F32
    )


def contract_cols(left_side, right_side):
    return lax.dot_general(
        left_side, right_side, (((1,), (1,)), ((), ())), preferred_element_type=F32
    )


def cost(flops, bytes_accessed, transcendentals=0):
    return pl.CostEstimate(
        flops=int(flops), bytes_accessed=int(bytes_accessed), transcendentals=int(transcendentals)
    )


def rotary_tables(places):
    frequency = 10000.0 ** (-2.0 * jnp.arange(HEAD // 2, dtype=F32) / HEAD)
    angles = places[:, None] * frequency[None, :]
    cosine, sine = jnp.cos(angles), jnp.sin(angles)
    nothing = jnp.zeros_like(sine)
    wide = jnp.concatenate([cosine] * 4, axis=1)
    first = jnp.concatenate([-sine, nothing] * 2, axis=1)
    second = jnp.concatenate([nothing, sine] * 2, axis=1)
    return wide, first, second


def turn(block, wide, first, second):
    return (
        block * wide
        + pltpu.roll(block, 96, 1) * first
        + pltpu.roll(block, 32, 1) * second
    )


def assemble_kernel(spec, count, pos_ref, *refs):
    pieces = refs[:count]
    outs = refs[count : count + len(spec)]
    held, in_sem, out_sem = refs[count + len(spec) :]
    copies = []
    for index, piece in enumerate(pieces):
        rows = piece.shape[0]
        start = pl.multiple_of(pos_ref[index], 16)
        copies.append(
            pltpu.make_async_copy(piece, held.at[pl.ds(start, rows), :], in_sem.at[index])
        )
    for copy in copies:
        copy.start()
    for copy in copies:
        copy.wait()
    copies = []
    column = 0
    for slot, (kind, width) in enumerate(spec):
        if kind == "rows":
            copies.append((held.at[:, pl.ds(column, width)], outs[slot]))
        else:
            shard = held.shape[0] // 4
            for source in range(4):
                for part in range(width // D):
                    copies.append(
                        (
                            held.at[pl.ds(source * shard, shard), pl.ds(column + part * D, D)],
                            outs[slot].at[pl.ds(source * 4 * shard + part * shard, shard), :],
                        )
                    )
        column += width
    copies = [
        pltpu.make_async_copy(src, dst, out_sem.at[index])
        for index, (src, dst) in enumerate(copies)
    ]
    for copy in copies:
        copy.start()
    for copy in copies:
        copy.wait()


def assemble(pieces, positions, spec):
    width = pieces[0].shape[1]
    out_shape = []
    outputs = 0
    for kind, columns in spec:
        if kind == "rows":
            out_shape.append(jax.ShapeDtypeStruct((D, columns), BF))
            outputs += 1
        else:
            out_shape.append(jax.ShapeDtypeStruct((columns, D), BF))
            outputs += 4 * (columns // D)
    return pl.pallas_call(
        functools.partial(assemble_kernel, spec, len(pieces)),
        out_shape=out_shape,
        in_specs=[pl.BlockSpec(memory_space=pltpu.SMEM)]
        + [pl.BlockSpec(memory_space=pl.ANY)] * len(pieces),
        out_specs=[pl.BlockSpec(memory_space=pl.ANY)] * len(spec),
        scratch_shapes=[
            pltpu.VMEM((D, width), BF),
            pltpu.SemaphoreType.DMA((len(pieces),)),
            pltpu.SemaphoreType.DMA((outputs,)),
        ],
        cost_estimate=cost(0, 4 * D * width),
        name="assemble",
    )(positions, *pieces)


def pack_kernel(*refs):
    *parts, out_ref, flat_ref = refs
    offset = 0
    flat_ref[...] = jnp.zeros_like(flat_ref)
    for part in parts:
        width = part.shape[0] // 4
        values = part[...].reshape(1, 4 * width)
        for owner in range(4):
            flat_ref[owner : owner + 1, offset : offset + width] = values[
                :, owner * width : owner * width + width
            ]
        offset += width
    for owner in range(4):
        for row in range(8):
            out_ref[4 * owner + row // 2, row % 2 : row % 2 + 1, :] = flat_ref[
                owner : owner + 1, row * D : row * D + D
            ]


def spread_kernel(count, rows_ref, *refs):
    *outs, flat_ref = refs
    for row in range(8):
        flat_ref[:, row * D : row * D + D] = rows_ref[row // 2, row % 2 : row % 2 + 1, :]
    offset = 0
    for layer in range(LAYERS):
        for slot in range(count):
            width = outs[slot].shape[1]
            outs[slot][layer : layer + 1, :] = flat_ref[:, offset : offset + width]
            offset += width


def pack(parts):
    vmem = pl.BlockSpec(memory_space=pltpu.VMEM)
    return pl.pallas_call(
        pack_kernel,
        out_shape=jax.ShapeDtypeStruct((16, 2, D), F32),
        in_specs=[vmem] * len(parts),
        out_specs=vmem,
        scratch_shapes=[pltpu.VMEM((4, 8 * D), F32)],
        cost_estimate=cost(0, 200000),
        name="pack",
    )(*parts)


def spread(rows, widths):
    vmem = pl.BlockSpec(memory_space=pltpu.VMEM)
    return pl.pallas_call(
        functools.partial(spread_kernel, len(widths)),
        out_shape=[jax.ShapeDtypeStruct((LAYERS, width // 4), F32) for width in widths],
        in_specs=[vmem],
        out_specs=[vmem] * len(widths),
        scratch_shapes=[pltpu.VMEM((1, 8 * D), F32)],
        cost_estimate=cost(0, 50000),
        name="spread",
    )(rows)


def project_kernel(count, pos_ref, h_ref, b_ref, cos_ref, first_ref, second_ref, *refs):
    pieces = refs[:count]
    q_ref, *kv_refs, whole_ref, held, in_sem, out_sem = refs[count:]
    copies = []
    for part in range(3):
        for index, piece in enumerate(pieces):
            rows = piece.shape[0]
            start = pl.multiple_of(pos_ref[index], 16)
            copies.append(
                pltpu.make_async_copy(
                    piece.at[:, pl.ds(part * D, D)],
                    held.at[part, pl.ds(start, rows), :],
                    in_sem.at[part * count + index],
                )
            )
    for copy in copies:
        copy.start()
    outs = [
        pltpu.make_async_copy(
            held.at[part], whole_ref.at[:, pl.ds(part * D, D)], out_sem.at[part]
        )
        for part in range(3)
    ]
    for part in range(3):
        for copy in copies[part * count : part * count + count]:
            copy.wait()
        outs[part].start()
        joint = jnp.dot(h_ref[...], held[part], preferred_element_type=F32)
        joint = joint + b_ref[:, part * D : part * D + D]
        if part == 2:
            for index in range(PARTS):
                kv_refs[index][:, WIDE:] = joint[:, index * WIDE : index * WIDE + WIDE].astype(BF)
            continue
        for pair in range(PAIRS):
            span = slice(pair * 128, pair * 128 + 128)
            turned = turn(joint[:, span], cos_ref[...], first_ref[...], second_ref[...]).astype(BF)
            if part == 0:
                q_ref[:, span] = turned
            else:
                at = pair % GROUP * 128
                kv_refs[pair // GROUP][:, at : at + 128] = turned
    for copy in outs:
        copy.wait()


def project(rounded, pieces, positions, bias, tables):
    rows = rounded.shape[0]
    count = len(pieces)
    return pl.pallas_call(
        functools.partial(project_kernel, count),
        out_shape=[
            jax.ShapeDtypeStruct((rows, D), BF),
            *[jax.ShapeDtypeStruct((rows, 2 * WIDE), BF)] * PARTS,
            jax.ShapeDtypeStruct((D, 3 * D), BF),
        ],
        in_specs=[pl.BlockSpec(memory_space=pltpu.SMEM)]
        + [pl.BlockSpec(memory_space=pltpu.VMEM)] * 5
        + [pl.BlockSpec(memory_space=pl.ANY)] * count,
        out_specs=[pl.BlockSpec(memory_space=pltpu.VMEM)] * (1 + PARTS)
        + [pl.BlockSpec(memory_space=pl.ANY)],
        scratch_shapes=[
            pltpu.VMEM((3, D, D), BF),
            pltpu.SemaphoreType.DMA((3 * count,)),
            pltpu.SemaphoreType.DMA((3,)),
        ],
        cost_estimate=cost(2 * rows * D * 3 * D, 2 * (rows * 4 * D + 3 * D * D)),
        name="project",
    )(positions, rounded, bias, *tables, *pieces)


def unpack_kernel(widths, place_ref, *refs):
    pieces, outs, held = refs[:4], refs[4:-1], refs[-1]
    place = place_ref[0]
    for index in range(4):
        held[index] = pieces[index][...].astype(F32)
    for source in range(4):
        shard = held[source ^ place]
        offset = 0
        for slot, width in enumerate(widths):
            part = width // 4
            for layer in range(LAYERS):
                outs[layer * len(widths) + slot][:, source * part : source * part + part] = shard[
                    layer : layer + 1, offset : offset + part
                ]
            offset += part


def unpack(info, pieces, widths):
    vmem = pl.BlockSpec(memory_space=pltpu.VMEM)
    return pl.pallas_call(
        functools.partial(unpack_kernel, widths),
        out_shape=[jax.ShapeDtypeStruct((1, width), F32) for width in widths] * LAYERS,
        in_specs=[pl.BlockSpec(memory_space=pltpu.SMEM)] + [vmem] * 4,
        out_specs=[vmem] * (LAYERS * len(widths)),
        scratch_shapes=[pltpu.VMEM((4,) + pieces[0].shape, F32)],
        cost_estimate=cost(0, 100000),
        name="unpack",
    )(info, *pieces)


def attend_kernel(part, info_ref, q_ref, *refs):
    keys, values = refs[0:4], refs[4:8]
    out_ref, log_ref, column_ref, score_ref, prob_ref = refs[-5:]
    pair = pl.program_id(0)
    rows = q_ref.shape[0]
    place, length = info_ref[0], info_ref[1]
    lane = lax.broadcasted_iota(jnp.int32, (1, 128), 1)
    key_lane = lax.broadcasted_iota(jnp.int32, (1, rows), 1)
    bias = jnp.concatenate(
        [
            jnp.where((place ^ k) * rows + key_lane < length, 0.0, NEG).astype(F32)
            for k in range(4)
        ],
        axis=1,
    )
    factor = SCALE * LOG2E
    block = 32
    query = q_ref[...]
    owns = [(lane >= head * HEAD) & (lane < head * HEAD + HEAD) for head in range(2)]
    for head in range(2):
        masked = jnp.where(owns[head], query, jnp.zeros_like(query))
        for k in range(4):
            score_ref[head, :, k * rows : (k + 1) * rows] = contract_cols(masked, keys[k][...])
    for head in range(2):
        for index in range(rows // block):
            span = slice(index * block, index * block + block)
            scores = score_ref[head, span, :] + bias
            peak = jnp.max(scores, axis=1, keepdims=True)
            powers = jnp.exp2((scores - peak) * factor)
            total = jnp.sum(powers, axis=1, keepdims=True)
            prob_ref[head, span, :] = (powers * (1.0 / total)).astype(BF)
            column_ref[span, :] = jnp.where(
                lane == 2 * pair + head, peak * factor + jnp.log2(total), column_ref[span, :]
            )
    outs = []
    for head in range(2):
        gathered = jnp.dot(prob_ref[head, :, 0:rows], values[0][...], preferred_element_type=F32)
        for k in range(1, 4):
            gathered += jnp.dot(
                prob_ref[head, :, k * rows : (k + 1) * rows],
                values[k][...],
                preferred_element_type=F32,
            )
        outs.append(gathered)
    out_ref[...] = jnp.where(owns[0], outs[0], outs[1]).astype(BF)

    @pl.when(pair == GROUP - 1)
    def _():
        log_ref[...] = jnp.transpose(column_ref[...])[0:8, :]


def attend(info, queries, chunks, part, before):
    rows = queries.shape[0]
    own = pl.BlockSpec((rows, 128), lambda p: (0, part * GROUP + p))
    before = [] if before is None else [before]
    return pl.pallas_call(
        functools.partial(attend_kernel, part),
        out_shape=[
            jax.ShapeDtypeStruct((rows, D), BF),
            jax.ShapeDtypeStruct((8, rows), F32),
        ],
        grid=(GROUP,),
        in_specs=[pl.BlockSpec(memory_space=pltpu.SMEM), own]
        + [pl.BlockSpec((rows, 128), lambda p: (0, p))] * 4
        + [pl.BlockSpec((rows, 128), lambda p: (0, GROUP + p))] * 4
        + [pl.BlockSpec(memory_space=pl.ANY)] * len(before),
        out_specs=[own, pl.BlockSpec((8, rows), lambda p: (0, 0))],
        scratch_shapes=[
            pltpu.VMEM((rows, 128), F32),
            pltpu.VMEM((2, rows, 4 * rows), F32),
            pltpu.VMEM((2, rows, 4 * rows), BF),
        ],
        input_output_aliases={10: 0} if before else {},
        cost_estimate=cost(
            4 * rows * 4 * rows * WIDE, 2 * rows * 10 * WIDE, rows * 8 * rows * GROUP
        ),
        name="attend",
    )(info, queries, *chunks, *chunks, *before)


def pull_kernel(info_ref, q_ref, g_ref, log_ref, *refs):
    keys, values = refs[0:4], refs[4:8]
    dq_ref, own_ref, give_ref = refs[8:11]
    probs_ref, dp_ref, low_ref, ds_ref = refs[11:15]
    pair = pl.program_id(0)
    rows = q_ref.shape[0]
    block = 64
    place, length = info_ref[0], info_ref[1]
    lane = lax.broadcasted_iota(jnp.int32, (1, 128), 1)
    row = lax.broadcasted_iota(jnp.int32, (block, 1), 0)
    factor = SCALE * LOG2E
    query, grad = q_ref[...], g_ref[...]
    nothing = jnp.zeros_like(query)
    owns = [(lane >= head * HEAD) & (lane < head * HEAD + HEAD) for head in range(2)]
    queries = [jnp.where(own, query, nothing) for own in owns]
    grads = [jnp.where(own, grad, nothing) for own in owns]
    for head in range(2):
        for chunk in range(4):
            at = slice(chunk * rows, chunk * rows + rows)
            probs_ref[head, at, :] = contract_cols(keys[chunk][...], queries[head])
            dp_ref[head, at, :] = contract_cols(values[chunk][...], grads[head])
    for head in range(2):
        logged = log_ref[pl.ds(2 * pair + head, 1), :]
        inner = jnp.zeros((8, rows), F32)
        for index in range(4 * rows // block):
            span = slice(index * block, index * block + block)
            chunk, start = divmod(index * block, rows)
            base = (place ^ chunk) * rows + start
            bias = jnp.where(base + row < length, 0.0, NEG).astype(F32)
            probs = jnp.exp2(probs_ref[head, span, :] * factor + (bias - logged))
            probs_ref[head, span, :] = probs
            low_ref[head, span, :] = probs.astype(BF)
            inner += jnp.sum((probs * dp_ref[head, span, :]).reshape(block // 8, 8, rows), axis=0)
        inner = jnp.sum(inner, axis=0, keepdims=True)
        for index in range(4 * rows // block):
            span = slice(index * block, index * block + block)
            ds_ref[head, span, :] = (
                probs_ref[head, span, :] * (dp_ref[head, span, :] - inner)
            ).astype(BF)
    dq = jnp.zeros((128, rows), F32)
    for chunk in range(4):
        slot, out = 2 * (chunk // 2), (own_ref, give_ref)[chunk % 2]
        at = slice(chunk * rows, chunk * rows + rows)
        dk = jnp.dot(ds_ref[0, at, :], queries[0], preferred_element_type=F32)
        dk += jnp.dot(ds_ref[1, at, :], queries[1], preferred_element_type=F32)
        dv = jnp.dot(low_ref[0, at, :], grads[0], preferred_element_type=F32)
        dv += jnp.dot(low_ref[1, at, :], grads[1], preferred_element_type=F32)
        out[slot, :, :] = dk.astype(out.dtype)
        out[slot + 1, :, :] = dv.astype(out.dtype)
        key = keys[chunk][...]
        for head in range(2):
            dq += contract_rows(jnp.where(owns[head], key, nothing), ds_ref[head, at, :])
    dq_ref[...] = jnp.transpose(dq)


def pull(info, queries, grads, logs, chunks, part):
    rows = queries.shape[0]
    own = pl.BlockSpec((rows, 128), lambda p: (0, part * GROUP + p))
    stacked = pl.BlockSpec((4, rows, 128), lambda p: (0, 0, p))
    return pl.pallas_call(
        pull_kernel,
        out_shape=[
            jax.ShapeDtypeStruct((rows, WIDE), F32),
            jax.ShapeDtypeStruct((4, rows, WIDE), F32),
            jax.ShapeDtypeStruct((4, rows, WIDE), BF),
        ],
        grid=(GROUP,),
        in_specs=[
            pl.BlockSpec(memory_space=pltpu.SMEM),
            own,
            own,
            pl.BlockSpec((8, rows), lambda p: (0, 0)),
        ]
        + [pl.BlockSpec((rows, 128), lambda p: (0, p))] * 4
        + [pl.BlockSpec((rows, 128), lambda p: (0, GROUP + p))] * 4,
        out_specs=[pl.BlockSpec((rows, 128), lambda p: (0, p)), stacked, stacked],
        scratch_shapes=[
            pltpu.VMEM((2, 4 * rows, rows), F32),
            pltpu.VMEM((2, 4 * rows, rows), F32),
            pltpu.VMEM((2, 4 * rows, rows), BF),
            pltpu.VMEM((2, 4 * rows, rows), BF),
        ],
        cost_estimate=cost(
            10 * rows * 4 * rows * WIDE, 2 * rows * 24 * WIDE, rows * 4 * rows * 2 * GROUP
        ),
        name="pull",
    )(info, queries, grads, logs, *chunks, *chunks)


def unturn_kernel(halves, *refs):
    cos_ref, first_ref, second_ref, out_ref = refs[4 * halves :]
    wide, first, second = cos_ref[...], -first_ref[...], -second_ref[...]
    column = 0
    for half in range(halves):
        dq_ref, own_ref, near_ref, far_ref = refs[4 * half : 4 * half + 4]
        width = dq_ref.shape[1]
        for part in range(width // 128):
            span = slice(part * 128, part * 128 + 128)
            at = column + part * 128
            out_ref[:, at : at + 128] = turn(dq_ref[:, span] * SCALE, wide, first, second).astype(
                BF
            )
            dk = own_ref[0, :, span] + near_ref[0, :, span].astype(F32)
            dk = (dk + far_ref[0, :, span].astype(F32)) * SCALE
            out_ref[:, D + at : D + at + 128] = turn(dk, wide, first, second).astype(BF)
            dv = own_ref[1, :, span] + near_ref[1, :, span].astype(F32)
            dv = dv + far_ref[1, :, span].astype(F32)
            out_ref[:, 2 * D + at : 2 * D + at + 128] = dv.astype(BF)
        column += width


def unturn(parts, tables):
    rows = tables[0].shape[0]
    arrays = [value for part in parts for value in part]
    vmem = pl.BlockSpec(memory_space=pltpu.VMEM)
    return pl.pallas_call(
        functools.partial(unturn_kernel, len(parts)),
        out_shape=jax.ShapeDtypeStruct((rows, 3 * D), BF),
        in_specs=[vmem] * (len(arrays) + 3),
        out_specs=vmem,
        cost_estimate=cost(20 * rows * 3 * D, rows * D * 30),
        name="unturn",
    )(*arrays, *tables)


def piece_bits(order, index):
    picked = dict(zip(order, ((index >> 2) & 1, (index >> 1) & 1, index & 1)))
    return picked["y"], picked["x"], picked["z"]


def rows_kernel(orders, lefts, spots_ref, *refs):
    left_refs = refs[: 2 * lefts]
    right_refs = refs[2 * lefts : 4 * lefts]
    split_orders = len(orders) == 2
    riders = refs[4 * lefts : 4 * lefts + 2] if split_orders else ()
    outs = refs[4 * lefts + len(riders) : -2]
    turned_ref, picked_ref = refs[-2:]
    y, core, x, z = spots_ref[0], spots_ref[1], spots_ref[2], spots_ref[3]
    rows = left_refs[0].shape[0]
    high = D // 16

    def turned(own_ref, other_ref, slot):
        turned_ref[slot, :, 0:rows] = jnp.transpose(own_ref[...])
        turned_ref[slot, :, rows : 2 * rows] = jnp.transpose(other_ref[...])

    def pick(slot, order, place):
        for index in range(8):
            dy, dx, dz = piece_bits(order, index)
            start = (y ^ dy) * (D // 2) + core * (D // 4) + ((x ^ dx) * 2 + (z ^ dz)) * high
            picked_ref[place, index * high : index * high + high, :] = turned_ref[
                slot, pl.ds(pl.multiple_of(start, 16), high), :
            ]

    def multiply(place, own_ref, other_ref, source, block, keep_ref, send_ref):
        columns = pl.ds(pl.multiple_of(source * D, D), D)
        product = jnp.dot(
            picked_ref[place, :, 0:rows], own_ref[:, columns], preferred_element_type=F32
        )
        product += jnp.dot(
            picked_ref[place, :, rows : 2 * rows],
            other_ref[:, columns],
            preferred_element_type=F32,
        )
        span = pl.ds(pl.multiple_of(block * high, 16), high)
        for index in range(4):
            keep_ref[index, span, :] = product[index * high : index * high + high, :]
            send_ref[index, span, :] = product[
                (4 + index) * high : (4 + index) * high + high, :
            ].astype(BF)

    turned(left_refs[0], left_refs[1], 0)
    pick(0, orders[0], 0)
    blocks = right_refs[0].shape[1] // D
    split = 2 if len(orders) == 2 else blocks

    def body(block, carry):
        multiply(0, right_refs[0], right_refs[1], block, block, *outs[:2])
        return carry

    lax.fori_loop(0, split, body, 0)
    if len(orders) == 2:
        for index in range(8):
            dy, dx, dz = piece_bits(orders[0], index)
            entry = ((y ^ dy) * 2 + core) * 4 + (x ^ dx) * 2 + (z ^ dz)
            value = riders[0][entry] + riders[1][entry]
            value = jnp.concatenate([value, jnp.zeros((14, D), F32)], axis=0)
            if index < 4:
                outs[0][index, 2 * high : 2 * high + 16, :] = value
            else:
                outs[1][index - 4, 2 * high : 2 * high + 16, :] = value.astype(BF)
        pick(0, orders[1], 1)
        multiply(1, right_refs[0], right_refs[1], 2, 0, *outs[2:])
    if lefts == 2:
        turned(left_refs[2], left_refs[3], 1)
        pick(1, orders[-1], 2)
        multiply(2, right_refs[2], right_refs[3], 0, 1 if len(orders) == 2 else blocks, *outs[-2:])


def rows_unit(spots, orders, lefts, rights, riders=()):
    rows = lefts[0][0].shape[0]
    arrays = [value for pair in (*lefts, *rights) for value in pair] + list(riders)
    high = D // 4 // len(orders)
    heights = [high + 16, high] if riders else [high] * len(orders)
    vmem = pl.BlockSpec(memory_space=pltpu.VMEM)
    return pl.pallas_call(
        functools.partial(rows_kernel, orders, len(lefts)),
        out_shape=[
            jax.ShapeDtypeStruct((4, tall, D), kind) for tall in heights for kind in (F32, BF)
        ],
        in_specs=[pl.BlockSpec(memory_space=pltpu.SMEM)] + [vmem] * len(arrays),
        out_specs=[vmem] * (2 * len(orders)),
        scratch_shapes=[
            pltpu.VMEM((len(lefts), D, 2 * rows), BF),
            pltpu.VMEM((3 if len(lefts) == 2 else 1, D // 2, 2 * rows), BF),
        ],
        cost_estimate=cost(4 * rows * (D // 2) * 4 * D, rows * D * 20 + 3 * D * D),
        name="rows_unit",
    )(spots, *arrays)


def forward_kernel(orders, spots_ref, n0, n1, u0, u1, a0, a1, d0, d1, *refs):
    turned_ref, picked_ref, tall_ref = refs[-3:]
    keep_ref, send_ref, keep_down, send_down = (refs[:-3] * 2)[:4]
    y, core, x, z = spots_ref[0], spots_ref[1], spots_ref[2], spots_ref[3]
    rows = n0.shape[0]
    high = D // 16
    tall = D // 4
    first = tall if len(orders) == 1 else 0
    turned_ref[:, 0:rows] = jnp.transpose(n0[...])
    turned_ref[:, rows : 2 * rows] = jnp.transpose(n1[...])
    for index in range(8):
        dy, dx, dz = piece_bits(orders[0], index)
        start = (y ^ dy) * (D // 2) + core * (D // 4) + ((x ^ dx) * 2 + (z ^ dz)) * high
        picked_ref[index * high : index * high + high, :] = turned_ref[
            pl.ds(pl.multiple_of(start, 16), high), :
        ]

    def body(block, carry):
        columns = pl.ds(pl.multiple_of(block * D, D), D)
        product = jnp.dot(picked_ref[:, 0:rows], u0[:, columns], preferred_element_type=F32)
        product += jnp.dot(
            picked_ref[:, rows : 2 * rows], u1[:, columns], preferred_element_type=F32
        )
        span = pl.ds(pl.multiple_of(block * high, 16), high)
        for index in range(4):
            keep_ref[index, span, :] = product[index * high : index * high + high, :]
            send_ref[index, span, :] = product[
                (4 + index) * high : (4 + index) * high + high, :
            ].astype(BF)
        return carry

    lax.fori_loop(0, 4, body, 0)
    for dy in range(2):
        columns = pl.ds(pl.multiple_of(((y ^ dy) * 2 + core) * D, D), D)
        tall_ref[dy, :, 0:rows] = jnp.transpose(a0[:, columns])
        tall_ref[dy, :, rows : 2 * rows] = jnp.transpose(a1[:, columns])
        for dx in range(2):
            for dz in range(2):
                start = pl.multiple_of(((x ^ dx) * 2 + (z ^ dz)) * tall, 16)
                left = tall_ref[dy, pl.ds(start, tall), :]
                product = jnp.dot(left[:, 0:rows], d0[...], preferred_element_type=F32)
                product += jnp.dot(left[:, rows : 2 * rows], d1[...], preferred_element_type=F32)
                index = [k for k in range(8) if piece_bits(orders[-1], k) == (dy, dx, dz)][0]
                if index < 4:
                    keep_down[index, first : first + tall, :] = product
                else:
                    send_down[index - 4, first : first + tall, :] = product.astype(BF)


def forward_unit(spots, orders, normed, grad_up, activated, grad_down):
    rows = normed[0].shape[0]
    vmem = pl.BlockSpec(memory_space=pltpu.VMEM)
    return pl.pallas_call(
        functools.partial(forward_kernel, orders),
        out_shape=[
            jax.ShapeDtypeStruct((4, D // 2 // len(orders), D), kind)
            for _ in orders
            for kind in (F32, BF)
        ],
        in_specs=[pl.BlockSpec(memory_space=pltpu.SMEM)] + [vmem] * 8,
        out_specs=[vmem] * (2 * len(orders)),
        scratch_shapes=[
            pltpu.VMEM((D, 2 * rows), BF),
            pltpu.VMEM((D // 2, 2 * rows), BF),
            pltpu.VMEM((2, D, 2 * rows), BF),
        ],
        cost_estimate=cost(8 * rows * (D // 2) * 4 * D, rows * D * 40 + 6 * D * D),
        name="forward_unit",
    )(spots, *normed, *grad_up, *activated, *grad_down)


AXES = {"y": ("fsdp", 2), "x": ("dp", 1), "z": ("dp", 2)}


class Sum:
    def __init__(self, line, unit, order):
        self.line, self.order, self.stage = line, order, 0
        self.keep, send = unit
        self.moving = swap(send, *AXES[order[0]])
        self.far = [1 << k for k in range(2, 20) if (1 << k) < lax.axis_size("dp")]
        self.rest = [name for name in order if name != "y"]

    def step(self):
        got, keep = self.line.enter(self.moving, self.keep)
        line, stage = self.line, self.stage
        self.stage += 1
        if stage < 3:
            half = keep.shape[0] // 2
            if stage < 2:
                self.keep = keep[:half] + got[:half].astype(F32)
                send = (keep[half:] + got[half:].astype(F32)).astype(BF)
                line.leave(self.keep, send)
                self.moving = swap(send, *AXES[self.order[stage + 1]])
                return
            self.keep = (keep + got.astype(F32)).astype(BF)
        elif stage < 3 + len(self.far):
            self.keep = (keep.astype(F32) + got.astype(F32)).astype(BF)
        elif stage == 3 + len(self.far):
            self.keep = jnp.concatenate([keep, got], axis=0)
            line.leave(self.keep)
            self.moving = swap(self.keep, *AXES[self.rest[0]])
            return
        else:
            self.result = (keep, got)
            return
        line.leave(self.keep)
        if stage - 2 < len(self.far):
            self.moving = swap(self.keep, "dp", self.far[stage - 2])
        else:
            self.moving = swap(self.keep, *AXES[self.rest[1]])

    def finish(self):
        while self.stage < 5 + len(self.far):
            self.step()
        return self.result


def emit_kernel(orders, places, count, spots_ref, *refs):
    outs = refs[-count:]
    x, z = spots_ref[2], spots_ref[3]
    high = D // 16
    for number, order in enumerate(orders):
        rest = [name for name in order if name != "y"]
        for outer in range(2):
            piece = refs[2 * number + outer]
            for inner in range(2):
                picked = dict(zip(rest, (outer, inner)))
                which = (x ^ picked["x"]) * 2 + (z ^ picked["z"])
                at = 0
                for slot, block in places[number]:
                    if block == RIDER:
                        outs[slot][which] = piece[inner, at : at + 16, :].astype(F32)[0:2]
                        continue
                    tall = high if block is not None else 4 * high
                    start = pl.multiple_of(which * tall, 16)
                    first = 0 if block is None else block * D
                    outs[slot][0, pl.ds(start, tall), first : first + D] = piece[
                        inner, at : at + tall, :
                    ].astype(F32)
                    at += tall


def emit(spots, sums, orders, places, shapes, layer, before):
    out_shape = [jax.ShapeDtypeStruct((LAYERS,) + shape, F32) for shape in shapes]
    before = list(before) if before is not None else []
    pieces = [piece for pair in sums for piece in pair]
    extra = []
    if any(block == RIDER for place in places for _, block in place):
        out_shape.append(jax.ShapeDtypeStruct((4, 2, D), F32))
        extra.append(pl.BlockSpec((4, 2, D), lambda i, spots: (0, 0, 0)))
    return pl.pallas_call(
        functools.partial(emit_kernel, orders, places, len(out_shape)),
        out_shape=out_shape,
        grid_spec=pltpu.PrefetchScalarGridSpec(
            num_scalar_prefetch=1,
            grid=(1,),
            in_specs=[pl.BlockSpec(memory_space=pltpu.VMEM)] * len(pieces)
            + [pl.BlockSpec(memory_space=pl.ANY)] * len(before),
            out_specs=[
                pl.BlockSpec((1,) + shape, lambda i, spots: (layer, 0, 0)) for shape in shapes
            ]
            + extra,
        ),
        input_output_aliases={1 + len(pieces) + i: i for i in range(len(before))},
        cost_estimate=cost(0, D * D * 6),
        name="emit",
    )(spots, *pieces, *before)


class Line:
    def __init__(self):
        self.last = ()

    def enter(self, *values):
        out = lax.optimization_barrier(tuple(values) + tuple(self.last))
        return out[: len(values)]

    def leave(self, *values):
        self.last = tuple(values)

    def sync(self, *values):
        out = self.enter(*values)
        self.last = tuple(out)
        return out


def after(value, *others):
    return lax.optimization_barrier((value,) + others)[0]


NAMES = (
    "input_bias",
    "output_bias",
    "first_gain",
    "first_shift",
    "up_bias",
    "down_bias",
    "second_gain",
    "second_shift",
)
WIDTHS = (3 * D, D, D, D, 4 * D, D, D, D)


def feed_forward(hidden, context, weights, small, between):
    _, output_weight, up_weight, down_weight = weights
    attn_out = jnp.dot(context, output_weight, preferred_element_type=F32) + small["output_bias"]
    first_in = hidden + attn_out
    normed = layer_norm(first_in, small["first_gain"], small["first_shift"])
    normed_low = between(normed.astype(BF))
    up_value = jnp.dot(normed_low, up_weight, preferred_element_type=F32) + small["up_bias"]
    part = normal_part(up_value)
    activated = (up_value * part).astype(BF)
    slope = gelu_slope(up_value, part)
    down_value = (
        jnp.dot(activated, down_weight, preferred_element_type=F32) + small["down_bias"]
    )
    second_in = normed + down_value
    output = layer_norm(second_in, small["second_gain"], small["second_shift"])
    return output, first_in, normed_low, slope, activated, second_in


def feed_backward(grad_output, weights, small, first_in, slope, second_in):
    _, output_weight, up_weight, down_weight = weights
    pull_second = jax.vjp(layer_norm, second_in, small["second_gain"], small["second_shift"])[1]
    grad_second, grad_second_gain, grad_second_shift = pull_second(grad_output)
    grad_down = grad_second.astype(BF)
    grad_down_bias = jnp.sum(grad_down, axis=0, dtype=F32)
    grad_activated = contract_cols(grad_down, down_weight)
    grad_up = (grad_activated * slope).astype(BF)
    grad_up_bias = jnp.sum(grad_up, axis=0, dtype=F32)
    grad_normed = grad_second + contract_cols(grad_up, up_weight)
    pull_first = jax.vjp(layer_norm, first_in, small["first_gain"], small["first_shift"])[1]
    grad_first, grad_first_gain, grad_first_shift = pull_first(grad_normed)
    grad_attn = grad_first.astype(BF)
    grad_output_bias = jnp.sum(grad_attn, axis=0, dtype=F32)
    grad_context = contract_cols(grad_attn, output_weight).astype(BF)
    little = (
        grad_output_bias,
        grad_first_gain,
        grad_first_shift,
        grad_up_bias,
        grad_down_bias,
        grad_second_gain,
        grad_second_shift,
    )
    return grad_down, grad_up, grad_attn, grad_context, grad_first, little


FORWARD_ORDER = (("xzy", "zxy"), ("xzy",))
JOINT_ORDER = (("yxz", "xzy"), ("xzy",))


def on_device(
    tokens,
    cotangent,
    lengths,
    input_weight,
    input_bias,
    output_weight,
    output_bias,
    first_gain,
    first_shift,
    up_weight,
    up_bias,
    down_weight,
    down_bias,
    second_gain,
    second_shift,
):
    place = lax.axis_index("fsdp")
    group = lax.axis_index("dp")
    core = place & 1
    x_bit, z_bit = group & 1, (group >> 1) & 1
    spots = jnp.stack([place >> 1, core, x_bit, z_bit]).astype(jnp.int32)
    row_count = tokens.shape[0]
    places = place * row_count + jnp.arange(row_count, dtype=jnp.int32)
    length = lengths[0]
    info = jnp.stack([place, length]).astype(jnp.int32)
    row_valid = (places < length).astype(F32)

    swap_core = lambda value: swap(value, "fsdp", 1)
    swap_y = lambda value: swap(value, "fsdp", 2)
    swap_x = lambda value: swap(value, "dp", 1)
    swap_z = lambda value: swap(value, "dp", 2)

    rows_of = D // 4
    quarter = rows_of // 4
    start = (x_bit * 2 + z_bit) * quarter
    quarters = [
        x_bit * 2 + z_bit,
        x_bit * 2 + (1 - z_bit),
        (1 - x_bit) * 2 + z_bit,
        (1 - x_bit) * 2 + (1 - z_bit),
    ]
    spread_spots = jnp.stack(
        [place * rows_of, (place ^ 1) * rows_of]
        + [(place ^ 2) * rows_of + q * quarter for q in quarters]
        + [(place ^ 3) * rows_of + q * quarter for q in quarters]
    ).astype(jnp.int32)
    direct_spots = jnp.stack([(place ^ k) * rows_of for k in range(4)]).astype(jnp.int32)
    rest_spec = (("rows", D), ("rows", 4 * D), ("split", 4 * D))

    def wide(i):
        split = [down_weight[i, k * 192 : k * 192 + 192] for k in range(4)]
        return jnp.concatenate([output_weight[i], up_weight[i]] + split, axis=1)

    line = Line()

    input_one, input_two = input_weight[0], input_weight[1]
    over_y = swap_y(input_one)
    packed = jnp.concatenate(
        (
            input_bias,
            output_bias,
            first_gain,
            first_shift,
            up_bias,
            down_bias,
            second_gain,
            second_shift,
        ),
        axis=1,
    )
    packed_y, packed_c, input_c = swap_y(packed), swap_core(packed), swap_core(input_one)
    tables = rotary_tables(places.astype(F32))
    rests = (wide(0), wide(1))
    mine = [lax.dynamic_slice(r, (start, 0), (quarter, r.shape[1])) for r in rests]
    line.leave(*mine, *tables, spread_spots, direct_spots, info, spots)
    over_y, packed_y, packed_c, input_c = line.sync(over_y, packed_y, packed_c, input_c)
    spread_y = swap_y(after(mine[0], over_y))
    rest_c = swap_core(after(rests[0], over_y))
    packed_yc, input_yc = swap_core(packed_y), swap_core(over_y)
    fields = unpack(info, [packed, packed_c, packed_y, packed_yc], WIDTHS)
    smalls = [
        dict(zip(NAMES, fields[i * len(NAMES) : (i + 1) * len(NAMES)])) for i in range(LAYERS)
    ]
    pieces = [input_one, input_c, over_y, input_yc]
    line.leave(*fields)
    hidden, rounded = tokens.astype(F32), tokens
    kept, weights = [], []
    for i in range(LAYERS):
        more = i + 1 < LAYERS
        small = smalls[i]
        pieces = line.enter(*pieces)
        queries, *kvs, whole = project(
            rounded, pieces, direct_spots, small["input_bias"], tables
        )
        line.leave(queries, *kvs, whole)
        kv_y, kv_c = [swap_y(kv) for kv in kvs], [swap_core(kv) for kv in kvs]
        if i == 0:
            spread_y, rest_c = line.sync(spread_y, rest_c)
            spread_z, spread_x = swap_z(spread_y), swap_x(spread_y)
        else:
            (rest_c,) = line.sync(rest_c)
            saved = [kept[0][8], kept[0][6], kept[0][4], rounded]
            shared = line.sync(*[swap_core(v) for v in saved[:2]])
            shared += line.sync(*[swap_core(v) for v in saved[2:]])
            act1, normed1, context1, rounded2 = list(zip(saved, shared))
        chunks, logs = [], []
        context, rest = None, None
        for part in range(PARTS):
            if part == 1:
                spread_z, spread_x = line.sync(spread_z, spread_x)
                spread_xz = swap_x(spread_z)
                crossed = [swap_core(v) for v in (spread_y, spread_z, spread_x)]
            if part == 2:
                crossed = list(line.sync(*crossed))
            got_y, got_c = line.sync(kv_y[part], kv_c[part])
            (got_yc,) = line.sync(swap_core(got_y))
            if more and part == PARTS - 1:
                over_y, input_c = swap_y(after(input_two, got_yc)), swap_core(after(input_two, got_yc))
                next_y = swap_y(after(mine[1], got_yc))
            chunks.append([kvs[part], got_c, got_y, got_yc])
            (query_in,) = line.enter(queries)
            context, log = attend(info, query_in, chunks[-1], part, context)
            line.leave(context, log)
            logs.append(log)
        (spread_xz,) = line.sync(spread_xz)
        crossed.append(swap_core(spread_xz))
        crossed[3:] = line.sync(*crossed[3:])
        pieces = [rests[i], rest_c, spread_y, spread_z, spread_x, spread_xz, *crossed]
        pieces = line.enter(*pieces)
        rest = assemble(pieces, spread_spots, rest_spec)
        weights.append((whole, *rest))
        line.leave(*rest)
        if more:
            over_y, input_c = line.sync(over_y, input_c)
            input_yc = swap_core(over_y)
            rest_c = swap_core(after(rests[1], over_y))
        moving = []

        def between(value):
            if not more:
                return value
            line.leave(value)
            (arrived,) = line.sync(next_y)
            moving.extend((arrived, swap_z(arrived), swap_x(arrived)))
            return line.enter(value)[0]

        (context_in,) = line.enter(context)
        output, first_in, normed, slope, activated, second_in = feed_forward(
            hidden, context_in, weights[i], small, between
        )
        kept.append(
            (rounded, queries, chunks, logs, context, first_in, normed, slope, activated, second_in)
        )
        hidden, rounded = output, output.astype(BF)
        line.leave(hidden, rounded)
        if more:
            spread_y, spread_z, spread_x = moving
            pieces = [input_two, input_c, over_y, input_yc]
    result = rounded

    def both_cores(*values):
        values = line.enter(*values)
        return [(value, swap_core(value)) for value in values]

    def feed_back(grad_output, i):
        (grad_output,) = line.enter(grad_output)
        _, _, _, _, _, first_in, _, slope, _, second_in = kept[i]
        out = feed_backward(grad_output, weights[i], smalls[i], first_in, slope, second_in)
        line.leave(*out[:5])
        return out

    def attention_back(i, grad_context, part):
        queries, chunks, logs = kept[i][1:4]
        (grad_context,) = line.enter(grad_context)
        dq, own, give = pull(info, queries, grad_context, logs[part], chunks[part], part)
        line.leave(dq, own, give)
        return dq, own, swap_core(give)

    def far_back(pulled):
        dq, own, near = pulled
        own, near = line.enter(own, near)
        far = (own[2:] + near[2:].astype(F32)).astype(BF)
        line.leave(far)
        return dq, own, near, swap_y(far)

    def arrive(far):
        dq, own, near, moving = far
        (moving,) = line.sync(moving)
        return dq, own, near, moving

    def forward_sum(i, normed, grad_up, activated, grad_down):
        pairs = (normed, grad_up, activated, grad_down)
        got = line.enter(*[pair[1] for pair in pairs])
        unit = forward_unit(
            spots, FORWARD_ORDER[i], *[(pair[0], g) for pair, g in zip(pairs, got)]
        )
        line.leave(*unit)
        return [
            Sum(line, unit[2 * k : 2 * k + 2], order) for k, order in enumerate(FORWARD_ORDER[i])
        ]

    def joint_sum(i, rounded, grad_joint, context, grad_attn, riders=()):
        got = line.enter(rounded[1], grad_joint[1], context[1], grad_attn[1])
        pairs = [(p[0], g) for p, g in zip((rounded, grad_joint, context, grad_attn), got)]
        unit = rows_unit(
            spots, JOINT_ORDER[i], [pairs[0], pairs[2]], [pairs[1], pairs[3]], riders
        )
        line.leave(*unit)
        return [
            Sum(line, unit[2 * k : 2 * k + 2], order) for k, order in enumerate(JOINT_ORDER[i])
        ]

    def joint_back(i, parts, grad_first):
        flat = line.enter(*[v for part in parts for v in part])
        parts = [flat[4 * k : 4 * k + 4] for k in range(len(parts))]
        grad_joint = unturn(parts, tables)
        line.leave(grad_joint)
        grad_hidden = grad_first + contract_cols(grad_joint, weights[i][0])
        return grad_joint, jnp.sum(grad_joint, axis=0, dtype=F32), grad_hidden

    grad_hidden = cotangent.astype(F32) * row_valid[:, None]
    act2, normed2 = both_cores(kept[1][8], kept[1][6])
    dd2, du2, da2, dc2, grad_first2, little2 = feed_back(grad_hidden, 1)

    def retire(*pairs):
        got = line.sync(*[pair[1] for pair in pairs])
        return [(pair[0], value) for pair, value in zip(pairs, got)]

    act2, normed2 = retire(act2, normed2)
    dd2, du2 = both_cores(dd2, du2)
    p0 = attention_back(1, dc2, 0)
    dd2, du2 = retire(dd2, du2)
    context2, da2 = both_cores(kept[1][4], da2)
    p1 = attention_back(1, dc2, 1)
    context2, da2 = retire(context2, da2)
    p0 = far_back(p0)
    p2 = attention_back(1, dc2, 2)
    p0 = arrive(p0)
    p1 = far_back(p1)
    (f2,) = forward_sum(1, normed2, du2, act2, dd2)
    p1 = arrive(p1)
    p2 = far_back(p2)
    p2 = arrive(p2)
    joint2, bias2, grad_hidden = joint_back(1, (p0, p1, p2), grad_first2)
    (joint2,) = both_cores(joint2)
    dd1, du1, da1, dc1, grad_first1, little1 = feed_back(grad_hidden, 0)
    (joint2,) = retire(joint2)
    f2.step()
    dd1, du1 = both_cores(dd1, du1)
    (j2,) = joint_sum(1, rounded2, joint2, context2, da2)
    dd1, du1 = retire(dd1, du1)
    u1, d1 = forward_sum(0, normed1, du1, act1, dd1)
    f2.step()
    rounded1, da1 = both_cores(kept[0][0], da1)
    p0 = attention_back(0, dc1, 0)
    rounded1, da1 = retire(rounded1, da1)
    j2.step()
    f2.step()
    p1 = attention_back(0, dc1, 1)
    p0 = far_back(p0)
    u1.step()
    d1.step()
    p2 = attention_back(0, dc1, 2)
    p0 = arrive(p0)
    p1 = far_back(p1)
    f2.step()
    j2.step()
    u1.step()
    p1 = arrive(p1)
    p2 = far_back(p2)
    d1.step()
    j2.step()
    f2.step()
    shape_forward = [(D // 4, 4 * D), (D, D)]
    shape_joint = [(D // 4, 3 * D), (D // 4, D)]
    up_places, down_places = [(0, 0), (0, 1), (0, 2), (0, 3)], [(1, None)]

    def write(chains, orders, places, shapes, layer, before):
        sums = [chain.finish() for chain in chains]
        out = emit(spots, sums, orders, places, shapes, layer, before)
        line.leave(*out)
        return out

    p2 = arrive(p2)
    joint1, bias1, grad_hidden = joint_back(0, (p0, p1, p2), grad_first1)
    (joint1,) = both_cores(joint1)
    packed = pack(
        [part.reshape(-1) for layer in ((bias1, *little1), (bias2, *little2)) for part in layer]
    )
    line.leave(packed)
    packed_pair = both_cores(packed)
    u1.step()
    d1.step()
    j2.step()
    joint1, packed_pair = retire(joint1, *packed_pair)
    j1 = joint_sum(0, rounded1, joint1, context1, da1, packed_pair)
    u1.step()
    d1.step()
    j2.step()
    out_forward = write(
        [f2], FORWARD_ORDER[1], ([*up_places, *down_places],), shape_forward, 1, None
    )
    j1[0].step()
    j1[1].step()
    u1.step()
    d1.step()
    j1[0].step()
    j1[1].step()
    out_joint = write(
        [j2],
        JOINT_ORDER[1],
        ([(0, 0), (0, 1), (0, 2), (1, 0)],),
        shape_joint,
        1,
        None,
    )
    j1[0].step()
    j1[1].step()
    j1[0].step()
    j1[1].step()
    out_forward = write(
        [u1, d1], FORWARD_ORDER[0], (up_places, down_places), shape_forward, 0, out_forward
    )
    j1[0].step()
    j1[1].step()
    *out_joint, flat = write(
        j1,
        JOINT_ORDER[0],
        ([(0, 0), (0, 1), (2, RIDER)], [(0, 2), (1, 0)]),
        shape_joint,
        0,
        out_joint,
    )
    flat = spread(flat, WIDTHS)

    small_grads = dict(zip(NAMES, flat))
    return (
        result,
        grad_hidden,
        out_joint[0],
        small_grads["input_bias"],
        out_joint[1],
        small_grads["output_bias"],
        small_grads["first_gain"],
        small_grads["first_shift"],
        out_forward[0],
        small_grads["up_bias"],
        out_forward[1],
        small_grads["down_bias"],
        small_grads["second_gain"],
        small_grads["second_shift"],
    )


def solution(mesh):
    rows = P(("dp", "fsdp"), None)
    matrix = P(None, "fsdp", None)
    vector = P(None, "fsdp")
    parameters = (
        matrix,
        vector,
        matrix,
        vector,
        vector,
        vector,
        matrix,
        vector,
        matrix,
        vector,
        vector,
        vector,
    )
    return jax.shard_map(
        on_device,
        mesh=mesh,
        in_specs=(rows, rows, P("dp"), *parameters),
        out_specs=(rows, rows, *parameters),
        check_vma=False,
    )
```

```python
import functools

import jax
import jax.numpy as jnp
from jax import lax
from jax.experimental import pallas as pl
from jax.experimental.pallas import tpu as pltpu
from jax.sharding import PartitionSpec as P

D = 768
HEADS = 12
HEAD = 64
PAIRS = HEADS // 2
LAYERS = 2
RIDER = -1
PARTS = 3
GROUP = PAIRS // PARTS
WIDE = GROUP * 128
LOG2E = 1.4426950408889634
SCALE = HEAD ** (-0.5)
NEG = -1e30
BF = jnp.bfloat16
F32 = jnp.float32

norm_eps = 1e-12


def swap(value, axis, bit):
    count = lax.axis_size(axis)
    return lax.ppermute(value, axis, [(i, i ^ bit) for i in range(count)])


def layer_norm(matrix, norm_gain, norm_shift):
    row_mean = jnp.mean(matrix, axis=-1, keepdims=True)
    centred = matrix - row_mean
    spread = jnp.mean(centred * centred, axis=-1, keepdims=True)
    return centred * lax.rsqrt(spread + norm_eps) * norm_gain + norm_shift


def normal_part(value):
    return 0.5 + 0.5 * lax.erf(value * 0.7071067811865476)


def gelu_slope(value, part):
    return part + value * jnp.exp(-0.5 * value * value) * 0.3989422804014327


def contract_rows(left_side, right_side):
    return lax.dot_general(
        left_side, right_side, (((0,), (0,)), ((), ())), preferred_element_type=F32
    )


def contract_cols(left_side, right_side):
    return lax.dot_general(
        left_side, right_side, (((1,), (1,)), ((), ())), preferred_element_type=F32
    )


def cost(flops, bytes_accessed, transcendentals=0):
    return pl.CostEstimate(
        flops=int(flops), bytes_accessed=int(bytes_accessed), transcendentals=int(transcendentals)
    )


def rotary_tables(places):
    frequency = 10000.0 ** (-2.0 * jnp.arange(HEAD // 2, dtype=F32) / HEAD)
    angles = places[:, None] * frequency[None, :]
    cosine, sine = jnp.cos(angles), jnp.sin(angles)
    nothing = jnp.zeros_like(sine)
    wide = jnp.concatenate([cosine] * 4, axis=1)
    first = jnp.concatenate([-sine, nothing] * 2, axis=1)
    second = jnp.concatenate([nothing, sine] * 2, axis=1)
    return wide, first, second


def turn(block, wide, first, second):
    return (
        block * wide
        + pltpu.roll(block, 96, 1) * first
        + pltpu.roll(block, 32, 1) * second
    )


def assemble_kernel(spec, count, pos_ref, *refs):
    pieces = refs[:count]
    outs = refs[count : count + len(spec)]
    held, in_sem, out_sem = refs[count + len(spec) :]
    copies = []
    for index, piece in enumerate(pieces):
        rows = piece.shape[0]
        start = pl.multiple_of(pos_ref[index], 16)
        copies.append(
            pltpu.make_async_copy(piece, held.at[pl.ds(start, rows), :], in_sem.at[index])
        )
    for copy in copies:
        copy.start()
    for copy in copies:
        copy.wait()
    copies = []
    column = 0
    for slot, (kind, width) in enumerate(spec):
        if kind == "rows":
            copies.append((held.at[:, pl.ds(column, width)], outs[slot]))
        else:
            shard = held.shape[0] // 4
            for source in range(4):
                for part in range(width // D):
                    copies.append(
                        (
                            held.at[pl.ds(source * shard, shard), pl.ds(column + part * D, D)],
                            outs[slot].at[pl.ds(source * 4 * shard + part * shard, shard), :],
                        )
                    )
        column += width
    copies = [
        pltpu.make_async_copy(src, dst, out_sem.at[index])
        for index, (src, dst) in enumerate(copies)
    ]
    for copy in copies:
        copy.start()
    for copy in copies:
        copy.wait()


def assemble(pieces, positions, spec):
    width = pieces[0].shape[1]
    out_shape = []
    outputs = 0
    for kind, columns in spec:
        if kind == "rows":
            out_shape.append(jax.ShapeDtypeStruct((D, columns), BF))
            outputs += 1
        else:
            out_shape.append(jax.ShapeDtypeStruct((columns, D), BF))
            outputs += 4 * (columns // D)
    return pl.pallas_call(
        functools.partial(assemble_kernel, spec, len(pieces)),
        out_shape=out_shape,
        in_specs=[pl.BlockSpec(memory_space=pltpu.SMEM)]
        + [pl.BlockSpec(memory_space=pl.ANY)] * len(pieces),
        out_specs=[pl.BlockSpec(memory_space=pl.ANY)] * len(spec),
        scratch_shapes=[
            pltpu.VMEM((D, width), BF),
            pltpu.SemaphoreType.DMA((len(pieces),)),
            pltpu.SemaphoreType.DMA((outputs,)),
        ],
        cost_estimate=cost(0, 4 * D * width),
        name="assemble",
    )(positions, *pieces)


def pack_kernel(*refs):
    *parts, out_ref, flat_ref = refs
    offset = 0
    flat_ref[...] = jnp.zeros_like(flat_ref)
    for part in parts:
        width = part.shape[0] // 4
        values = part[...].reshape(1, 4 * width)
        for owner in range(4):
            flat_ref[owner : owner + 1, offset : offset + width] = values[
                :, owner * width : owner * width + width
            ]
        offset += width
    for owner in range(4):
        for row in range(8):
            out_ref[4 * owner + row // 2, row % 2 : row % 2 + 1, :] = flat_ref[
                owner : owner + 1, row * D : row * D + D
            ]


def spread_kernel(count, rows_ref, *refs):
    *outs, flat_ref = refs
    for row in range(8):
        flat_ref[:, row * D : row * D + D] = rows_ref[row // 2, row % 2 : row % 2 + 1, :]
    offset = 0
    for layer in range(LAYERS):
        for slot in range(count):
            width = outs[slot].shape[1]
            outs[slot][layer : layer + 1, :] = flat_ref[:, offset : offset + width]
            offset += width


def pack(parts):
    vmem = pl.BlockSpec(memory_space=pltpu.VMEM)
    return pl.pallas_call(
        pack_kernel,
        out_shape=jax.ShapeDtypeStruct((16, 2, D), F32),
        in_specs=[vmem] * len(parts),
        out_specs=vmem,
        scratch_shapes=[pltpu.VMEM((4, 8 * D), F32)],
        cost_estimate=cost(0, 200000),
        name="pack",
    )(*parts)


def spread(rows, widths):
    vmem = pl.BlockSpec(memory_space=pltpu.VMEM)
    return pl.pallas_call(
        functools.partial(spread_kernel, len(widths)),
        out_shape=[jax.ShapeDtypeStruct((LAYERS, width // 4), F32) for width in widths],
        in_specs=[vmem],
        out_specs=[vmem] * len(widths),
        scratch_shapes=[pltpu.VMEM((1, 8 * D), F32)],
        cost_estimate=cost(0, 50000),
        name="spread",
    )(rows)


def project_kernel(count, pos_ref, h_ref, b_ref, cos_ref, first_ref, second_ref, *refs):
    pieces = refs[:count]
    q_ref, *kv_refs, whole_ref, held, in_sem, out_sem = refs[count:]
    copies = []
    for part in range(3):
        for index, piece in enumerate(pieces):
            rows = piece.shape[0]
            start = pl.multiple_of(pos_ref[index], 16)
            copies.append(
                pltpu.make_async_copy(
                    piece.at[:, pl.ds(part * D, D)],
                    held.at[part, pl.ds(start, rows), :],
                    in_sem.at[part * count + index],
                )
            )
    for copy in copies:
        copy.start()
    outs = [
        pltpu.make_async_copy(
            held.at[part], whole_ref.at[:, pl.ds(part * D, D)], out_sem.at[part]
        )
        for part in range(3)
    ]
    for part in range(3):
        for copy in copies[part * count : part * count + count]:
            copy.wait()
        outs[part].start()
        joint = jnp.dot(h_ref[...], held[part], preferred_element_type=F32)
        joint = joint + b_ref[:, part * D : part * D + D]
        if part == 2:
            for index in range(PARTS):
                kv_refs[index][:, WIDE:] = joint[:, index * WIDE : index * WIDE + WIDE].astype(BF)
            continue
        for pair in range(PAIRS):
            span = slice(pair * 128, pair * 128 + 128)
            turned = turn(joint[:, span], cos_ref[...], first_ref[...], second_ref[...]).astype(BF)
            if part == 0:
                q_ref[:, span] = turned
            else:
                at = pair % GROUP * 128
                kv_refs[pair // GROUP][:, at : at + 128] = turned
    for copy in outs:
        copy.wait()


def project(rounded, pieces, positions, bias, tables):
    rows = rounded.shape[0]
    count = len(pieces)
    return pl.pallas_call(
        functools.partial(project_kernel, count),
        out_shape=[
            jax.ShapeDtypeStruct((rows, D), BF),
            *[jax.ShapeDtypeStruct((rows, 2 * WIDE), BF)] * PARTS,
            jax.ShapeDtypeStruct((D, 3 * D), BF),
        ],
        in_specs=[pl.BlockSpec(memory_space=pltpu.SMEM)]
        + [pl.BlockSpec(memory_space=pltpu.VMEM)] * 5
        + [pl.BlockSpec(memory_space=pl.ANY)] * count,
        out_specs=[pl.BlockSpec(memory_space=pltpu.VMEM)] * (1 + PARTS)
        + [pl.BlockSpec(memory_space=pl.ANY)],
        scratch_shapes=[
            pltpu.VMEM((3, D, D), BF),
            pltpu.SemaphoreType.DMA((3 * count,)),
            pltpu.SemaphoreType.DMA((3,)),
        ],
        cost_estimate=cost(2 * rows * D * 3 * D, 2 * (rows * 4 * D + 3 * D * D)),
        name="project",
    )(positions, rounded, bias, *tables, *pieces)


def unpack_kernel(widths, place_ref, *refs):
    pieces, outs, held = refs[:4], refs[4:-1], refs[-1]
    place = place_ref[0]
    for index in range(4):
        held[index] = pieces[index][...].astype(F32)
    for source in range(4):
        shard = held[source ^ place]
        offset = 0
        for slot, width in enumerate(widths):
            part = width // 4
            for layer in range(LAYERS):
                outs[layer * len(widths) + slot][:, source * part : source * part + part] = shard[
                    layer : layer + 1, offset : offset + part
                ]
            offset += part


def unpack(info, pieces, widths):
    vmem = pl.BlockSpec(memory_space=pltpu.VMEM)
    return pl.pallas_call(
        functools.partial(unpack_kernel, widths),
        out_shape=[jax.ShapeDtypeStruct((1, width), F32) for width in widths] * LAYERS,
        in_specs=[pl.BlockSpec(memory_space=pltpu.SMEM)] + [vmem] * 4,
        out_specs=[vmem] * (LAYERS * len(widths)),
        scratch_shapes=[pltpu.VMEM((4,) + pieces[0].shape, F32)],
        cost_estimate=cost(0, 100000),
        name="unpack",
    )(info, *pieces)


def attend_kernel(part, info_ref, q_ref, *refs):
    keys, values = refs[0:4], refs[4:8]
    out_ref, log_ref, column_ref, score_ref, prob_ref = refs[-5:]
    pair = pl.program_id(0)
    rows = q_ref.shape[0]
    place, length = info_ref[0], info_ref[1]
    lane = lax.broadcasted_iota(jnp.int32, (1, 128), 1)
    key_lane = lax.broadcasted_iota(jnp.int32, (1, rows), 1)
    bias = jnp.concatenate(
        [
            jnp.where((place ^ k) * rows + key_lane < length, 0.0, NEG).astype(F32)
            for k in range(4)
        ],
        axis=1,
    )
    factor = SCALE * LOG2E
    block = 32
    query = q_ref[...]
    owns = [(lane >= head * HEAD) & (lane < head * HEAD + HEAD) for head in range(2)]
    for head in range(2):
        masked = jnp.where(owns[head], query, jnp.zeros_like(query))
        for k in range(4):
            score_ref[head, :, k * rows : (k + 1) * rows] = contract_cols(masked, keys[k][...])
    for head in range(2):
        for index in range(rows // block):
            span = slice(index * block, index * block + block)
            scores = score_ref[head, span, :] + bias
            peak = jnp.max(scores, axis=1, keepdims=True)
            powers = jnp.exp2((scores - peak) * factor)
            total = jnp.sum(powers, axis=1, keepdims=True)
            prob_ref[head, span, :] = (powers * (1.0 / total)).astype(BF)
            column_ref[span, :] = jnp.where(
                lane == 2 * pair + head, peak * factor + jnp.log2(total), column_ref[span, :]
            )
    outs = []
    for head in range(2):
        gathered = jnp.dot(prob_ref[head, :, 0:rows], values[0][...], preferred_element_type=F32)
        for k in range(1, 4):
            gathered += jnp.dot(
                prob_ref[head, :, k * rows : (k + 1) * rows],
                values[k][...],
                preferred_element_type=F32,
            )
        outs.append(gathered)
    out_ref[...] = jnp.where(owns[0], outs[0], outs[1]).astype(BF)

    @pl.when(pair == GROUP - 1)
    def _():
        log_ref[...] = jnp.transpose(column_ref[...])[0:8, :]


def attend(info, queries, chunks, part, before):
    rows = queries.shape[0]
    own = pl.BlockSpec((rows, 128), lambda p: (0, part * GROUP + p))
    before = [] if before is None else [before]
    return pl.pallas_call(
        functools.partial(attend_kernel, part),
        out_shape=[
            jax.ShapeDtypeStruct((rows, D), BF),
            jax.ShapeDtypeStruct((8, rows), F32),
        ],
        grid=(GROUP,),
        in_specs=[pl.BlockSpec(memory_space=pltpu.SMEM), own]
        + [pl.BlockSpec((rows, 128), lambda p: (0, p))] * 4
        + [pl.BlockSpec((rows, 128), lambda p: (0, GROUP + p))] * 4
        + [pl.BlockSpec(memory_space=pl.ANY)] * len(before),
        out_specs=[own, pl.BlockSpec((8, rows), lambda p: (0, 0))],
        scratch_shapes=[
            pltpu.VMEM((rows, 128), F32),
            pltpu.VMEM((2, rows, 4 * rows), F32),
            pltpu.VMEM((2, rows, 4 * rows), BF),
        ],
        input_output_aliases={10: 0} if before else {},
        cost_estimate=cost(
            4 * rows * 4 * rows * WIDE, 2 * rows * 10 * WIDE, rows * 8 * rows * GROUP
        ),
        name="attend",
    )(info, queries, *chunks, *chunks, *before)


def pull_kernel(info_ref, q_ref, g_ref, log_ref, *refs):
    keys, values = refs[0:4], refs[4:8]
    dq_ref, own_ref, give_ref = refs[8:11]
    probs_ref, dp_ref, low_ref, ds_ref = refs[11:15]
    pair = pl.program_id(0)
    rows = q_ref.shape[0]
    block = 64
    place, length = info_ref[0], info_ref[1]
    lane = lax.broadcasted_iota(jnp.int32, (1, 128), 1)
    row = lax.broadcasted_iota(jnp.int32, (block, 1), 0)
    factor = SCALE * LOG2E
    query, grad = q_ref[...], g_ref[...]
    nothing = jnp.zeros_like(query)
    owns = [(lane >= head * HEAD) & (lane < head * HEAD + HEAD) for head in range(2)]
    queries = [jnp.where(own, query, nothing) for own in owns]
    grads = [jnp.where(own, grad, nothing) for own in owns]
    for head in range(2):
        for chunk in range(4):
            at = slice(chunk * rows, chunk * rows + rows)
            probs_ref[head, at, :] = contract_cols(keys[chunk][...], queries[head])
            dp_ref[head, at, :] = contract_cols(values[chunk][...], grads[head])
    for head in range(2):
        logged = log_ref[pl.ds(2 * pair + head, 1), :]
        inner = jnp.zeros((8, rows), F32)
        for index in range(4 * rows // block):
            span = slice(index * block, index * block + block)
            chunk, start = divmod(index * block, rows)
            base = (place ^ chunk) * rows + start
            bias = jnp.where(base + row < length, 0.0, NEG).astype(F32)
            probs = jnp.exp2(probs_ref[head, span, :] * factor + (bias - logged))
            probs_ref[head, span, :] = probs
            low_ref[head, span, :] = probs.astype(BF)
            inner += jnp.sum((probs * dp_ref[head, span, :]).reshape(block // 8, 8, rows), axis=0)
        inner = jnp.sum(inner, axis=0, keepdims=True)
        for index in range(4 * rows // block):
            span = slice(index * block, index * block + block)
            ds_ref[head, span, :] = (
                probs_ref[head, span, :] * (dp_ref[head, span, :] - inner)
            ).astype(BF)
    dq = jnp.zeros((128, rows), F32)
    for chunk in range(4):
        slot, out = 2 * (chunk // 2), (own_ref, give_ref)[chunk % 2]
        at = slice(chunk * rows, chunk * rows + rows)
        dk = jnp.dot(ds_ref[0, at, :], queries[0], preferred_element_type=F32)
        dk += jnp.dot(ds_ref[1, at, :], queries[1], preferred_element_type=F32)
        dv = jnp.dot(low_ref[0, at, :], grads[0], preferred_element_type=F32)
        dv += jnp.dot(low_ref[1, at, :], grads[1], preferred_element_type=F32)
        out[slot, :, :] = dk.astype(out.dtype)
        out[slot + 1, :, :] = dv.astype(out.dtype)
        key = keys[chunk][...]
        for head in range(2):
            dq += contract_rows(jnp.where(owns[head], key, nothing), ds_ref[head, at, :])
    dq_ref[...] = jnp.transpose(dq)


def pull(info, queries, grads, logs, chunks, part):
    rows = queries.shape[0]
    own = pl.BlockSpec((rows, 128), lambda p: (0, part * GROUP + p))
    stacked = pl.BlockSpec((4, rows, 128), lambda p: (0, 0, p))
    return pl.pallas_call(
        pull_kernel,
        out_shape=[
            jax.ShapeDtypeStruct((rows, WIDE), F32),
            jax.ShapeDtypeStruct((4, rows, WIDE), F32),
            jax.ShapeDtypeStruct((4, rows, WIDE), BF),
        ],
        grid=(GROUP,),
        in_specs=[
            pl.BlockSpec(memory_space=pltpu.SMEM),
            own,
            own,
            pl.BlockSpec((8, rows), lambda p: (0, 0)),
        ]
        + [pl.BlockSpec((rows, 128), lambda p: (0, p))] * 4
        + [pl.BlockSpec((rows, 128), lambda p: (0, GROUP + p))] * 4,
        out_specs=[pl.BlockSpec((rows, 128), lambda p: (0, p)), stacked, stacked],
        scratch_shapes=[
            pltpu.VMEM((2, 4 * rows, rows), F32),
            pltpu.VMEM((2, 4 * rows, rows), F32),
            pltpu.VMEM((2, 4 * rows, rows), BF),
            pltpu.VMEM((2, 4 * rows, rows), BF),
        ],
        cost_estimate=cost(
            10 * rows * 4 * rows * WIDE, 2 * rows * 24 * WIDE, rows * 4 * rows * 2 * GROUP
        ),
        name="pull",
    )(info, queries, grads, logs, *chunks, *chunks)


def unturn_kernel(halves, *refs):
    cos_ref, first_ref, second_ref, out_ref = refs[4 * halves :]
    wide, first, second = cos_ref[...], -first_ref[...], -second_ref[...]
    column = 0
    for half in range(halves):
        dq_ref, own_ref, near_ref, far_ref = refs[4 * half : 4 * half + 4]
        width = dq_ref.shape[1]
        for part in range(width // 128):
            span = slice(part * 128, part * 128 + 128)
            at = column + part * 128
            out_ref[:, at : at + 128] = turn(dq_ref[:, span] * SCALE, wide, first, second).astype(
                BF
            )
            dk = own_ref[0, :, span] + near_ref[0, :, span].astype(F32)
            dk = (dk + far_ref[0, :, span].astype(F32)) * SCALE
            out_ref[:, D + at : D + at + 128] = turn(dk, wide, first, second).astype(BF)
            dv = own_ref[1, :, span] + near_ref[1, :, span].astype(F32)
            dv = dv + far_ref[1, :, span].astype(F32)
            out_ref[:, 2 * D + at : 2 * D + at + 128] = dv.astype(BF)
        column += width


def unturn(parts, tables):
    rows = tables[0].shape[0]
    arrays = [value for part in parts for value in part]
    vmem = pl.BlockSpec(memory_space=pltpu.VMEM)
    return pl.pallas_call(
        functools.partial(unturn_kernel, len(parts)),
        out_shape=jax.ShapeDtypeStruct((rows, 3 * D), BF),
        in_specs=[vmem] * (len(arrays) + 3),
        out_specs=vmem,
        cost_estimate=cost(20 * rows * 3 * D, rows * D * 30),
        name="unturn",
    )(*arrays, *tables)


def piece_bits(order, index):
    picked = dict(zip(order, ((index >> 2) & 1, (index >> 1) & 1, index & 1)))
    return picked["y"], picked["x"], picked["z"]


def rows_kernel(orders, lefts, spots_ref, *refs):
    left_refs = refs[: 2 * lefts]
    right_refs = refs[2 * lefts : 4 * lefts]
    split_orders = len(orders) == 2
    riders = refs[4 * lefts : 4 * lefts + 2] if split_orders else ()
    outs = refs[4 * lefts + len(riders) : -2]
    turned_ref, picked_ref = refs[-2:]
    y, core, x, z = spots_ref[0], spots_ref[1], spots_ref[2], spots_ref[3]
    rows = left_refs[0].shape[0]
    high = D // 16

    def turned(own_ref, other_ref, slot):
        turned_ref[slot, :, 0:rows] = jnp.transpose(own_ref[...])
        turned_ref[slot, :, rows : 2 * rows] = jnp.transpose(other_ref[...])

    def pick(slot, order, place):
        for index in range(8):
            dy, dx, dz = piece_bits(order, index)
            start = (y ^ dy) * (D // 2) + core * (D // 4) + ((x ^ dx) * 2 + (z ^ dz)) * high
            picked_ref[place, index * high : index * high + high, :] = turned_ref[
                slot, pl.ds(pl.multiple_of(start, 16), high), :
            ]

    def multiply(place, own_ref, other_ref, source, block, keep_ref, send_ref):
        columns = pl.ds(pl.multiple_of(source * D, D), D)
        product = jnp.dot(
            picked_ref[place, :, 0:rows], own_ref[:, columns], preferred_element_type=F32
        )
        product += jnp.dot(
            picked_ref[place, :, rows : 2 * rows],
            other_ref[:, columns],
            preferred_element_type=F32,
        )
        span = pl.ds(pl.multiple_of(block * high, 16), high)
        for index in range(4):
            keep_ref[index, span, :] = product[index * high : index * high + high, :]
            send_ref[index, span, :] = product[
                (4 + index) * high : (4 + index) * high + high, :
            ].astype(BF)

    turned(left_refs[0], left_refs[1], 0)
    pick(0, orders[0], 0)
    blocks = right_refs[0].shape[1] // D
    split = 2 if len(orders) == 2 else blocks

    def body(block, carry):
        multiply(0, right_refs[0], right_refs[1], block, block, *outs[:2])
        return carry

    lax.fori_loop(0, split, body, 0)
    if len(orders) == 2:
        for index in range(8):
            dy, dx, dz = piece_bits(orders[0], index)
            entry = ((y ^ dy) * 2 + core) * 4 + (x ^ dx) * 2 + (z ^ dz)
            value = riders[0][entry] + riders[1][entry]
            value = jnp.concatenate([value, jnp.zeros((14, D), F32)], axis=0)
            if index < 4:
                outs[0][index, 2 * high : 2 * high + 16, :] = value
            else:
                outs[1][index - 4, 2 * high : 2 * high + 16, :] = value.astype(BF)
        pick(0, orders[1], 1)
        multiply(1, right_refs[0], right_refs[1], 2, 0, *outs[2:])
    if lefts == 2:
        turned(left_refs[2], left_refs[3], 1)
        pick(1, orders[-1], 2)
        multiply(2, right_refs[2], right_refs[3], 0, 1 if len(orders) == 2 else blocks, *outs[-2:])


def rows_unit(spots, orders, lefts, rights, riders=()):
    rows = lefts[0][0].shape[0]
    arrays = [value for pair in (*lefts, *rights) for value in pair] + list(riders)
    high = D // 4 // len(orders)
    heights = [high + 16, high] if riders else [high] * len(orders)
    vmem = pl.BlockSpec(memory_space=pltpu.VMEM)
    return pl.pallas_call(
        functools.partial(rows_kernel, orders, len(lefts)),
        out_shape=[
            jax.ShapeDtypeStruct((4, tall, D), kind) for tall in heights for kind in (F32, BF)
        ],
        in_specs=[pl.BlockSpec(memory_space=pltpu.SMEM)] + [vmem] * len(arrays),
        out_specs=[vmem] * (2 * len(orders)),
        scratch_shapes=[
            pltpu.VMEM((len(lefts), D, 2 * rows), BF),
            pltpu.VMEM((3 if len(lefts) == 2 else 1, D // 2, 2 * rows), BF),
        ],
        cost_estimate=cost(4 * rows * (D // 2) * 4 * D, rows * D * 20 + 3 * D * D),
        name="rows_unit",
    )(spots, *arrays)


def forward_kernel(orders, spots_ref, n0, n1, u0, u1, a0, a1, d0, d1, *refs):
    turned_ref, picked_ref, tall_ref = refs[-3:]
    keep_ref, send_ref, keep_down, send_down = (refs[:-3] * 2)[:4]
    y, core, x, z = spots_ref[0], spots_ref[1], spots_ref[2], spots_ref[3]
    rows = n0.shape[0]
    high = D // 16
    tall = D // 4
    first = tall if len(orders) == 1 else 0
    turned_ref[:, 0:rows] = jnp.transpose(n0[...])
    turned_ref[:, rows : 2 * rows] = jnp.transpose(n1[...])
    for index in range(8):
        dy, dx, dz = piece_bits(orders[0], index)
        start = (y ^ dy) * (D // 2) + core * (D // 4) + ((x ^ dx) * 2 + (z ^ dz)) * high
        picked_ref[index * high : index * high + high, :] = turned_ref[
            pl.ds(pl.multiple_of(start, 16), high), :
        ]

    def body(block, carry):
        columns = pl.ds(pl.multiple_of(block * D, D), D)
        product = jnp.dot(picked_ref[:, 0:rows], u0[:, columns], preferred_element_type=F32)
        product += jnp.dot(
            picked_ref[:, rows : 2 * rows], u1[:, columns], preferred_element_type=F32
        )
        span = pl.ds(pl.multiple_of(block * high, 16), high)
        for index in range(4):
            keep_ref[index, span, :] = product[index * high : index * high + high, :]
            send_ref[index, span, :] = product[
                (4 + index) * high : (4 + index) * high + high, :
            ].astype(BF)
        return carry

    lax.fori_loop(0, 4, body, 0)
    for dy in range(2):
        columns = pl.ds(pl.multiple_of(((y ^ dy) * 2 + core) * D, D), D)
        tall_ref[dy, :, 0:rows] = jnp.transpose(a0[:, columns])
        tall_ref[dy, :, rows : 2 * rows] = jnp.transpose(a1[:, columns])
        for dx in range(2):
            for dz in range(2):
                start = pl.multiple_of(((x ^ dx) * 2 + (z ^ dz)) * tall, 16)
                left = tall_ref[dy, pl.ds(start, tall), :]
                product = jnp.dot(left[:, 0:rows], d0[...], preferred_element_type=F32)
                product += jnp.dot(left[:, rows : 2 * rows], d1[...], preferred_element_type=F32)
                index = [k for k in range(8) if piece_bits(orders[-1], k) == (dy, dx, dz)][0]
                if index < 4:
                    keep_down[index, first : first + tall, :] = product
                else:
                    send_down[index - 4, first : first + tall, :] = product.astype(BF)


def forward_unit(spots, orders, normed, grad_up, activated, grad_down):
    rows = normed[0].shape[0]
    vmem = pl.BlockSpec(memory_space=pltpu.VMEM)
    return pl.pallas_call(
        functools.partial(forward_kernel, orders),
        out_shape=[
            jax.ShapeDtypeStruct((4, D // 2 // len(orders), D), kind)
            for _ in orders
            for kind in (F32, BF)
        ],
        in_specs=[pl.BlockSpec(memory_space=pltpu.SMEM)] + [vmem] * 8,
        out_specs=[vmem] * (2 * len(orders)),
        scratch_shapes=[
            pltpu.VMEM((D, 2 * rows), BF),
            pltpu.VMEM((D // 2, 2 * rows), BF),
            pltpu.VMEM((2, D, 2 * rows), BF),
        ],
        cost_estimate=cost(8 * rows * (D // 2) * 4 * D, rows * D * 40 + 6 * D * D),
        name="forward_unit",
    )(spots, *normed, *grad_up, *activated, *grad_down)


AXES = {"y": ("fsdp", 2), "x": ("dp", 1), "z": ("dp", 2)}


class Sum:
    def __init__(self, line, unit, order):
        self.line, self.order, self.stage = line, order, 0
        self.keep, send = unit
        self.moving = swap(send, *AXES[order[0]])
        self.far = [1 << k for k in range(2, 20) if (1 << k) < lax.axis_size("dp")]
        self.rest = [name for name in order if name != "y"]

    def step(self):
        got, keep = self.line.enter(self.moving, self.keep)
        line, stage = self.line, self.stage
        self.stage += 1
        if stage < 3:
            half = keep.shape[0] // 2
            if stage < 2:
                self.keep = keep[:half] + got[:half].astype(F32)
                send = (keep[half:] + got[half:].astype(F32)).astype(BF)
                line.leave(self.keep, send)
                self.moving = swap(send, *AXES[self.order[stage + 1]])
                return
            self.keep = (keep + got.astype(F32)).astype(BF)
        elif stage < 3 + len(self.far):
            self.keep = (keep.astype(F32) + got.astype(F32)).astype(BF)
        elif stage == 3 + len(self.far):
            self.keep = jnp.concatenate([keep, got], axis=0)
            line.leave(self.keep)
            self.moving = swap(self.keep, *AXES[self.rest[0]])
            return
        else:
            self.result = (keep, got)
            return
        line.leave(self.keep)
        if stage - 2 < len(self.far):
            self.moving = swap(self.keep, "dp", self.far[stage - 2])
        else:
            self.moving = swap(self.keep, *AXES[self.rest[1]])

    def finish(self):
        while self.stage < 5 + len(self.far):
            self.step()
        return self.result


def emit_kernel(orders, places, count, spots_ref, *refs):
    outs = refs[-count:]
    x, z = spots_ref[2], spots_ref[3]
    high = D // 16
    for number, order in enumerate(orders):
        rest = [name for name in order if name != "y"]
        for outer in range(2):
            piece = refs[2 * number + outer]
            for inner in range(2):
                picked = dict(zip(rest, (outer, inner)))
                which = (x ^ picked["x"]) * 2 + (z ^ picked["z"])
                at = 0
                for slot, block in places[number]:
                    if block == RIDER:
                        outs[slot][which] = piece[inner, at : at + 16, :].astype(F32)[0:2]
                        continue
                    tall = high if block is not None else 4 * high
                    start = pl.multiple_of(which * tall, 16)
                    first = 0 if block is None else block * D
                    outs[slot][0, pl.ds(start, tall), first : first + D] = piece[
                        inner, at : at + tall, :
                    ].astype(F32)
                    at += tall


def emit(spots, sums, orders, places, shapes, layer, before):
    out_shape = [jax.ShapeDtypeStruct((LAYERS,) + shape, F32) for shape in shapes]
    before = list(before) if before is not None else []
    pieces = [piece for pair in sums for piece in pair]
    extra = []
    if any(block == RIDER for place in places for _, block in place):
        out_shape.append(jax.ShapeDtypeStruct((4, 2, D), F32))
        extra.append(pl.BlockSpec((4, 2, D), lambda i, spots: (0, 0, 0)))
    return pl.pallas_call(
        functools.partial(emit_kernel, orders, places, len(out_shape)),
        out_shape=out_shape,
        grid_spec=pltpu.PrefetchScalarGridSpec(
            num_scalar_prefetch=1,
            grid=(1,),
            in_specs=[pl.BlockSpec(memory_space=pltpu.VMEM)] * len(pieces)
            + [pl.BlockSpec(memory_space=pl.ANY)] * len(before),
            out_specs=[
                pl.BlockSpec((1,) + shape, lambda i, spots: (layer, 0, 0)) for shape in shapes
            ]
            + extra,
        ),
        input_output_aliases={1 + len(pieces) + i: i for i in range(len(before))},
        cost_estimate=cost(0, D * D * 6),
        name="emit",
    )(spots, *pieces, *before)


class Line:
    def __init__(self):
        self.last = ()

    def enter(self, *values):
        out = lax.optimization_barrier(tuple(values) + tuple(self.last))
        return out[: len(values)]

    def leave(self, *values):
        self.last = tuple(values)

    def sync(self, *values):
        out = self.enter(*values)
        self.last = tuple(out)
        return out


def after(value, *others):
    return lax.optimization_barrier((value,) + others)[0]


NAMES = (
    "input_bias",
    "output_bias",
    "first_gain",
    "first_shift",
    "up_bias",
    "down_bias",
    "second_gain",
    "second_shift",
)
WIDTHS = (3 * D, D, D, D, 4 * D, D, D, D)


def feed_forward(hidden, context, weights, small, between):
    _, output_weight, up_weight, down_weight = weights
    attn_out = jnp.dot(context, output_weight, preferred_element_type=F32) + small["output_bias"]
    first_in = hidden + attn_out
    normed = layer_norm(first_in, small["first_gain"], small["first_shift"])
    normed_low = between(normed.astype(BF))
    up_value = jnp.dot(normed_low, up_weight, preferred_element_type=F32) + small["up_bias"]
    part = normal_part(up_value)
    activated = (up_value * part).astype(BF)
    slope = gelu_slope(up_value, part)
    down_value = (
        jnp.dot(activated, down_weight, preferred_element_type=F32) + small["down_bias"]
    )
    second_in = normed + down_value
    output = layer_norm(second_in, small["second_gain"], small["second_shift"])
    return output, first_in, normed_low, slope, activated, second_in


def feed_backward(grad_output, weights, small, first_in, slope, second_in):
    _, output_weight, up_weight, down_weight = weights
    pull_second = jax.vjp(layer_norm, second_in, small["second_gain"], small["second_shift"])[1]
    grad_second, grad_second_gain, grad_second_shift = pull_second(grad_output)
    grad_down = grad_second.astype(BF)
    grad_down_bias = jnp.sum(grad_down, axis=0, dtype=F32)
    grad_activated = contract_cols(grad_down, down_weight)
    grad_up = (grad_activated * slope).astype(BF)
    grad_up_bias = jnp.sum(grad_up, axis=0, dtype=F32)
    grad_normed = grad_second + contract_cols(grad_up, up_weight)
    pull_first = jax.vjp(layer_norm, first_in, small["first_gain"], small["first_shift"])[1]
    grad_first, grad_first_gain, grad_first_shift = pull_first(grad_normed)
    grad_attn = grad_first.astype(BF)
    grad_output_bias = jnp.sum(grad_attn, axis=0, dtype=F32)
    grad_context = contract_cols(grad_attn, output_weight).astype(BF)
    little = (
        grad_output_bias,
        grad_first_gain,
        grad_first_shift,
        grad_up_bias,
        grad_down_bias,
        grad_second_gain,
        grad_second_shift,
    )
    return grad_down, grad_up, grad_attn, grad_context, grad_first, little


FORWARD_ORDER = (("xzy", "zxy"), ("xzy",))
JOINT_ORDER = (("xzy", "yxz"), ("xzy",))


def on_device(
    tokens,
    cotangent,
    lengths,
    input_weight,
    input_bias,
    output_weight,
    output_bias,
    first_gain,
    first_shift,
    up_weight,
    up_bias,
    down_weight,
    down_bias,
    second_gain,
    second_shift,
):
    place = lax.axis_index("fsdp")
    group = lax.axis_index("dp")
    core = place & 1
    x_bit, z_bit = group & 1, (group >> 1) & 1
    spots = jnp.stack([place >> 1, core, x_bit, z_bit]).astype(jnp.int32)
    row_count = tokens.shape[0]
    places = place * row_count + jnp.arange(row_count, dtype=jnp.int32)
    length = lengths[0]
    info = jnp.stack([place, length]).astype(jnp.int32)
    row_valid = (places < length).astype(F32)

    swap_core = lambda value: swap(value, "fsdp", 1)
    swap_y = lambda value: swap(value, "fsdp", 2)
    swap_x = lambda value: swap(value, "dp", 1)
    swap_z = lambda value: swap(value, "dp", 2)

    rows_of = D // 4
    quarter = rows_of // 4
    start = (x_bit * 2 + z_bit) * quarter
    quarters = [
        x_bit * 2 + z_bit,
        x_bit * 2 + (1 - z_bit),
        (1 - x_bit) * 2 + z_bit,
        (1 - x_bit) * 2 + (1 - z_bit),
    ]
    spread_spots = jnp.stack(
        [place * rows_of, (place ^ 1) * rows_of]
        + [(place ^ 2) * rows_of + q * quarter for q in quarters]
        + [(place ^ 3) * rows_of + q * quarter for q in quarters]
    ).astype(jnp.int32)
    direct_spots = jnp.stack([(place ^ k) * rows_of for k in range(4)]).astype(jnp.int32)
    rest_spec = (("rows", D), ("rows", 4 * D), ("split", 4 * D))

    def wide(i):
        split = [down_weight[i, k * 192 : k * 192 + 192] for k in range(4)]
        return jnp.concatenate([output_weight[i], up_weight[i]] + split, axis=1)

    line = Line()

    input_one, input_two = input_weight[0], input_weight[1]
    over_y = swap_y(input_one)
    packed = jnp.concatenate(
        (
            input_bias,
            output_bias,
            first_gain,
            first_shift,
            up_bias,
            down_bias,
            second_gain,
            second_shift,
        ),
        axis=1,
    )
    packed_y, packed_c, input_c = swap_y(packed), swap_core(packed), swap_core(input_one)
    tables = rotary_tables(places.astype(F32))
    rests = (wide(0), wide(1))
    mine = [lax.dynamic_slice(r, (start, 0), (quarter, r.shape[1])) for r in rests]
    line.leave(*mine, *tables, spread_spots, direct_spots, info, spots)
    over_y, packed_y, packed_c, input_c = line.sync(over_y, packed_y, packed_c, input_c)
    spread_y = swap_y(after(mine[0], over_y))
    rest_c = swap_core(after(rests[0], over_y))
    packed_yc, input_yc = swap_core(packed_y), swap_core(over_y)
    fields = unpack(info, [packed, packed_c, packed_y, packed_yc], WIDTHS)
    smalls = [
        dict(zip(NAMES, fields[i * len(NAMES) : (i + 1) * len(NAMES)])) for i in range(LAYERS)
    ]
    pieces = [input_one, input_c, over_y, input_yc]
    line.leave(*fields)
    hidden, rounded = tokens.astype(F32), tokens
    kept, weights = [], []
    for i in range(LAYERS):
        more = i + 1 < LAYERS
        small = smalls[i]
        pieces = line.enter(*pieces)
        queries, *kvs, whole = project(
            rounded, pieces, direct_spots, small["input_bias"], tables
        )
        line.leave(queries, *kvs, whole)
        kv_y, kv_c = [swap_y(kv) for kv in kvs], [swap_core(kv) for kv in kvs]
        if i == 0:
            spread_y, rest_c = line.sync(spread_y, rest_c)
            spread_z, spread_x = swap_z(spread_y), swap_x(spread_y)
        else:
            (rest_c,) = line.sync(rest_c)
            saved = [kept[0][8], kept[0][6], kept[0][4], rounded]
            shared = line.sync(*[swap_core(v) for v in saved[:2]])
            shared += line.sync(*[swap_core(v) for v in saved[2:]])
            act1, normed1, context1, rounded2 = list(zip(saved, shared))
        chunks, logs = [], []
        context, rest = None, None
        for part in range(PARTS):
            if part == 1:
                spread_z, spread_x = line.sync(spread_z, spread_x)
                spread_xz = swap_x(spread_z)
                crossed = [swap_core(v) for v in (spread_y, spread_z, spread_x)]
            if part == 2:
                crossed = list(line.sync(*crossed))
            got_y, got_c = line.sync(kv_y[part], kv_c[part])
            (got_yc,) = line.sync(swap_core(got_y))
            if more and part == PARTS - 1:
                over_y, input_c = swap_y(after(input_two, got_yc)), swap_core(after(input_two, got_yc))
                next_y = swap_y(after(mine[1], got_yc))
            chunks.append([kvs[part], got_c, got_y, got_yc])
            (query_in,) = line.enter(queries)
            context, log = attend(info, query_in, chunks[-1], part, context)
            line.leave(context, log)
            logs.append(log)
        (spread_xz,) = line.sync(spread_xz)
        crossed.append(swap_core(spread_xz))
        crossed[3:] = line.sync(*crossed[3:])
        pieces = [rests[i], rest_c, spread_y, spread_z, spread_x, spread_xz, *crossed]
        pieces = line.enter(*pieces)
        rest = assemble(pieces, spread_spots, rest_spec)
        weights.append((whole, *rest))
        line.leave(*rest)
        if more:
            over_y, input_c = line.sync(over_y, input_c)
            input_yc = swap_core(over_y)
            rest_c = swap_core(after(rests[1], over_y))
        moving = []

        def between(value):
            if not more:
                return value
            line.leave(value)
            (arrived,) = line.sync(next_y)
            moving.extend((arrived, swap_z(arrived), swap_x(arrived)))
            return line.enter(value)[0]

        (context_in,) = line.enter(context)
        output, first_in, normed, slope, activated, second_in = feed_forward(
            hidden, context_in, weights[i], small, between
        )
        kept.append(
            (rounded, queries, chunks, logs, context, first_in, normed, slope, activated, second_in)
        )
        hidden, rounded = output, output.astype(BF)
        line.leave(hidden, rounded)
        if more:
            spread_y, spread_z, spread_x = moving
            pieces = [input_two, input_c, over_y, input_yc]
    result = rounded

    def both_cores(*values):
        values = line.enter(*values)
        return [(value, swap_core(value)) for value in values]

    def feed_back(grad_output, i):
        (grad_output,) = line.enter(grad_output)
        _, _, _, _, _, first_in, _, slope, _, second_in = kept[i]
        out = feed_backward(grad_output, weights[i], smalls[i], first_in, slope, second_in)
        line.leave(*out[:5])
        return out

    def attention_back(i, grad_context, part):
        queries, chunks, logs = kept[i][1:4]
        (grad_context,) = line.enter(grad_context)
        dq, own, give = pull(info, queries, grad_context, logs[part], chunks[part], part)
        line.leave(dq, own, give)
        return dq, own, swap_core(give)

    def far_back(pulled):
        dq, own, near = pulled
        own, near = line.enter(own, near)
        far = (own[2:] + near[2:].astype(F32)).astype(BF)
        line.leave(far)
        return dq, own, near, swap_y(far)

    def arrive(far):
        dq, own, near, moving = far
        (moving,) = line.sync(moving)
        return dq, own, near, moving

    def forward_sum(i, normed, grad_up, activated, grad_down):
        pairs = (normed, grad_up, activated, grad_down)
        got = line.enter(*[pair[1] for pair in pairs])
        unit = forward_unit(
            spots, FORWARD_ORDER[i], *[(pair[0], g) for pair, g in zip(pairs, got)]
        )
        line.leave(*unit)
        return [
            Sum(line, unit[2 * k : 2 * k + 2], order) for k, order in enumerate(FORWARD_ORDER[i])
        ]

    def joint_sum(i, rounded, grad_joint, context, grad_attn, riders=()):
        got = line.enter(rounded[1], grad_joint[1], context[1], grad_attn[1])
        pairs = [(p[0], g) for p, g in zip((rounded, grad_joint, context, grad_attn), got)]
        unit = rows_unit(
            spots, JOINT_ORDER[i], [pairs[0], pairs[2]], [pairs[1], pairs[3]], riders
        )
        line.leave(*unit)
        return [
            Sum(line, unit[2 * k : 2 * k + 2], order) for k, order in enumerate(JOINT_ORDER[i])
        ]

    def joint_back(i, parts, grad_first):
        flat = line.enter(*[v for part in parts for v in part])
        parts = [flat[4 * k : 4 * k + 4] for k in range(len(parts))]
        grad_joint = unturn(parts, tables)
        line.leave(grad_joint)
        grad_hidden = grad_first + contract_cols(grad_joint, weights[i][0])
        return grad_joint, jnp.sum(grad_joint, axis=0, dtype=F32), grad_hidden

    grad_hidden = cotangent.astype(F32) * row_valid[:, None]
    act2, normed2 = both_cores(kept[1][8], kept[1][6])
    dd2, du2, da2, dc2, grad_first2, little2 = feed_back(grad_hidden, 1)

    def retire(*pairs):
        got = line.sync(*[pair[1] for pair in pairs])
        return [(pair[0], value) for pair, value in zip(pairs, got)]

    act2, normed2 = retire(act2, normed2)
    dd2, du2 = both_cores(dd2, du2)
    p0 = attention_back(1, dc2, 0)
    dd2, du2 = retire(dd2, du2)
    context2, da2 = both_cores(kept[1][4], da2)
    p1 = attention_back(1, dc2, 1)
    context2, da2 = retire(context2, da2)
    p0 = far_back(p0)
    p2 = attention_back(1, dc2, 2)
    p0 = arrive(p0)
    p1 = far_back(p1)
    (f2,) = forward_sum(1, normed2, du2, act2, dd2)
    p1 = arrive(p1)
    p2 = far_back(p2)
    p2 = arrive(p2)
    joint2, bias2, grad_hidden = joint_back(1, (p0, p1, p2), grad_first2)
    (joint2,) = both_cores(joint2)
    dd1, du1, da1, dc1, grad_first1, little1 = feed_back(grad_hidden, 0)
    (joint2,) = retire(joint2)
    f2.step()
    dd1, du1 = both_cores(dd1, du1)
    (j2,) = joint_sum(1, rounded2, joint2, context2, da2)
    dd1, du1 = retire(dd1, du1)
    u1, d1 = forward_sum(0, normed1, du1, act1, dd1)
    f2.step()
    rounded1, da1 = both_cores(kept[0][0], da1)
    p0 = attention_back(0, dc1, 0)
    rounded1, da1 = retire(rounded1, da1)
    j2.step()
    f2.step()
    p1 = attention_back(0, dc1, 1)
    p0 = far_back(p0)
    d1.step()
    u1.step()
    p2 = attention_back(0, dc1, 2)
    p0 = arrive(p0)
    p1 = far_back(p1)
    f2.step()
    j2.step()
    u1.step()
    p1 = arrive(p1)
    p2 = far_back(p2)
    d1.step()
    j2.step()
    f2.step()
    shape_forward = [(D // 4, 4 * D), (D, D)]
    shape_joint = [(D // 4, 3 * D), (D // 4, D)]
    up_places, down_places = [(0, 0), (0, 1), (0, 2), (0, 3)], [(1, None)]

    def write(chains, orders, places, shapes, layer, before):
        sums = [chain.finish() for chain in chains]
        out = emit(spots, sums, orders, places, shapes, layer, before)
        line.leave(*out)
        return out

    p2 = arrive(p2)
    joint1, bias1, grad_hidden = joint_back(0, (p0, p1, p2), grad_first1)
    (joint1,) = both_cores(joint1)
    packed = pack(
        [part.reshape(-1) for layer in ((bias1, *little1), (bias2, *little2)) for part in layer]
    )
    line.leave(packed)
    packed_pair = both_cores(packed)
    u1.step()
    d1.step()
    joint1, packed_pair = retire(joint1, *packed_pair)
    j1 = joint_sum(0, rounded1, joint1, context1, da1, packed_pair)
    u1.step()
    d1.step()
    j2.step()
    out_forward = write(
        [f2], FORWARD_ORDER[1], ([*up_places, *down_places],), shape_forward, 1, None
    )
    (grad_hidden,) = line.sync(grad_hidden)
    j1[0].step()
    j1[1].step()
    j2.step()
    u1.step()
    d1.step()
    j1[0].step()
    j1[1].step()
    out_joint = write(
        [j2],
        JOINT_ORDER[1],
        ([(0, 0), (0, 1), (0, 2), (1, 0)],),
        shape_joint,
        1,
        None,
    )
    j1[0].step()
    j1[1].step()
    j1[0].step()
    j1[1].step()
    j1[0].step()
    j1[1].step()
    out_forward = write(
        [u1, d1], FORWARD_ORDER[0], (up_places, down_places), shape_forward, 0, out_forward
    )
    *out_joint, flat = write(
        j1,
        JOINT_ORDER[0],
        ([(0, 0), (0, 1), (2, RIDER)], [(0, 2), (1, 0)]),
        shape_joint,
        0,
        out_joint,
    )
    flat = spread(flat, WIDTHS)

    small_grads = dict(zip(NAMES, flat))
    return (
        result,
        grad_hidden,
        out_joint[0],
        small_grads["input_bias"],
        out_joint[1],
        small_grads["output_bias"],
        small_grads["first_gain"],
        small_grads["first_shift"],
        out_forward[0],
        small_grads["up_bias"],
        out_forward[1],
        small_grads["down_bias"],
        small_grads["second_gain"],
        small_grads["second_shift"],
    )


def solution(mesh):
    rows = P(("dp", "fsdp"), None)
    matrix = P(None, "fsdp", None)
    vector = P(None, "fsdp")
    parameters = (
        matrix,
        vector,
        matrix,
        vector,
        vector,
        vector,
        matrix,
        vector,
        matrix,
        vector,
        vector,
        vector,
    )
    return jax.shard_map(
        on_device,
        mesh=mesh,
        in_specs=(rows, rows, P("dp"), *parameters),
        out_specs=(rows, rows, *parameters),
        check_vma=False,
    )
```

```python
import functools

import jax
import jax.numpy as jnp
from jax import lax
from jax.experimental import pallas as pl
from jax.experimental.pallas import tpu as pltpu
from jax.sharding import PartitionSpec as P

D = 768
HEADS = 12
HEAD = 64
PAIRS = HEADS // 2
LAYERS = 2
RIDER = -1
PARTS = 3
GROUP = PAIRS // PARTS
WIDE = GROUP * 128
LOG2E = 1.4426950408889634
SCALE = HEAD ** (-0.5)
NEG = -1e30
BF = jnp.bfloat16
F32 = jnp.float32

norm_eps = 1e-12


def swap(value, axis, bit):
    count = lax.axis_size(axis)
    return lax.ppermute(value, axis, [(i, i ^ bit) for i in range(count)])


def layer_norm(matrix, norm_gain, norm_shift):
    row_mean = jnp.mean(matrix, axis=-1, keepdims=True)
    centred = matrix - row_mean
    spread = jnp.mean(centred * centred, axis=-1, keepdims=True)
    return centred * lax.rsqrt(spread + norm_eps) * norm_gain + norm_shift


def normal_part(value):
    return 0.5 + 0.5 * lax.erf(value * 0.7071067811865476)


def gelu_slope(value, part):
    return part + value * jnp.exp(-0.5 * value * value) * 0.3989422804014327


def contract_rows(left_side, right_side):
    return lax.dot_general(
        left_side, right_side, (((0,), (0,)), ((), ())), preferred_element_type=F32
    )


def contract_cols(left_side, right_side):
    return lax.dot_general(
        left_side, right_side, (((1,), (1,)), ((), ())), preferred_element_type=F32
    )


def cost(flops, bytes_accessed, transcendentals=0):
    return pl.CostEstimate(
        flops=int(flops), bytes_accessed=int(bytes_accessed), transcendentals=int(transcendentals)
    )


def rotary_tables(places):
    frequency = 10000.0 ** (-2.0 * jnp.arange(HEAD // 2, dtype=F32) / HEAD)
    angles = places[:, None] * frequency[None, :]
    cosine, sine = jnp.cos(angles), jnp.sin(angles)
    nothing = jnp.zeros_like(sine)
    wide = jnp.concatenate([cosine] * 4, axis=1)
    first = jnp.concatenate([-sine, nothing] * 2, axis=1)
    second = jnp.concatenate([nothing, sine] * 2, axis=1)
    return wide, first, second


def turn(block, wide, first, second):
    return (
        block * wide
        + pltpu.roll(block, 96, 1) * first
        + pltpu.roll(block, 32, 1) * second
    )


def assemble_kernel(spec, count, pos_ref, *refs):
    pieces = refs[:count]
    outs = refs[count : count + len(spec)]
    held, in_sem, out_sem = refs[count + len(spec) :]
    copies = []
    for index, piece in enumerate(pieces):
        rows = piece.shape[0]
        start = pl.multiple_of(pos_ref[index], 16)
        copies.append(
            pltpu.make_async_copy(piece, held.at[pl.ds(start, rows), :], in_sem.at[index])
        )
    for copy in copies:
        copy.start()
    for copy in copies:
        copy.wait()
    copies = []
    column = 0
    for slot, (kind, width) in enumerate(spec):
        if kind == "rows":
            copies.append((held.at[:, pl.ds(column, width)], outs[slot]))
        else:
            shard = held.shape[0] // 4
            for source in range(4):
                for part in range(width // D):
                    copies.append(
                        (
                            held.at[pl.ds(source * shard, shard), pl.ds(column + part * D, D)],
                            outs[slot].at[pl.ds(source * 4 * shard + part * shard, shard), :],
                        )
                    )
        column += width
    copies = [
        pltpu.make_async_copy(src, dst, out_sem.at[index])
        for index, (src, dst) in enumerate(copies)
    ]
    for copy in copies:
        copy.start()
    for copy in copies:
        copy.wait()


def assemble(pieces, positions, spec):
    width = pieces[0].shape[1]
    out_shape = []
    outputs = 0
    for kind, columns in spec:
        if kind == "rows":
            out_shape.append(jax.ShapeDtypeStruct((D, columns), BF))
            outputs += 1
        else:
            out_shape.append(jax.ShapeDtypeStruct((columns, D), BF))
            outputs += 4 * (columns // D)
    return pl.pallas_call(
        functools.partial(assemble_kernel, spec, len(pieces)),
        out_shape=out_shape,
        in_specs=[pl.BlockSpec(memory_space=pltpu.SMEM)]
        + [pl.BlockSpec(memory_space=pl.ANY)] * len(pieces),
        out_specs=[pl.BlockSpec(memory_space=pl.ANY)] * len(spec),
        scratch_shapes=[
            pltpu.VMEM((D, width), BF),
            pltpu.SemaphoreType.DMA((len(pieces),)),
            pltpu.SemaphoreType.DMA((outputs,)),
        ],
        cost_estimate=cost(0, 4 * D * width),
        name="assemble",
    )(positions, *pieces)


def pack_kernel(*refs):
    *parts, out_ref, flat_ref = refs
    offset = 0
    flat_ref[...] = jnp.zeros_like(flat_ref)
    for part in parts:
        width = part.shape[0] // 4
        values = part[...].reshape(1, 4 * width)
        for owner in range(4):
            flat_ref[owner : owner + 1, offset : offset + width] = values[
                :, owner * width : owner * width + width
            ]
        offset += width
    for owner in range(4):
        for row in range(8):
            out_ref[4 * owner + row // 2, row % 2 : row % 2 + 1, :] = flat_ref[
                owner : owner + 1, row * D : row * D + D
            ]


def spread_kernel(count, rows_ref, *refs):
    *outs, flat_ref = refs
    for row in range(8):
        flat_ref[:, row * D : row * D + D] = rows_ref[row // 2, row % 2 : row % 2 + 1, :]
    offset = 0
    for layer in range(LAYERS):
        for slot in range(count):
            width = outs[slot].shape[1]
            outs[slot][layer : layer + 1, :] = flat_ref[:, offset : offset + width]
            offset += width


def pack(parts):
    vmem = pl.BlockSpec(memory_space=pltpu.VMEM)
    return pl.pallas_call(
        pack_kernel,
        out_shape=jax.ShapeDtypeStruct((16, 2, D), F32),
        in_specs=[vmem] * len(parts),
        out_specs=vmem,
        scratch_shapes=[pltpu.VMEM((4, 8 * D), F32)],
        cost_estimate=cost(0, 200000),
        name="pack",
    )(*parts)


def spread(rows, widths):
    vmem = pl.BlockSpec(memory_space=pltpu.VMEM)
    return pl.pallas_call(
        functools.partial(spread_kernel, len(widths)),
        out_shape=[jax.ShapeDtypeStruct((LAYERS, width // 4), F32) for width in widths],
        in_specs=[vmem],
        out_specs=[vmem] * len(widths),
        scratch_shapes=[pltpu.VMEM((1, 8 * D), F32)],
        cost_estimate=cost(0, 50000),
        name="spread",
    )(rows)


def project_kernel(count, pos_ref, h_ref, b_ref, cos_ref, first_ref, second_ref, *refs):
    pieces = refs[:count]
    q_ref, *kv_refs, whole_ref, held, in_sem, out_sem = refs[count:]
    copies = []
    for part in range(3):
        for index, piece in enumerate(pieces):
            rows = piece.shape[0]
            start = pl.multiple_of(pos_ref[index], 16)
            copies.append(
                pltpu.make_async_copy(
                    piece.at[:, pl.ds(part * D, D)],
                    held.at[part, pl.ds(start, rows), :],
                    in_sem.at[part * count + index],
                )
            )
    for copy in copies:
        copy.start()
    outs = [
        pltpu.make_async_copy(
            held.at[part], whole_ref.at[:, pl.ds(part * D, D)], out_sem.at[part]
        )
        for part in range(3)
    ]
    for part in range(3):
        for copy in copies[part * count : part * count + count]:
            copy.wait()
        outs[part].start()
        joint = jnp.dot(h_ref[...], held[part], preferred_element_type=F32)
        joint = joint + b_ref[:, part * D : part * D + D]
        if part == 2:
            for index in range(PARTS):
                kv_refs[index][:, WIDE:] = joint[:, index * WIDE : index * WIDE + WIDE].astype(BF)
            continue
        for pair in range(PAIRS):
            span = slice(pair * 128, pair * 128 + 128)
            turned = turn(joint[:, span], cos_ref[...], first_ref[...], second_ref[...]).astype(BF)
            if part == 0:
                q_ref[:, span] = turned
            else:
                at = pair % GROUP * 128
                kv_refs[pair // GROUP][:, at : at + 128] = turned
    for copy in outs:
        copy.wait()


def project(rounded, pieces, positions, bias, tables):
    rows = rounded.shape[0]
    count = len(pieces)
    return pl.pallas_call(
        functools.partial(project_kernel, count),
        out_shape=[
            jax.ShapeDtypeStruct((rows, D), BF),
            *[jax.ShapeDtypeStruct((rows, 2 * WIDE), BF)] * PARTS,
            jax.ShapeDtypeStruct((D, 3 * D), BF),
        ],
        in_specs=[pl.BlockSpec(memory_space=pltpu.SMEM)]
        + [pl.BlockSpec(memory_space=pltpu.VMEM)] * 5
        + [pl.BlockSpec(memory_space=pl.ANY)] * count,
        out_specs=[pl.BlockSpec(memory_space=pltpu.VMEM)] * (1 + PARTS)
        + [pl.BlockSpec(memory_space=pl.ANY)],
        scratch_shapes=[
            pltpu.VMEM((3, D, D), BF),
            pltpu.SemaphoreType.DMA((3 * count,)),
            pltpu.SemaphoreType.DMA((3,)),
        ],
        cost_estimate=cost(2 * rows * D * 3 * D, 2 * (rows * 4 * D + 3 * D * D)),
        name="project",
    )(positions, rounded, bias, *tables, *pieces)


def unpack_kernel(widths, place_ref, *refs):
    pieces, outs, held = refs[:4], refs[4:-1], refs[-1]
    place = place_ref[0]
    for index in range(4):
        held[index] = pieces[index][...].astype(F32)
    for source in range(4):
        shard = held[source ^ place]
        offset = 0
        for slot, width in enumerate(widths):
            part = width // 4
            for layer in range(LAYERS):
                outs[layer * len(widths) + slot][:, source * part : source * part + part] = shard[
                    layer : layer + 1, offset : offset + part
                ]
            offset += part


def unpack(info, pieces, widths):
    vmem = pl.BlockSpec(memory_space=pltpu.VMEM)
    return pl.pallas_call(
        functools.partial(unpack_kernel, widths),
        out_shape=[jax.ShapeDtypeStruct((1, width), F32) for width in widths] * LAYERS,
        in_specs=[pl.BlockSpec(memory_space=pltpu.SMEM)] + [vmem] * 4,
        out_specs=[vmem] * (LAYERS * len(widths)),
        scratch_shapes=[pltpu.VMEM((4,) + pieces[0].shape, F32)],
        cost_estimate=cost(0, 100000),
        name="unpack",
    )(info, *pieces)


def attend_kernel(part, info_ref, q_ref, *refs):
    keys, values = refs[0:4], refs[4:8]
    out_ref, log_ref, column_ref, score_ref, prob_ref = refs[-5:]
    pair = pl.program_id(0)
    rows = q_ref.shape[0]
    place, length = info_ref[0], info_ref[1]
    lane = lax.broadcasted_iota(jnp.int32, (1, 128), 1)
    key_lane = lax.broadcasted_iota(jnp.int32, (1, rows), 1)
    bias = jnp.concatenate(
        [
            jnp.where((place ^ k) * rows + key_lane < length, 0.0, NEG).astype(F32)
            for k in range(4)
        ],
        axis=1,
    )
    factor = SCALE * LOG2E
    block = 32
    query = q_ref[...]
    owns = [(lane >= head * HEAD) & (lane < head * HEAD + HEAD) for head in range(2)]
    for head in range(2):
        masked = jnp.where(owns[head], query, jnp.zeros_like(query))
        for k in range(4):
            score_ref[head, :, k * rows : (k + 1) * rows] = contract_cols(masked, keys[k][...])
    for head in range(2):
        for index in range(rows // block):
            span = slice(index * block, index * block + block)
            scores = score_ref[head, span, :] + bias
            peak = jnp.max(scores, axis=1, keepdims=True)
            powers = jnp.exp2((scores - peak) * factor)
            total = jnp.sum(powers, axis=1, keepdims=True)
            prob_ref[head, span, :] = (powers * (1.0 / total)).astype(BF)
            column_ref[span, :] = jnp.where(
                lane == 2 * pair + head, peak * factor + jnp.log2(total), column_ref[span, :]
            )
    outs = []
    for head in range(2):
        gathered = jnp.dot(prob_ref[head, :, 0:rows], values[0][...], preferred_element_type=F32)
        for k in range(1, 4):
            gathered += jnp.dot(
                prob_ref[head, :, k * rows : (k + 1) * rows],
                values[k][...],
                preferred_element_type=F32,
            )
        outs.append(gathered)
    out_ref[...] = jnp.where(owns[0], outs[0], outs[1]).astype(BF)

    @pl.when(pair == GROUP - 1)
    def _():
        log_ref[...] = jnp.transpose(column_ref[...])[0:8, :]


def attend(info, queries, chunks, part, before):
    rows = queries.shape[0]
    own = pl.BlockSpec((rows, 128), lambda p: (0, part * GROUP + p))
    before = [] if before is None else [before]
    return pl.pallas_call(
        functools.partial(attend_kernel, part),
        out_shape=[
            jax.ShapeDtypeStruct((rows, D), BF),
            jax.ShapeDtypeStruct((8, rows), F32),
        ],
        grid=(GROUP,),
        in_specs=[pl.BlockSpec(memory_space=pltpu.SMEM), own]
        + [pl.BlockSpec((rows, 128), lambda p: (0, p))] * 4
        + [pl.BlockSpec((rows, 128), lambda p: (0, GROUP + p))] * 4
        + [pl.BlockSpec(memory_space=pl.ANY)] * len(before),
        out_specs=[own, pl.BlockSpec((8, rows), lambda p: (0, 0))],
        scratch_shapes=[
            pltpu.VMEM((rows, 128), F32),
            pltpu.VMEM((2, rows, 4 * rows), F32),
            pltpu.VMEM((2, rows, 4 * rows), BF),
        ],
        input_output_aliases={10: 0} if before else {},
        cost_estimate=cost(
            4 * rows * 4 * rows * WIDE, 2 * rows * 10 * WIDE, rows * 8 * rows * GROUP
        ),
        name="attend",
    )(info, queries, *chunks, *chunks, *before)


def pull_kernel(info_ref, q_ref, g_ref, log_ref, *refs):
    keys, values = refs[0:4], refs[4:8]
    dq_ref, own_ref, give_ref = refs[8:11]
    probs_ref, dp_ref, low_ref, ds_ref = refs[11:15]
    pair = pl.program_id(0)
    rows = q_ref.shape[0]
    block = 64
    place, length = info_ref[0], info_ref[1]
    lane = lax.broadcasted_iota(jnp.int32, (1, 128), 1)
    row = lax.broadcasted_iota(jnp.int32, (block, 1), 0)
    factor = SCALE * LOG2E
    query, grad = q_ref[...], g_ref[...]
    nothing = jnp.zeros_like(query)
    owns = [(lane >= head * HEAD) & (lane < head * HEAD + HEAD) for head in range(2)]
    queries = [jnp.where(own, query, nothing) for own in owns]
    grads = [jnp.where(own, grad, nothing) for own in owns]
    for head in range(2):
        for chunk in range(4):
            at = slice(chunk * rows, chunk * rows + rows)
            probs_ref[head, at, :] = contract_cols(keys[chunk][...], queries[head])
            dp_ref[head, at, :] = contract_cols(values[chunk][...], grads[head])
    for head in range(2):
        logged = log_ref[pl.ds(2 * pair + head, 1), :]
        inner = jnp.zeros((8, rows), F32)
        for index in range(4 * rows // block):
            span = slice(index * block, index * block + block)
            chunk, start = divmod(index * block, rows)
            base = (place ^ chunk) * rows + start
            bias = jnp.where(base + row < length, 0.0, NEG).astype(F32)
            probs = jnp.exp2(probs_ref[head, span, :] * factor + (bias - logged))
            probs_ref[head, span, :] = probs
            low_ref[head, span, :] = probs.astype(BF)
            inner += jnp.sum((probs * dp_ref[head, span, :]).reshape(block // 8, 8, rows), axis=0)
        inner = jnp.sum(inner, axis=0, keepdims=True)
        for index in range(4 * rows // block):
            span = slice(index * block, index * block + block)
            ds_ref[head, span, :] = (
                probs_ref[head, span, :] * (dp_ref[head, span, :] - inner)
            ).astype(BF)
    dq = jnp.zeros((128, rows), F32)
    for chunk in range(4):
        slot, out = 2 * (chunk // 2), (own_ref, give_ref)[chunk % 2]
        at = slice(chunk * rows, chunk * rows + rows)
        dk = jnp.dot(ds_ref[0, at, :], queries[0], preferred_element_type=F32)
        dk += jnp.dot(ds_ref[1, at, :], queries[1], preferred_element_type=F32)
        dv = jnp.dot(low_ref[0, at, :], grads[0], preferred_element_type=F32)
        dv += jnp.dot(low_ref[1, at, :], grads[1], preferred_element_type=F32)
        out[slot, :, :] = dk.astype(out.dtype)
        out[slot + 1, :, :] = dv.astype(out.dtype)
        key = keys[chunk][...]
        for head in range(2):
            dq += contract_rows(jnp.where(owns[head], key, nothing), ds_ref[head, at, :])
    dq_ref[...] = jnp.transpose(dq)


def pull(info, queries, grads, logs, chunks, part):
    rows = queries.shape[0]
    own = pl.BlockSpec((rows, 128), lambda p: (0, part * GROUP + p))
    stacked = pl.BlockSpec((4, rows, 128), lambda p: (0, 0, p))
    return pl.pallas_call(
        pull_kernel,
        out_shape=[
            jax.ShapeDtypeStruct((rows, WIDE), F32),
            jax.ShapeDtypeStruct((4, rows, WIDE), F32),
            jax.ShapeDtypeStruct((4, rows, WIDE), BF),
        ],
        grid=(GROUP,),
        in_specs=[
            pl.BlockSpec(memory_space=pltpu.SMEM),
            own,
            own,
            pl.BlockSpec((8, rows), lambda p: (0, 0)),
        ]
        + [pl.BlockSpec((rows, 128), lambda p: (0, p))] * 4
        + [pl.BlockSpec((rows, 128), lambda p: (0, GROUP + p))] * 4,
        out_specs=[pl.BlockSpec((rows, 128), lambda p: (0, p)), stacked, stacked],
        scratch_shapes=[
            pltpu.VMEM((2, 4 * rows, rows), F32),
            pltpu.VMEM((2, 4 * rows, rows), F32),
            pltpu.VMEM((2, 4 * rows, rows), BF),
            pltpu.VMEM((2, 4 * rows, rows), BF),
        ],
        cost_estimate=cost(
            10 * rows * 4 * rows * WIDE, 2 * rows * 24 * WIDE, rows * 4 * rows * 2 * GROUP
        ),
        name="pull",
    )(info, queries, grads, logs, *chunks, *chunks)


def unturn_kernel(halves, *refs):
    cos_ref, first_ref, second_ref, out_ref = refs[4 * halves :]
    wide, first, second = cos_ref[...], -first_ref[...], -second_ref[...]
    column = 0
    for half in range(halves):
        dq_ref, own_ref, near_ref, far_ref = refs[4 * half : 4 * half + 4]
        width = dq_ref.shape[1]
        for part in range(width // 128):
            span = slice(part * 128, part * 128 + 128)
            at = column + part * 128
            out_ref[:, at : at + 128] = turn(dq_ref[:, span] * SCALE, wide, first, second).astype(
                BF
            )
            dk = own_ref[0, :, span] + near_ref[0, :, span].astype(F32)
            dk = (dk + far_ref[0, :, span].astype(F32)) * SCALE
            out_ref[:, D + at : D + at + 128] = turn(dk, wide, first, second).astype(BF)
            dv = own_ref[1, :, span] + near_ref[1, :, span].astype(F32)
            dv = dv + far_ref[1, :, span].astype(F32)
            out_ref[:, 2 * D + at : 2 * D + at + 128] = dv.astype(BF)
        column += width


def unturn(parts, tables):
    rows = tables[0].shape[0]
    arrays = [value for part in parts for value in part]
    vmem = pl.BlockSpec(memory_space=pltpu.VMEM)
    return pl.pallas_call(
        functools.partial(unturn_kernel, len(parts)),
        out_shape=jax.ShapeDtypeStruct((rows, 3 * D), BF),
        in_specs=[vmem] * (len(arrays) + 3),
        out_specs=vmem,
        cost_estimate=cost(20 * rows * 3 * D, rows * D * 30),
        name="unturn",
    )(*arrays, *tables)


def piece_bits(order, index):
    picked = dict(zip(order, ((index >> 2) & 1, (index >> 1) & 1, index & 1)))
    return picked["y"], picked["x"], picked["z"]


def rows_kernel(orders, lefts, spots_ref, *refs):
    left_refs = refs[: 2 * lefts]
    right_refs = refs[2 * lefts : 4 * lefts]
    split_orders = len(orders) == 2
    riders = refs[4 * lefts : 4 * lefts + 2] if split_orders else ()
    outs = refs[4 * lefts + len(riders) : -2]
    turned_ref, picked_ref = refs[-2:]
    y, core, x, z = spots_ref[0], spots_ref[1], spots_ref[2], spots_ref[3]
    rows = left_refs[0].shape[0]
    high = D // 16

    def turned(own_ref, other_ref, slot):
        turned_ref[slot, :, 0:rows] = jnp.transpose(own_ref[...])
        turned_ref[slot, :, rows : 2 * rows] = jnp.transpose(other_ref[...])

    def pick(slot, order, place):
        for index in range(8):
            dy, dx, dz = piece_bits(order, index)
            start = (y ^ dy) * (D // 2) + core * (D // 4) + ((x ^ dx) * 2 + (z ^ dz)) * high
            picked_ref[place, index * high : index * high + high, :] = turned_ref[
                slot, pl.ds(pl.multiple_of(start, 16), high), :
            ]

    def multiply(place, own_ref, other_ref, source, block, keep_ref, send_ref):
        columns = pl.ds(pl.multiple_of(source * D, D), D)
        product = jnp.dot(
            picked_ref[place, :, 0:rows], own_ref[:, columns], preferred_element_type=F32
        )
        product += jnp.dot(
            picked_ref[place, :, rows : 2 * rows],
            other_ref[:, columns],
            preferred_element_type=F32,
        )
        span = pl.ds(pl.multiple_of(block * high, 16), high)
        for index in range(4):
            keep_ref[index, span, :] = product[index * high : index * high + high, :]
            send_ref[index, span, :] = product[
                (4 + index) * high : (4 + index) * high + high, :
            ].astype(BF)

    turned(left_refs[0], left_refs[1], 0)
    pick(0, orders[0], 0)
    blocks = right_refs[0].shape[1] // D
    split = 2 if len(orders) == 2 else blocks

    def body(block, carry):
        multiply(0, right_refs[0], right_refs[1], block, block, *outs[:2])
        return carry

    lax.fori_loop(0, split, body, 0)
    if len(orders) == 2:
        for index in range(8):
            dy, dx, dz = piece_bits(orders[0], index)
            entry = ((y ^ dy) * 2 + core) * 4 + (x ^ dx) * 2 + (z ^ dz)
            value = riders[0][entry] + riders[1][entry]
            value = jnp.concatenate([value, jnp.zeros((14, D), F32)], axis=0)
            if index < 4:
                outs[0][index, 2 * high : 2 * high + 16, :] = value
            else:
                outs[1][index - 4, 2 * high : 2 * high + 16, :] = value.astype(BF)
        pick(0, orders[1], 1)
        multiply(1, right_refs[0], right_refs[1], 2, 0, *outs[2:])
    if lefts == 2:
        turned(left_refs[2], left_refs[3], 1)
        pick(1, orders[-1], 2)
        multiply(2, right_refs[2], right_refs[3], 0, 1 if len(orders) == 2 else blocks, *outs[-2:])


def rows_unit(spots, orders, lefts, rights, riders=()):
    rows = lefts[0][0].shape[0]
    arrays = [value for pair in (*lefts, *rights) for value in pair] + list(riders)
    high = D // 4 // len(orders)
    heights = [high + 16, high] if riders else [high] * len(orders)
    vmem = pl.BlockSpec(memory_space=pltpu.VMEM)
    return pl.pallas_call(
        functools.partial(rows_kernel, orders, len(lefts)),
        out_shape=[
            jax.ShapeDtypeStruct((4, tall, D), kind) for tall in heights for kind in (F32, BF)
        ],
        in_specs=[pl.BlockSpec(memory_space=pltpu.SMEM)] + [vmem] * len(arrays),
        out_specs=[vmem] * (2 * len(orders)),
        scratch_shapes=[
            pltpu.VMEM((len(lefts), D, 2 * rows), BF),
            pltpu.VMEM((3 if len(lefts) == 2 else 1, D // 2, 2 * rows), BF),
        ],
        cost_estimate=cost(4 * rows * (D // 2) * 4 * D, rows * D * 20 + 3 * D * D),
        name="rows_unit",
    )(spots, *arrays)


def forward_kernel(orders, spots_ref, n0, n1, u0, u1, a0, a1, d0, d1, *refs):
    turned_ref, picked_ref, tall_ref = refs[-3:]
    keep_ref, send_ref, keep_down, send_down = (refs[:-3] * 2)[:4]
    y, core, x, z = spots_ref[0], spots_ref[1], spots_ref[2], spots_ref[3]
    rows = n0.shape[0]
    high = D // 16
    tall = D // 4
    first = tall if len(orders) == 1 else 0
    turned_ref[:, 0:rows] = jnp.transpose(n0[...])
    turned_ref[:, rows : 2 * rows] = jnp.transpose(n1[...])
    for index in range(8):
        dy, dx, dz = piece_bits(orders[0], index)
        start = (y ^ dy) * (D // 2) + core * (D // 4) + ((x ^ dx) * 2 + (z ^ dz)) * high
        picked_ref[index * high : index * high + high, :] = turned_ref[
            pl.ds(pl.multiple_of(start, 16), high), :
        ]

    def body(block, carry):
        columns = pl.ds(pl.multiple_of(block * D, D), D)
        product = jnp.dot(picked_ref[:, 0:rows], u0[:, columns], preferred_element_type=F32)
        product += jnp.dot(
            picked_ref[:, rows : 2 * rows], u1[:, columns], preferred_element_type=F32
        )
        span = pl.ds(pl.multiple_of(block * high, 16), high)
        for index in range(4):
            keep_ref[index, span, :] = product[index * high : index * high + high, :]
            send_ref[index, span, :] = product[
                (4 + index) * high : (4 + index) * high + high, :
            ].astype(BF)
        return carry

    lax.fori_loop(0, 4, body, 0)
    for dy in range(2):
        columns = pl.ds(pl.multiple_of(((y ^ dy) * 2 + core) * D, D), D)
        tall_ref[dy, :, 0:rows] = jnp.transpose(a0[:, columns])
        tall_ref[dy, :, rows : 2 * rows] = jnp.transpose(a1[:, columns])
        for dx in range(2):
            for dz in range(2):
                start = pl.multiple_of(((x ^ dx) * 2 + (z ^ dz)) * tall, 16)
                left = tall_ref[dy, pl.ds(start, tall), :]
                product = jnp.dot(left[:, 0:rows], d0[...], preferred_element_type=F32)
                product += jnp.dot(left[:, rows : 2 * rows], d1[...], preferred_element_type=F32)
                index = [k for k in range(8) if piece_bits(orders[-1], k) == (dy, dx, dz)][0]
                if index < 4:
                    keep_down[index, first : first + tall, :] = product
                else:
                    send_down[index - 4, first : first + tall, :] = product.astype(BF)


def forward_unit(spots, orders, normed, grad_up, activated, grad_down):
    rows = normed[0].shape[0]
    vmem = pl.BlockSpec(memory_space=pltpu.VMEM)
    return pl.pallas_call(
        functools.partial(forward_kernel, orders),
        out_shape=[
            jax.ShapeDtypeStruct((4, D // 2 // len(orders), D), kind)
            for _ in orders
            for kind in (F32, BF)
        ],
        in_specs=[pl.BlockSpec(memory_space=pltpu.SMEM)] + [vmem] * 8,
        out_specs=[vmem] * (2 * len(orders)),
        scratch_shapes=[
            pltpu.VMEM((D, 2 * rows), BF),
            pltpu.VMEM((D // 2, 2 * rows), BF),
            pltpu.VMEM((2, D, 2 * rows), BF),
        ],
        cost_estimate=cost(8 * rows * (D // 2) * 4 * D, rows * D * 40 + 6 * D * D),
        name="forward_unit",
    )(spots, *normed, *grad_up, *activated, *grad_down)


AXES = {"y": ("fsdp", 2), "x": ("dp", 1), "z": ("dp", 2)}


class Sum:
    def __init__(self, line, unit, order):
        self.line, self.order, self.stage = line, order, 0
        self.keep, send = unit
        self.moving = swap(send, *AXES[order[0]])
        self.far = [1 << k for k in range(2, 20) if (1 << k) < lax.axis_size("dp")]
        self.rest = [name for name in order if name != "y"]

    def step(self):
        got, keep = self.line.enter(self.moving, self.keep)
        line, stage = self.line, self.stage
        self.stage += 1
        if stage < 3:
            half = keep.shape[0] // 2
            if stage < 2:
                self.keep = keep[:half] + got[:half].astype(F32)
                send = (keep[half:] + got[half:].astype(F32)).astype(BF)
                line.leave(self.keep, send)
                self.moving = swap(send, *AXES[self.order[stage + 1]])
                return
            self.keep = (keep + got.astype(F32)).astype(BF)
        elif stage < 3 + len(self.far):
            self.keep = (keep.astype(F32) + got.astype(F32)).astype(BF)
        elif stage == 3 + len(self.far):
            self.keep = jnp.concatenate([keep, got], axis=0)
            line.leave(self.keep)
            self.moving = swap(self.keep, *AXES[self.rest[0]])
            return
        else:
            self.result = (keep, got)
            return
        line.leave(self.keep)
        if stage - 2 < len(self.far):
            self.moving = swap(self.keep, "dp", self.far[stage - 2])
        else:
            self.moving = swap(self.keep, *AXES[self.rest[1]])

    def finish(self):
        while self.stage < 5 + len(self.far):
            self.step()
        return self.result


def emit_kernel(orders, places, count, spots_ref, *refs):
    outs = refs[-count:]
    x, z = spots_ref[2], spots_ref[3]
    high = D // 16
    for number, order in enumerate(orders):
        rest = [name for name in order if name != "y"]
        for outer in range(2):
            piece = refs[2 * number + outer]
            for inner in range(2):
                picked = dict(zip(rest, (outer, inner)))
                which = (x ^ picked["x"]) * 2 + (z ^ picked["z"])
                at = 0
                for slot, block in places[number]:
                    if block == RIDER:
                        outs[slot][which] = piece[inner, at : at + 16, :].astype(F32)[0:2]
                        continue
                    tall = high if block is not None else 4 * high
                    start = pl.multiple_of(which * tall, 16)
                    first = 0 if block is None else block * D
                    outs[slot][0, pl.ds(start, tall), first : first + D] = piece[
                        inner, at : at + tall, :
                    ].astype(F32)
                    at += tall


def emit(spots, sums, orders, places, shapes, layer, before):
    out_shape = [jax.ShapeDtypeStruct((LAYERS,) + shape, F32) for shape in shapes]
    before = list(before) if before is not None else []
    pieces = [piece for pair in sums for piece in pair]
    extra = []
    if any(block == RIDER for place in places for _, block in place):
        out_shape.append(jax.ShapeDtypeStruct((4, 2, D), F32))
        extra.append(pl.BlockSpec((4, 2, D), lambda i, spots: (0, 0, 0)))
    return pl.pallas_call(
        functools.partial(emit_kernel, orders, places, len(out_shape)),
        out_shape=out_shape,
        grid_spec=pltpu.PrefetchScalarGridSpec(
            num_scalar_prefetch=1,
            grid=(1,),
            in_specs=[pl.BlockSpec(memory_space=pltpu.VMEM)] * len(pieces)
            + [pl.BlockSpec(memory_space=pl.ANY)] * len(before),
            out_specs=[
                pl.BlockSpec((1,) + shape, lambda i, spots: (layer, 0, 0)) for shape in shapes
            ]
            + extra,
        ),
        input_output_aliases={1 + len(pieces) + i: i for i in range(len(before))},
        cost_estimate=cost(0, D * D * 6),
        name="emit",
    )(spots, *pieces, *before)


class Line:
    def __init__(self):
        self.last = ()

    def enter(self, *values):
        out = lax.optimization_barrier(tuple(values) + tuple(self.last))
        return out[: len(values)]

    def leave(self, *values):
        self.last = tuple(values)

    def sync(self, *values):
        out = self.enter(*values)
        self.last = tuple(out)
        return out


def after(value, *others):
    return lax.optimization_barrier((value,) + others)[0]


NAMES = (
    "input_bias",
    "output_bias",
    "first_gain",
    "first_shift",
    "up_bias",
    "down_bias",
    "second_gain",
    "second_shift",
)
WIDTHS = (3 * D, D, D, D, 4 * D, D, D, D)


def feed_forward(hidden, context, weights, small, between):
    _, output_weight, up_weight, down_weight = weights
    attn_out = jnp.dot(context, output_weight, preferred_element_type=F32) + small["output_bias"]
    first_in = hidden + attn_out
    normed = layer_norm(first_in, small["first_gain"], small["first_shift"])
    normed_low = normed.astype(BF)
    up_value = jnp.dot(normed_low, up_weight, preferred_element_type=F32) + small["up_bias"]
    part = normal_part(up_value)
    activated = between((up_value * part).astype(BF))
    slope = gelu_slope(up_value, part)
    down_value = (
        jnp.dot(activated, down_weight, preferred_element_type=F32) + small["down_bias"]
    )
    second_in = normed + down_value
    output = layer_norm(second_in, small["second_gain"], small["second_shift"])
    return output, first_in, normed_low, slope, activated, second_in


def feed_backward(grad_output, weights, small, first_in, slope, second_in):
    _, output_weight, up_weight, down_weight = weights
    pull_second = jax.vjp(layer_norm, second_in, small["second_gain"], small["second_shift"])[1]
    grad_second, grad_second_gain, grad_second_shift = pull_second(grad_output)
    grad_down = grad_second.astype(BF)
    grad_down_bias = jnp.sum(grad_down, axis=0, dtype=F32)
    grad_activated = contract_cols(grad_down, down_weight)
    grad_up = (grad_activated * slope).astype(BF)
    grad_up_bias = jnp.sum(grad_up, axis=0, dtype=F32)
    grad_normed = grad_second + contract_cols(grad_up, up_weight)
    pull_first = jax.vjp(layer_norm, first_in, small["first_gain"], small["first_shift"])[1]
    grad_first, grad_first_gain, grad_first_shift = pull_first(grad_normed)
    grad_attn = grad_first.astype(BF)
    grad_output_bias = jnp.sum(grad_attn, axis=0, dtype=F32)
    grad_context = contract_cols(grad_attn, output_weight).astype(BF)
    little = (
        grad_output_bias,
        grad_first_gain,
        grad_first_shift,
        grad_up_bias,
        grad_down_bias,
        grad_second_gain,
        grad_second_shift,
    )
    return grad_down, grad_up, grad_attn, grad_context, grad_first, little


FORWARD_ORDER = (("xzy", "zxy"), ("xzy",))
JOINT_ORDER = (("xzy", "yxz"), ("xzy",))


def on_device(
    tokens,
    cotangent,
    lengths,
    input_weight,
    input_bias,
    output_weight,
    output_bias,
    first_gain,
    first_shift,
    up_weight,
    up_bias,
    down_weight,
    down_bias,
    second_gain,
    second_shift,
):
    place = lax.axis_index("fsdp")
    group = lax.axis_index("dp")
    core = place & 1
    x_bit, z_bit = group & 1, (group >> 1) & 1
    spots = jnp.stack([place >> 1, core, x_bit, z_bit]).astype(jnp.int32)
    row_count = tokens.shape[0]
    places = place * row_count + jnp.arange(row_count, dtype=jnp.int32)
    length = lengths[0]
    info = jnp.stack([place, length]).astype(jnp.int32)
    row_valid = (places < length).astype(F32)

    swap_core = lambda value: swap(value, "fsdp", 1)
    swap_y = lambda value: swap(value, "fsdp", 2)
    swap_x = lambda value: swap(value, "dp", 1)
    swap_z = lambda value: swap(value, "dp", 2)

    rows_of = D // 4
    quarter = rows_of // 4
    start = (x_bit * 2 + z_bit) * quarter
    quarters = [
        x_bit * 2 + z_bit,
        x_bit * 2 + (1 - z_bit),
        (1 - x_bit) * 2 + z_bit,
        (1 - x_bit) * 2 + (1 - z_bit),
    ]
    spread_spots = jnp.stack(
        [place * rows_of, (place ^ 1) * rows_of]
        + [(place ^ 2) * rows_of + q * quarter for q in quarters]
        + [(place ^ 3) * rows_of + q * quarter for q in quarters]
    ).astype(jnp.int32)
    direct_spots = jnp.stack([(place ^ k) * rows_of for k in range(4)]).astype(jnp.int32)
    rest_spec = (("rows", D), ("rows", 4 * D), ("split", 4 * D))

    def wide(i):
        split = [down_weight[i, k * 192 : k * 192 + 192] for k in range(4)]
        return jnp.concatenate([output_weight[i], up_weight[i]] + split, axis=1)

    line = Line()

    input_one, input_two = input_weight[0], input_weight[1]
    over_y = swap_y(input_one)
    packed = jnp.concatenate(
        (
            input_bias,
            output_bias,
            first_gain,
            first_shift,
            up_bias,
            down_bias,
            second_gain,
            second_shift,
        ),
        axis=1,
    )
    packed_y, packed_c, input_c = swap_y(packed), swap_core(packed), swap_core(input_one)
    tables = rotary_tables(places.astype(F32))
    rests = (wide(0), wide(1))
    mine = [lax.dynamic_slice(r, (start, 0), (quarter, r.shape[1])) for r in rests]
    line.leave(*mine, *tables, spread_spots, direct_spots, info, spots)
    over_y, packed_y, packed_c, input_c = line.sync(over_y, packed_y, packed_c, input_c)
    spread_y = swap_y(after(mine[0], over_y))
    rest_c = swap_core(after(rests[0], over_y))
    packed_yc, input_yc = swap_core(packed_y), swap_core(over_y)
    fields = unpack(info, [packed, packed_c, packed_y, packed_yc], WIDTHS)
    smalls = [
        dict(zip(NAMES, fields[i * len(NAMES) : (i + 1) * len(NAMES)])) for i in range(LAYERS)
    ]
    pieces = [input_one, input_c, over_y, input_yc]
    line.leave(*fields)
    hidden, rounded = tokens.astype(F32), tokens
    kept, weights = [], []
    for i in range(LAYERS):
        more = i + 1 < LAYERS
        small = smalls[i]
        pieces = line.enter(*pieces)
        queries, *kvs, whole = project(
            rounded, pieces, direct_spots, small["input_bias"], tables
        )
        line.leave(queries, *kvs, whole)
        kv_y, kv_c = [swap_y(kv) for kv in kvs], [swap_core(kv) for kv in kvs]
        if i == 0:
            spread_y, rest_c = line.sync(spread_y, rest_c)
            spread_z, spread_x = swap_z(spread_y), swap_x(spread_y)
        else:
            (rest_c,) = line.sync(rest_c)
            saved = [kept[0][8], kept[0][6], kept[0][4], rounded]
            shared = line.sync(*[swap_core(v) for v in saved[:2]])
            shared += line.sync(*[swap_core(v) for v in saved[2:]])
            act1, normed1, context1, rounded2 = list(zip(saved, shared))
        chunks, logs = [], []
        context, rest = None, None
        for part in range(PARTS):
            if part == 1:
                spread_z, spread_x = line.sync(spread_z, spread_x)
                spread_xz = swap_x(spread_z)
                crossed = [swap_core(v) for v in (spread_y, spread_z, spread_x)]
            if part == 2:
                crossed = list(line.sync(*crossed))
            got_y, got_c = line.sync(kv_y[part], kv_c[part])
            (got_yc,) = line.sync(swap_core(got_y))
            if more and part == PARTS - 1:
                over_y, input_c = swap_y(after(input_two, got_yc)), swap_core(after(input_two, got_yc))
                next_y = swap_y(after(mine[1], got_yc))
            chunks.append([kvs[part], got_c, got_y, got_yc])
            (query_in,) = line.enter(queries)
            context, log = attend(info, query_in, chunks[-1], part, context)
            line.leave(context, log)
            logs.append(log)
        (spread_xz,) = line.sync(spread_xz)
        crossed.append(swap_core(spread_xz))
        crossed[3:] = line.sync(*crossed[3:])
        pieces = [rests[i], rest_c, spread_y, spread_z, spread_x, spread_xz, *crossed]
        pieces = line.enter(*pieces)
        rest = assemble(pieces, spread_spots, rest_spec)
        weights.append((whole, *rest))
        line.leave(*rest)
        if more:
            over_y, input_c = line.sync(over_y, input_c)
            input_yc = swap_core(over_y)
            rest_c = swap_core(after(rests[1], over_y))
        moving = []

        def between(value):
            if not more:
                return value
            line.leave(value)
            (arrived,) = line.sync(next_y)
            moving.extend((arrived, swap_z(arrived), swap_x(arrived)))
            return line.enter(value)[0]

        (context_in,) = line.enter(context)
        output, first_in, normed, slope, activated, second_in = feed_forward(
            hidden, context_in, weights[i], small, between
        )
        kept.append(
            (rounded, queries, chunks, logs, context, first_in, normed, slope, activated, second_in)
        )
        hidden, rounded = output, output.astype(BF)
        line.leave(hidden, rounded)
        if more:
            spread_y, spread_z, spread_x = moving
            pieces = [input_two, input_c, over_y, input_yc]
    result = rounded

    def both_cores(*values):
        values = line.enter(*values)
        return [(value, swap_core(value)) for value in values]

    def feed_back(grad_output, i):
        (grad_output,) = line.enter(grad_output)
        _, _, _, _, _, first_in, _, slope, _, second_in = kept[i]
        out = feed_backward(grad_output, weights[i], smalls[i], first_in, slope, second_in)
        line.leave(*out[:5])
        return out

    def attention_back(i, grad_context, part):
        queries, chunks, logs = kept[i][1:4]
        (grad_context,) = line.enter(grad_context)
        dq, own, give = pull(info, queries, grad_context, logs[part], chunks[part], part)
        line.leave(dq, own, give)
        return dq, own, swap_core(give)

    def far_back(pulled):
        dq, own, near = pulled
        own, near = line.enter(own, near)
        far = (own[2:] + near[2:].astype(F32)).astype(BF)
        line.leave(far)
        return dq, own, near, swap_y(far)

    def arrive(far):
        dq, own, near, moving = far
        (moving,) = line.sync(moving)
        return dq, own, near, moving

    def forward_sum(i, normed, grad_up, activated, grad_down):
        pairs = (normed, grad_up, activated, grad_down)
        got = line.enter(*[pair[1] for pair in pairs])
        unit = forward_unit(
            spots, FORWARD_ORDER[i], *[(pair[0], g) for pair, g in zip(pairs, got)]
        )
        line.leave(*unit)
        return [
            Sum(line, unit[2 * k : 2 * k + 2], order) for k, order in enumerate(FORWARD_ORDER[i])
        ]

    def joint_sum(i, rounded, grad_joint, context, grad_attn, riders=()):
        got = line.enter(rounded[1], grad_joint[1], context[1], grad_attn[1])
        pairs = [(p[0], g) for p, g in zip((rounded, grad_joint, context, grad_attn), got)]
        unit = rows_unit(
            spots, JOINT_ORDER[i], [pairs[0], pairs[2]], [pairs[1], pairs[3]], riders
        )
        line.leave(*unit)
        return [
            Sum(line, unit[2 * k : 2 * k + 2], order) for k, order in enumerate(JOINT_ORDER[i])
        ]

    def joint_back(i, parts, grad_first):
        flat = line.enter(*[v for part in parts for v in part])
        parts = [flat[4 * k : 4 * k + 4] for k in range(len(parts))]
        grad_joint = unturn(parts, tables)
        line.leave(grad_joint)
        grad_hidden = grad_first + contract_cols(grad_joint, weights[i][0])
        return grad_joint, jnp.sum(grad_joint, axis=0, dtype=F32), grad_hidden

    grad_hidden = cotangent.astype(F32) * row_valid[:, None]
    act2, normed2 = both_cores(kept[1][8], kept[1][6])
    dd2, du2, da2, dc2, grad_first2, little2 = feed_back(grad_hidden, 1)

    def retire(*pairs):
        got = line.sync(*[pair[1] for pair in pairs])
        return [(pair[0], value) for pair, value in zip(pairs, got)]

    act2, normed2 = retire(act2, normed2)
    dd2, du2 = both_cores(dd2, du2)
    p0 = attention_back(1, dc2, 0)
    dd2, du2 = retire(dd2, du2)
    context2, da2 = both_cores(kept[1][4], da2)
    p1 = attention_back(1, dc2, 1)
    context2, da2 = retire(context2, da2)
    p0 = far_back(p0)
    p2 = attention_back(1, dc2, 2)
    p0 = arrive(p0)
    p1 = far_back(p1)
    (f2,) = forward_sum(1, normed2, du2, act2, dd2)
    p1 = arrive(p1)
    p2 = far_back(p2)
    p2 = arrive(p2)
    joint2, bias2, grad_hidden = joint_back(1, (p0, p1, p2), grad_first2)
    (joint2,) = both_cores(joint2)
    dd1, du1, da1, dc1, grad_first1, little1 = feed_back(grad_hidden, 0)
    (joint2,) = retire(joint2)
    f2.step()
    dd1, du1 = both_cores(dd1, du1)
    (j2,) = joint_sum(1, rounded2, joint2, context2, da2)
    dd1, du1 = retire(dd1, du1)
    u1, d1 = forward_sum(0, normed1, du1, act1, dd1)
    f2.step()
    rounded1, da1 = both_cores(kept[0][0], da1)
    p0 = attention_back(0, dc1, 0)
    rounded1, da1 = retire(rounded1, da1)
    j2.step()
    f2.step()
    p1 = attention_back(0, dc1, 1)
    p0 = far_back(p0)
    d1.step()
    u1.step()
    p2 = attention_back(0, dc1, 2)
    p0 = arrive(p0)
    p1 = far_back(p1)
    f2.step()
    j2.step()
    u1.step()
    p1 = arrive(p1)
    p2 = far_back(p2)
    d1.step()
    j2.step()
    f2.step()
    shape_forward = [(D // 4, 4 * D), (D, D)]
    shape_joint = [(D // 4, 3 * D), (D // 4, D)]
    up_places, down_places = [(0, 0), (0, 1), (0, 2), (0, 3)], [(1, None)]

    def write(chains, orders, places, shapes, layer, before):
        sums = [chain.finish() for chain in chains]
        out = emit(spots, sums, orders, places, shapes, layer, before)
        line.leave(*out)
        return out

    p2 = arrive(p2)
    joint1, bias1, grad_hidden = joint_back(0, (p0, p1, p2), grad_first1)
    (joint1,) = both_cores(joint1)
    packed = pack(
        [part.reshape(-1) for layer in ((bias1, *little1), (bias2, *little2)) for part in layer]
    )
    line.leave(packed)
    packed_pair = both_cores(packed)
    u1.step()
    d1.step()
    joint1, packed_pair = retire(joint1, *packed_pair)
    j1 = joint_sum(0, rounded1, joint1, context1, da1, packed_pair)
    u1.step()
    d1.step()
    j2.step()
    out_forward = write(
        [f2], FORWARD_ORDER[1], ([*up_places, *down_places],), shape_forward, 1, None
    )
    (grad_hidden,) = line.sync(grad_hidden)
    j1[0].step()
    j1[1].step()
    j2.step()
    u1.step()
    d1.step()
    j1[0].step()
    j1[1].step()
    j1[0].step()
    j1[1].step()
    out_joint = write(
        [j2],
        JOINT_ORDER[1],
        ([(0, 0), (0, 1), (0, 2), (1, 0)],),
        shape_joint,
        1,
        None,
    )
    j1[0].step()
    j1[1].step()
    j1[0].step()
    j1[1].step()
    out_forward = write(
        [u1, d1], FORWARD_ORDER[0], (up_places, down_places), shape_forward, 0, out_forward
    )
    *out_joint, flat = write(
        j1,
        JOINT_ORDER[0],
        ([(0, 0), (0, 1), (2, RIDER)], [(0, 2), (1, 0)]),
        shape_joint,
        0,
        out_joint,
    )
    flat = spread(flat, WIDTHS)

    small_grads = dict(zip(NAMES, flat))
    return (
        result,
        grad_hidden,
        out_joint[0],
        small_grads["input_bias"],
        out_joint[1],
        small_grads["output_bias"],
        small_grads["first_gain"],
        small_grads["first_shift"],
        out_forward[0],
        small_grads["up_bias"],
        out_forward[1],
        small_grads["down_bias"],
        small_grads["second_gain"],
        small_grads["second_shift"],
    )


def solution(mesh):
    rows = P(("dp", "fsdp"), None)
    matrix = P(None, "fsdp", None)
    vector = P(None, "fsdp")
    parameters = (
        matrix,
        vector,
        matrix,
        vector,
        vector,
        vector,
        matrix,
        vector,
        matrix,
        vector,
        vector,
        vector,
    )
    return jax.shard_map(
        on_device,
        mesh=mesh,
        in_specs=(rows, rows, P("dp"), *parameters),
        out_specs=(rows, rows, *parameters),
        check_vma=False,
    )
```
